32 devices in a mesh: fsdp: 16 (over z, y, core), tp: 2 (over x).
Axes of the slice: x: 2, y: 2, z: 4, core: 2. Of those that a mesh axis runs over, the one named last changes fastest.
Arguments:
- layer_in: bfloat16 [32, 1024, 1024], P('fsdp', 'tp'), may hold values from -6 to 6
- memory: bfloat16 [32, 1024, 1024], P('fsdp', 'tp'), may hold values from -6 to 6
- out_grad: bfloat16 [32, 1024, 1024], P('fsdp', 'tp'), may hold values from -6 to 6
- w_self_in: bfloat16 [1024, 3, 1024], P('fsdp', None, 'tp'), may hold values from -1 to 1
- w_self_out: bfloat16 [1024, 1024], P('tp', 'fsdp'), may hold values from -1 to 1
- w_cross_in: bfloat16 [1024, 3, 1024], P('fsdp', None, 'tp'), may hold values from -1 to 1
- w_cross_out: bfloat16 [1024, 1024], P('tp', 'fsdp'), may hold values from -1 to 1
- w_up: bfloat16 [1024, 4096], P('fsdp', 'tp'), may hold values from -0.1875 to 0.1875
- w_down: bfloat16 [4096, 1024], P('tp', 'fsdp'), may hold values from -0.125 to 0.125
- head_bias: bfloat16 [4, 1024], P(None, 'tp'), may hold values from -3 to 3
- up_bias: bfloat16 [4096], P('tp'), may hold values from -3 to 3
- norm_gain: bfloat16 [3, 1024], replicated, may hold values from 0.5 to 1.5
- row_bias: bfloat16 [6, 1024], replicated, may hold values from -2 to 2
Outputs:
- mixed: bfloat16 [32, 1024, 1024], P('fsdp', 'tp')
- d_layer_in: bfloat16 [32, 1024, 1024], P('fsdp', 'tp')
- d_memory: bfloat16 [32, 1024, 1024], P('fsdp', 'tp')
- d_self_in: float32 [1024, 3, 1024], P('fsdp', None, 'tp')
- d_self_out: float32 [1024, 1024], P('tp', 'fsdp')
- d_cross_in: float32 [1024, 3, 1024], P('fsdp', None, 'tp')
- d_cross_out: float32 [1024, 1024], P('tp', 'fsdp')
- d_up: float32 [1024, 4096], P('fsdp', 'tp')
- d_down: float32 [4096, 1024], P('tp', 'fsdp')
- d_head_bias: float32 [4, 1024], P(None, 'tp')
- d_up_bias: float32 [4096], P('tp')
- d_norm_gain: float32 [3, 1024], replicated
- d_row_bias: float32 [6, 1024], replicated
The draws below stay inside these ranges and needn't reach their ends.
All inputs are finite; a program needn't handle non-finite values.
Results may differ from the reference program's by a relative error of at most 0.035.
Values may be sent and summed in bfloat16 or wider, within the bound.
A program may use at most 256 MiB of HBM per device.

```python
import math
import jax
import jax.numpy as jnp
from jax import lax

D = 1024
H = 16
HD = 64
FF = 4096
LEN = 1024
SRC = 1024
BATCH = 32


def drawn_field(key, shape, scale, bound):
    values = jax.random.truncated_normal(key, -bound, bound, shape, jnp.float32)
    return (values * scale).astype(jnp.bfloat16)


def draw_layer_in(key, part):
    return drawn_field(jax.random.fold_in(key, 11), (BATCH, LEN, D), 1.0, 6.0)


def draw_memory(key, part):
    return drawn_field(jax.random.fold_in(key, 12), (BATCH, SRC, D), 1.0, 6.0)


def draw_w_self_in(key, part):
    return drawn_field(jax.random.fold_in(key, 13), (D, 3, D), (D // 2) ** (-0.5), 3.0)


def draw_w_cross_in(key, part):
    return drawn_field(jax.random.fold_in(key, 14), (D, 3, D), (D // 2) ** (-0.5), 3.0)


def block_levels(own_key, dims, shards, smallest, top_value):
    def one(dim, shards_of):
        steps = jax.random.uniform(jax.random.fold_in(jax.random.fold_in(own_key, 6), dim), (shards_of,), jnp.float32, smallest / len(shards), top_value / len(shards))
        return jnp.repeat(jnp.exp(steps), dims[dim] // shards_of).reshape((-1,) + (1,) * (len(dims) - dim - 1))

    loudness = one(*shards[0])
    for cut in shards[1:]:
        loudness = loudness * one(*cut)
    return loudness


def gaussian(own_key, extent, scale, reach, pieces=(), held_as=jnp.bfloat16):
    values = scale * jax.random.normal(own_key, extent, jnp.float32)
    if pieces:
        values = values * block_levels(own_key, extent, pieces, -0.22, 0.18)
    return jnp.clip(values, -reach, reach).astype(held_as)


def setup_inputs(seed: int = 0) -> dict:
    arg_keys = jax.random.split(jax.random.key(seed), 14)
    layer_in = draw_layer_in(jax.random.fold_in(arg_keys[13], 71), 0)
    memory = draw_memory(jax.random.fold_in(arg_keys[13], 71), 0)
    out_grad = gaussian(arg_keys[2], (BATCH, LEN, D), 1.0, 6.0, ((0, 16), (1, 2)))
    w_self_in = draw_w_self_in(jax.random.fold_in(arg_keys[13], 71), 0)
    w_self_out = gaussian(arg_keys[4], (D, D), (D // 32) ** -0.5, 1.0, ((0, 2), (1, 16)))
    w_cross_in = draw_w_cross_in(jax.random.fold_in(arg_keys[13], 71), 0)
    w_cross_out = gaussian(arg_keys[6], (D, D), (D // 32) ** -0.5, 1.0, ((0, 2), (1, 16)))
    w_up = gaussian(arg_keys[7], (D, FF), D ** -0.5, 0.1875, ((0, 16), (1, 2)))
    w_down = gaussian(arg_keys[8], (FF, D), (FF // 2) ** -0.5, 0.125, ((0, 2), (1, 16)))
    head_bias = gaussian(arg_keys[9], (4, D), 0.5, 3.0, ((1, 2),))
    up_bias = gaussian(arg_keys[10], (FF,), 0.5, 3.0, ((0, 2),))
    norm_gain = jnp.clip(1.0 + 0.1 * jax.random.normal(arg_keys[11], (3, D), jnp.float32), 0.5, 1.5).astype(jnp.bfloat16)
    row_bias = gaussian(arg_keys[12], (6, D), 0.3, 2.0)
    return dict(layer_in=layer_in, memory=memory, out_grad=out_grad, w_self_in=w_self_in, w_self_out=w_self_out, w_cross_in=w_cross_in, w_cross_out=w_cross_out, w_up=w_up, w_down=w_down, head_bias=head_bias, up_bias=up_bias, norm_gain=norm_gain, row_bias=row_bias)


@jax.custom_vjp
def low(v):
    return lax.optimization_barrier(v.astype(jnp.bfloat16)).astype(jnp.float32)

@jax.custom_vjp
def low_back(v):
    return v

def low_keep(v):
    return (low(v), None)

def low_pass(kept, grad):
    return (grad,)

def back_keep(v):
    return (v, None)

def back_low(kept, grad):
    return (low(grad),)
low.defvjp(low_keep, low_pass)
low_back.defvjp(back_keep, back_low)
HIGHEST = lax.Precision.HIGHEST
NORM_EPS = 1e-05
ATT_SCALE = 0.125

def layer_norm(resid, gain, shift):
    center = resid - lax.optimization_barrier(jnp.mean(resid, -1, keepdims=True))
    spread = lax.optimization_barrier(jnp.mean(center * center, -1, keepdims=True))
    return center * lax.rsqrt(spread + NORM_EPS) * gain + shift

def attention(query, keys, values, seq_count, key_len, causal):
    query_all = query.reshape(seq_count, LEN, H, HD)
    keys_all = keys.reshape(seq_count, key_len, H, HD)
    values_all = values.reshape(seq_count, key_len, H, HD)
    block_rows = min(512, LEN)
    block_count = LEN // block_rows
    block_starts = jnp.arange(block_count, dtype=jnp.int32) * block_rows

    def one_sequence(seq_item):
        query_seq, keys_seq, values_seq = seq_item

        def one_block(blk_item):
            query_blk, block_start = blk_item
            scores = low_back(jnp.einsum('qhc,khc->hqk', query_blk, keys_seq, precision=HIGHEST))
            if causal:
                row_pos = block_start + lax.broadcasted_iota(jnp.int32, scores.shape[1:], 0)
                col_pos = lax.broadcasted_iota(jnp.int32, scores.shape[1:], 1)
                scores = jnp.where(row_pos >= col_pos, scores, -1e+30)
            row_max = lax.optimization_barrier(jnp.max(scores, -1, keepdims=True))
            log_total = row_max + jnp.log(lax.optimization_barrier(jnp.sum(jnp.exp(scores - row_max), -1, keepdims=True)))
            probs = low(jnp.exp(scores - log_total))
            return jnp.einsum('hqk,khc->qhc', probs, values_seq, precision=HIGHEST)
        block_outs = lax.map(jax.checkpoint(one_block), (query_seq.reshape(block_count, block_rows, H, HD), block_starts))
        return block_outs.reshape(LEN, H * HD)
    return lax.map(one_sequence, (query_all, keys_all, values_all)).reshape(seq_count * LEN, H * HD)

def forward(params, layer_rows, memory_rows):
    w_self_in, w_self_out, w_cross_in, w_cross_out, w_up, w_down, head_bias, up_bias, norm_gain, row_bias = params
    seq_count = layer_rows.shape[0]
    token_rows = layer_rows.reshape(seq_count * LEN, D)
    source_rows = memory_rows.reshape(seq_count * SRC, D)
    self_proj = jnp.einsum('rd,dkc->rkc', token_rows, w_self_in, precision=HIGHEST)
    self_query = low(low_back((self_proj[:, 0] + head_bias[0]) * ATT_SCALE))
    self_keys = low(low_back(self_proj[:, 1]))
    self_values = low(low_back(self_proj[:, 2] + head_bias[1]))
    self_att = low(low_back(attention(self_query, self_keys, self_values, seq_count, LEN, True)))
    resid_one = token_rows + low_back(jnp.dot(self_att, w_self_out, precision=HIGHEST)) + row_bias[0]
    normed_one = layer_norm(resid_one, norm_gain[0], row_bias[3])
    normed_low = low(normed_one)
    cross_query = low(low_back((jnp.dot(normed_low, w_cross_in[:, 0], precision=HIGHEST) + head_bias[2]) * ATT_SCALE))
    cross_keys = low(low_back(jnp.dot(source_rows, w_cross_in[:, 1], precision=HIGHEST)))
    cross_values = low(low_back(jnp.dot(source_rows, w_cross_in[:, 2], precision=HIGHEST) + head_bias[3]))
    cross_att = low(low_back(attention(cross_query, cross_keys, cross_values, seq_count, SRC, False)))
    resid_two = normed_one + low_back(jnp.dot(cross_att, w_cross_out, precision=HIGHEST)) + row_bias[1]
    normed_two = layer_norm(resid_two, norm_gain[1], row_bias[4])
    normed_two_low = low(normed_two)
    pre_act = low_back(jnp.dot(normed_two_low, w_up, precision=HIGHEST) + up_bias)
    hidden_act = low(jax.nn.gelu(pre_act, approximate=False))
    resid_three = normed_two + low_back(jnp.dot(hidden_act, w_down, precision=HIGHEST)) + row_bias[2]
    return layer_norm(resid_three, norm_gain[2], row_bias[5]).reshape(seq_count, LEN, D)

def reference(layer_in, memory, out_grad, w_self_in, w_self_out, w_cross_in, w_cross_out, w_up, w_down, head_bias, up_bias, norm_gain, row_bias):
    params = (w_self_in.astype(jnp.float32), w_self_out.astype(jnp.float32), w_cross_in.astype(jnp.float32), w_cross_out.astype(jnp.float32), w_up.astype(jnp.float32), w_down.astype(jnp.float32), head_bias.astype(jnp.float32), up_bias.astype(jnp.float32), norm_gain.astype(jnp.float32), row_bias.astype(jnp.float32))
    group_size = math.gcd(BATCH, max(1, 4096 // LEN))
    group_count = BATCH // group_size
    layer_groups = layer_in.astype(jnp.float32).reshape(group_count, group_size, LEN, D)
    memory_groups = memory.astype(jnp.float32).reshape(group_count, group_size, SRC, D)
    grad_groups = out_grad.astype(jnp.float32).reshape(group_count, group_size, LEN, D)

    def one_group(totals, group_item):
        layer_grp, memory_grp, grad_grp = group_item
        layer_out, pull_back = jax.vjp(forward, params, layer_grp, memory_grp)
        grad_params, grad_layer, grad_memory = pull_back(grad_grp)
        totals = jax.tree.map(jnp.add, totals, grad_params)
        return (totals, (layer_out.astype(jnp.bfloat16), grad_layer.astype(jnp.bfloat16), grad_memory.astype(jnp.bfloat16)))
    zero_totals = jax.tree.map(jnp.zeros_like, params)
    totals, (layer_outs, layer_grads, memory_grads) = lax.scan(one_group, zero_totals, (layer_groups, memory_groups, grad_groups))
    mixed = layer_outs.reshape(BATCH, LEN, D)
    d_layer_in = layer_grads.reshape(BATCH, LEN, D)
    d_memory = memory_grads.reshape(BATCH, SRC, D)
    return (mixed, d_layer_in, d_memory, totals[0], totals[1], totals[2], totals[3], totals[4], totals[5], totals[6], totals[7], totals[8], totals[9])
```

```python
import functools

import jax
import jax.numpy as jnp
from jax import lax
from jax.experimental import pallas as pl
from jax.experimental.pallas import tpu as pltpu
from jax.sharding import PartitionSpec as P

HD = 64
NORM_EPS = 1e-05
ATT_SCALE = 0.125


def times_back(left, right):
    return lax.dot_general(
        left, right, (((1,), (1,)), ((), ())), preferred_element_type=jnp.float32
    )


def over_rows(left, right):
    return lax.dot_general(
        left, right, (((0,), (0,)), ((), ())), preferred_element_type=jnp.float32
    )


def whole_rows(piece):
    return lax.all_gather(piece, "tp", axis=1, tiled=True)


def whole_grads(piece):
    return lax.all_gather(piece, "tp", axis=1, tiled=True)


def branch_sum(term):
    return lax.psum_scatter(
        term.astype(jnp.bfloat16), "tp", scatter_dimension=1, tiled=True
    ).astype(jnp.float32)


def piece_sum(term):
    return lax.psum_scatter(
        term.astype(jnp.bfloat16), "tp", scatter_dimension=1, tiled=True
    ).astype(jnp.float32)


def norm_forward(resid, gain, shift):
    center = resid - jnp.mean(resid, -1, keepdims=True)
    spread = jnp.mean(center * center, -1, keepdims=True)
    inv_std = lax.rsqrt(spread + NORM_EPS)
    normed = center * inv_std
    return (normed * gain + shift, normed, inv_std)


def norm_backward(grad_out, normed, inv_std, gain):
    grad_normed = grad_out * gain
    grad_resid = inv_std * (
        grad_normed
        - jnp.mean(grad_normed, -1, keepdims=True)
        - normed * jnp.mean(grad_normed * normed, -1, keepdims=True)
    )
    return (grad_resid, jnp.sum(grad_out * normed, (0, 1)), jnp.sum(grad_out, (0, 1)))


def gelu_exact(pre_act):
    return jax.nn.gelu(pre_act, approximate=False)


def gelu_back(pre_act, grad_act):
    unused_out, pull_back = jax.vjp(gelu_exact, pre_act)
    return pull_back(grad_act)[0]


def masked_scores(query_blk, block_start, keys_seq, causal):
    scores = jnp.einsum("qhc,khc->hqk", query_blk, keys_seq, preferred_element_type=jnp.float32)
    if causal:
        row_pos = block_start + lax.broadcasted_iota(jnp.int32, scores.shape[1:], 0)
        col_pos = lax.broadcasted_iota(jnp.int32, scores.shape[1:], 1)
        scores = jnp.where(row_pos >= col_pos, scores, -1e30)
    return scores


def attend_forward(query, keys, values, causal):
    seq_count, length, heads_dev, depth = query.shape
    block_rows = min(512, length)
    block_count = length // block_rows
    block_starts = jnp.arange(block_count, dtype=jnp.int32) * block_rows

    def one_sequence(seq_item):
        query_seq, keys_seq, values_seq = seq_item

        def one_block(blk_item):
            query_blk, block_start = blk_item
            scores = masked_scores(query_blk, block_start, keys_seq, causal)
            row_max = jnp.max(scores, -1, keepdims=True)
            log_total = row_max + jnp.log(jnp.sum(jnp.exp(scores - row_max), -1, keepdims=True))
            probs = jnp.exp(scores - log_total).astype(jnp.bfloat16)
            block_out = jnp.einsum(
                "hqk,khc->qhc", probs, values_seq, preferred_element_type=jnp.float32
            )
            return (block_out.astype(jnp.bfloat16), log_total)

        block_outs, log_totals = lax.map(
            one_block, (query_seq.reshape(block_count, block_rows, heads_dev, depth), block_starts)
        )
        return (block_outs.reshape(length, heads_dev, depth), log_totals)

    return lax.map(one_sequence, (query, keys, values))


def attend_backward(query, keys, values, log_totals, grad_out, causal):
    seq_count, length, heads_dev, depth = query.shape
    block_rows = min(512, length)
    block_count = length // block_rows
    block_starts = jnp.arange(block_count, dtype=jnp.int32) * block_rows

    def one_sequence(seq_item):
        query_seq, keys_seq, values_seq, total_seq, grad_seq = seq_item

        def one_block(carry, blk_item):
            query_blk, grad_blk, total_blk, block_start = blk_item
            probs = jnp.exp(masked_scores(query_blk, block_start, keys_seq, causal) - total_blk)
            grad_probs = jnp.einsum(
                "qhc,khc->hqk", grad_blk, values_seq, preferred_element_type=jnp.float32
            )
            row_delta = jnp.sum(probs * grad_probs, -1, keepdims=True)
            grad_scores = (probs * (grad_probs - row_delta)).astype(jnp.bfloat16)
            grad_query = jnp.einsum(
                "hqk,khc->qhc", grad_scores, keys_seq, preferred_element_type=jnp.float32
            )
            grad_keys = carry[0] + jnp.einsum(
                "hqk,qhc->khc", grad_scores, query_blk, preferred_element_type=jnp.float32
            )
            grad_values = carry[1] + jnp.einsum(
                "hqk,qhc->khc",
                probs.astype(jnp.bfloat16),
                grad_blk,
                preferred_element_type=jnp.float32,
            )
            return ((grad_keys, grad_values), grad_query)

        zero_keys = jnp.zeros(keys_seq.shape, jnp.float32)
        blk_items = (
            query_seq.reshape(block_count, block_rows, heads_dev, depth),
            grad_seq.reshape(block_count, block_rows, heads_dev, depth),
            total_seq,
            block_starts,
        )
        (grad_keys, grad_values), grad_query = lax.scan(
            one_block, (zero_keys, zero_keys), blk_items
        )
        return (grad_query.reshape(length, heads_dev, depth), grad_keys, grad_values)

    return lax.map(one_sequence, (query, keys, values, log_totals, grad_out))


def shared_sequences(
    layer_in,
    memory,
    out_grad,
    w_self_in,
    w_self_out,
    w_cross_in,
    w_cross_out,
    w_up,
    w_down,
    head_bias,
    up_bias,
    norm_gain,
    row_bias,
):
    seq_count, piece_len, model_width = layer_in.shape
    head_cols = w_self_in.shape[2]
    unit_cols = w_up.shape[1]
    heads_dev = head_cols // HD
    tp_place = lax.axis_index("tp")
    tp_count = lax.axis_size("tp")
    zero_index = jnp.zeros((), jnp.int32)
    gains = norm_gain.astype(jnp.float32)
    shifts = row_bias.astype(jnp.float32)
    col_bias = head_bias.astype(jnp.float32)
    unit_bias = up_bias.astype(jnp.float32)
    self_in, self_out, cross_in, cross_out, up_full, down_full = (
        lax.all_gather(w_self_in, "fsdp", axis=0, tiled=True),
        lax.all_gather(w_self_out, "fsdp", axis=1, tiled=True),
        lax.all_gather(w_cross_in, "fsdp", axis=0, tiled=True),
        lax.all_gather(w_cross_out, "fsdp", axis=1, tiled=True),
        lax.all_gather(w_up, "fsdp", axis=0, tiled=True),
        lax.all_gather(w_down, "fsdp", axis=1, tiled=True),
    )
    layer_whole = whole_rows(layer_in)
    length = layer_whole.shape[1]
    row_count = seq_count * length
    token_rows = layer_whole.reshape(row_count, model_width)
    self_proj = jnp.einsum("rd,dkc->rkc", token_rows, self_in, preferred_element_type=jnp.float32)
    self_query = ((self_proj[:, 0] + col_bias[0]) * ATT_SCALE).astype(jnp.bfloat16)
    self_keys = self_proj[:, 1].astype(jnp.bfloat16)
    self_values = (self_proj[:, 2] + col_bias[1]).astype(jnp.bfloat16)
    head_shape = (seq_count, length, heads_dev, HD)
    self_att, self_totals = attend_forward(
        self_query.reshape(head_shape),
        self_keys.reshape(head_shape),
        self_values.reshape(head_shape),
        True,
    )
    self_rows = self_att.reshape(row_count, head_cols)
    self_term = jnp.dot(self_rows, self_out, preferred_element_type=jnp.float32).reshape(
        seq_count, length, model_width
    )
    resid_one = layer_in.astype(jnp.float32) + branch_sum(self_term) + shifts[0]
    normed_one, unit_one, inv_one = norm_forward(resid_one, gains[0], shifts[3])
    normed_rows = whole_rows(normed_one.astype(jnp.bfloat16)).reshape(row_count, model_width)
    cross_query = (
        (jnp.dot(normed_rows, cross_in[:, 0], preferred_element_type=jnp.float32) + col_bias[2])
        * ATT_SCALE
    ).astype(jnp.bfloat16)
    memory_whole = lax.all_gather(memory, "tp", axis=1, tiled=True)
    source_len = memory_whole.shape[1]
    source_rows = memory_whole.reshape(seq_count * source_len, model_width)
    cross_proj = jnp.einsum(
        "rd,dkc->rkc", source_rows, cross_in[:, 1:], preferred_element_type=jnp.float32
    )
    cross_keys = cross_proj[:, 0].astype(jnp.bfloat16)
    cross_values = (cross_proj[:, 1] + col_bias[3]).astype(jnp.bfloat16)
    source_shape = (seq_count, source_len, heads_dev, HD)
    cross_att, cross_totals = attend_forward(
        cross_query.reshape(head_shape),
        cross_keys.reshape(source_shape),
        cross_values.reshape(source_shape),
        False,
    )
    cross_rows = cross_att.reshape(row_count, head_cols)
    cross_term = jnp.dot(cross_rows, cross_out, preferred_element_type=jnp.float32).reshape(
        seq_count, length, model_width
    )
    resid_two = normed_one + branch_sum(cross_term) + shifts[1]
    normed_two, unit_two, inv_two = norm_forward(resid_two, gains[1], shifts[4])
    normed_two_low = normed_two.astype(jnp.bfloat16)
    ffn_rows = whole_rows(normed_two_low).reshape(row_count, model_width)
    pre_act = jnp.dot(ffn_rows, up_full, preferred_element_type=jnp.float32) + unit_bias
    hidden_act = gelu_exact(pre_act).astype(jnp.bfloat16)
    ffn_term = jnp.dot(hidden_act, down_full, preferred_element_type=jnp.float32).reshape(
        seq_count, length, model_width
    )
    ffn_out = branch_sum(ffn_term)
    resid_three = normed_two + ffn_out + shifts[2]
    mixed, unit_three, inv_three = norm_forward(resid_three, gains[2], shifts[5])
    grad_three, gain_grad_three, shift_grad_three = norm_backward(
        out_grad.astype(jnp.float32), unit_three, inv_three, gains[2]
    )
    bias_grad_three = jnp.sum(grad_three, (0, 1))
    grad_three_low = grad_three.astype(jnp.bfloat16)
    grad_rows = whole_grads(grad_three_low).reshape(row_count, model_width)
    grad_act = times_back(grad_rows, down_full)
    grad_pre = gelu_back(pre_act, grad_act).astype(jnp.bfloat16)
    d_up = over_rows(ffn_rows, grad_pre)
    d_down = over_rows(hidden_act, grad_rows)
    unit_grad = jnp.sum(grad_pre, 0, dtype=jnp.float32)
    grad_two_in = piece_sum(times_back(grad_pre, up_full).reshape(seq_count, length, model_width))
    grad_normed_two = grad_three + grad_two_in
    grad_two, gain_grad_two, shift_grad_two = norm_backward(
        grad_normed_two, unit_two, inv_two, gains[1]
    )
    bias_grad_two = jnp.sum(grad_two, (0, 1))
    grad_two_rows = whole_grads(grad_two.astype(jnp.bfloat16)).reshape(row_count, model_width)
    d_cross_out = over_rows(cross_rows, grad_two_rows)
    grad_cross_att = times_back(grad_two_rows, cross_out).astype(jnp.bfloat16)
    cq_grad, ck_grad, cv_grad = attend_backward(
        cross_query.reshape(head_shape),
        cross_keys.reshape(source_shape),
        cross_values.reshape(source_shape),
        cross_totals,
        grad_cross_att.reshape(head_shape),
        False,
    )
    cq_pre = cq_grad.reshape(row_count, head_cols).astype(jnp.bfloat16) * jnp.asarray(
        ATT_SCALE, jnp.bfloat16
    )
    ckv_low = jnp.stack(
        [
            ck_grad.reshape(seq_count * source_len, head_cols),
            cv_grad.reshape(seq_count * source_len, head_cols),
        ],
        1,
    ).astype(jnp.bfloat16)
    cross_q_grad = over_rows(normed_rows, cq_pre)
    cq_bias_grad = jnp.sum(cq_pre, 0, dtype=jnp.float32)
    normed_part = times_back(cq_pre, cross_in[:, 0]).reshape(seq_count, length, model_width)
    source_part = jnp.einsum(
        "rkc,dkc->rd", ckv_low, cross_in[:, 1:], preferred_element_type=jnp.float32
    ).reshape(seq_count, source_len, model_width)
    grad_one_in, memory_grad = (
        lax.psum_scatter(
            normed_part.astype(jnp.bfloat16), "tp", scatter_dimension=1, tiled=True
        ).astype(jnp.float32),
        lax.psum_scatter(
            source_part.astype(jnp.bfloat16), "tp", scatter_dimension=1, tiled=True
        ).astype(jnp.float32),
    )
    d_memory = memory_grad.astype(jnp.bfloat16)
    cross_kv_grad = jnp.einsum(
        "rd,rkc->dkc", source_rows, ckv_low, preferred_element_type=jnp.float32
    )
    cross_grad_term = jnp.concatenate([cross_q_grad[:, None, :], cross_kv_grad], 1)
    cv_own = jnp.sum(ckv_low[:, 1], 0, dtype=jnp.float32)
    cv_wide = lax.dynamic_update_slice(
        jnp.zeros((head_cols * tp_count,), jnp.float32), cv_own, (tp_place * head_cols,)
    )
    grad_normed_one = grad_two + grad_one_in
    grad_one, gain_grad_one, shift_grad_one = norm_backward(
        grad_normed_one, unit_one, inv_one, gains[0]
    )
    bias_grad_one = jnp.sum(grad_one, (0, 1))
    grad_one_rows = whole_grads(grad_one.astype(jnp.bfloat16)).reshape(row_count, model_width)
    d_self_out = over_rows(self_rows, grad_one_rows)
    grad_self_att = times_back(grad_one_rows, self_out).astype(jnp.bfloat16)
    sq_grad, sk_grad, sv_grad = attend_backward(
        self_query.reshape(head_shape),
        self_keys.reshape(head_shape),
        self_values.reshape(head_shape),
        self_totals,
        grad_self_att.reshape(head_shape),
        True,
    )
    sq_pre = sq_grad.reshape(row_count, head_cols).astype(jnp.bfloat16) * jnp.asarray(
        ATT_SCALE, jnp.bfloat16
    )
    sqkv_low = jnp.stack(
        [
            sq_pre,
            sk_grad.reshape(row_count, head_cols).astype(jnp.bfloat16),
            sv_grad.reshape(row_count, head_cols).astype(jnp.bfloat16),
        ],
        1,
    )
    d_self_in = jnp.einsum("rd,rkc->dkc", token_rows, sqkv_low, preferred_element_type=jnp.float32)
    sq_bias_grad = jnp.sum(sq_pre, 0, dtype=jnp.float32)
    sv_bias_grad = jnp.sum(sqkv_low[:, 2], 0, dtype=jnp.float32)
    layer_part = jnp.einsum(
        "rkc,dkc->rd", sqkv_low, self_in, preferred_element_type=jnp.float32
    ).reshape(seq_count, length, model_width)
    d_layer_in = (grad_one + piece_sum(layer_part)).astype(jnp.bfloat16)
    slot_grad = jnp.stack([sq_bias_grad, sv_bias_grad, cq_bias_grad])
    slot_wide = lax.dynamic_update_slice(
        jnp.zeros((3, head_cols * tp_count), jnp.float32),
        slot_grad,
        (zero_index, tp_place * head_cols),
    )
    head_wide = jnp.concatenate([slot_wide, cv_wide[None, :]], 0)
    unit_wide_grad = lax.dynamic_update_slice(
        jnp.zeros((unit_cols * tp_count,), jnp.float32), unit_grad, (tp_place * unit_cols,)
    )
    gain_grads = jnp.stack([gain_grad_one, gain_grad_two, gain_grad_three])
    shift_grads = jnp.stack(
        [
            bias_grad_one,
            bias_grad_two,
            bias_grad_three,
            shift_grad_one,
            shift_grad_two,
            shift_grad_three,
        ]
    )
    gain_total, shift_total, head_total, unit_total = lax.psum(
        (gain_grads, shift_grads, head_wide, unit_wide_grad), ("fsdp", "tp")
    )
    d_head_bias = lax.dynamic_slice(head_total, (zero_index, tp_place * head_cols), (4, head_cols))
    d_up_bias = lax.dynamic_slice(unit_total, (tp_place * unit_cols,), (unit_cols,))
    g_self_in, g_self_out, g_cross_part, g_cross_out, g_up, g_down = (
        lax.psum_scatter(
            d_self_in.astype(jnp.bfloat16), "fsdp", scatter_dimension=0, tiled=True
        ).astype(jnp.float32),
        lax.psum_scatter(
            d_self_out.astype(jnp.bfloat16), "fsdp", scatter_dimension=1, tiled=True
        ).astype(jnp.float32),
        lax.psum_scatter(
            cross_grad_term.astype(jnp.bfloat16), "fsdp", scatter_dimension=0, tiled=True
        ).astype(jnp.float32),
        lax.psum_scatter(
            d_cross_out.astype(jnp.bfloat16), "fsdp", scatter_dimension=1, tiled=True
        ).astype(jnp.float32),
        lax.psum_scatter(d_up.astype(jnp.bfloat16), "fsdp", scatter_dimension=0, tiled=True).astype(
            jnp.float32
        ),
        lax.psum_scatter(
            d_down.astype(jnp.bfloat16), "fsdp", scatter_dimension=1, tiled=True
        ).astype(jnp.float32),
    )
    return (
        mixed.astype(jnp.bfloat16),
        d_layer_in,
        d_memory,
        g_self_in,
        g_self_out,
        g_cross_part,
        g_cross_out,
        g_up,
        g_down,
        d_head_bias,
        d_up_bias,
        gain_total,
        shift_total,
    )


NT=(((1,),(1,)),((),()))
NN=(((1,),(0,)),((),()))
f32=jnp.float32
bf16=jnp.bfloat16

def scores_t(k_h,q,i,bq,causal):
    s=lax.dot_general(k_h,q,NT,preferred_element_type=f32)
    return s

def att_fwd_kernel(q_ref,k_ref,v_ref,o_ref,lse_ref,*,bq,causal):
    n=q_ref.shape[0]; nk=k_ref.shape[0]
    lane=lax.broadcasted_iota(jnp.int32,(nk,128),1)
    k=k_ref[...]; v=v_ref[...]
    zero=jnp.zeros((),bf16)
    kh=[jnp.where(lane<HD,k,zero),jnp.where(lane>=HD,k,zero)]
    vt=v.astype(f32).T.astype(bf16)
    ones=jnp.ones((8,nk),bf16)
    vh=[jnp.concatenate([vt[h*HD:(h+1)*HD],ones],0) for h in range(2)]
    for i in range(n//bq):
        q=q_ref[i*bq:(i+1)*bq,:]
        L=(i+1)*bq if causal else nk
        outs=[];lses=[]
        for h in range(2):
            s=lax.dot_general(kh[h][:L],q,NT,preferred_element_type=f32)
            if causal:
                keep=lax.broadcasted_iota(jnp.int32,(bq,bq),0)<=lax.broadcasted_iota(jnp.int32,(bq,bq),1)
                sd=jnp.where(keep,s[L-bq:],-1e30)
                s=jnp.concatenate([s[:L-bq],sd],0) if L>bq else sd
            m=jnp.max(s,0,keepdims=True)
            p=jnp.exp(s-m).astype(bf16)
            ol=lax.dot_general(vh[h][:,:L],p,NN,preferred_element_type=f32)
            l=ol[HD:HD+1]
            outs.append(ol[:HD]*(1.0/l))
            lses.append(m+jnp.log(l))
        ot=jnp.concatenate(outs,0)
        o_ref[i*bq:(i+1)*bq,:]=ot.T.astype(bf16)
        lse_ref[0,:,i*bq:(i+1)*bq]=jnp.concatenate(lses,0)

def att_fwd(q,k,v,causal,bq=256,qo=0,ko=0,vo=0,width=None):
    n=q.shape[0]; nk=k.shape[0]; width=width or q.shape[1]; np_=width//128
    spec=lambda rows,off: pl.BlockSpec((rows,128),lambda p: (0,p+off))
    return pl.pallas_call(
        functools.partial(att_fwd_kernel,bq=bq,causal=causal),
        grid=(np_,),
        in_specs=[spec(n,qo),spec(nk,ko),spec(nk,vo)],
        out_specs=[spec(n,0),pl.BlockSpec((1,2,n),lambda p:(p,0,0))],
        out_shape=[jax.ShapeDtypeStruct((n,width),bf16),jax.ShapeDtypeStruct((np_,2,n),f32)],
        compiler_params=pltpu.CompilerParams(dimension_semantics=("arbitrary",),vmem_limit_bytes=56*2**20),
    )(q,k,v)

def att_bwd_kernel(q_ref,k_ref,v_ref,o_ref,do_ref,lse_ref,dq_ref,dk_ref,dv_ref,dk_acc,dv_acc,*,bq,causal):
    n=q_ref.shape[0]; nk=k_ref.shape[0]
    lane=lax.broadcasted_iota(jnp.int32,(nk,128),1)
    lq=lax.broadcasted_iota(jnp.int32,(bq,128),1)
    k=k_ref[...]; v=v_ref[...]
    zero=jnp.zeros((),bf16)
    kh=[jnp.where(lane<HD,k,zero),jnp.where(lane>=HD,k,zero)]
    vh=[jnp.where(lane<HD,v,zero),jnp.where(lane>=HD,v,zero)]
    kt=k.astype(f32).T.astype(bf16)
    dk_acc[...]=jnp.zeros_like(dk_acc); dv_acc[...]=jnp.zeros_like(dv_acc)
    for i in range(n//bq):
        rows=slice(i*bq,(i+1)*bq)
        q=q_ref[rows,:]; do=do_ref[rows,:]
        L=(i+1)*bq if causal else nk
        dot_=(do.astype(f32)*o_ref[rows,:].astype(f32)).T
        qm=[jnp.where(lq<HD,q,zero),jnp.where(lq>=HD,q,zero)]
        dm=[jnp.where(lq<HD,do,zero),jnp.where(lq>=HD,do,zero)]
        dqs=[]
        for h in range(2):
            s=lax.dot_general(kh[h][:L],q,NT,preferred_element_type=f32)
            dp=lax.dot_general(vh[h][:L],do,NT,preferred_element_type=f32)
            lse=lse_ref[0,h:h+1,rows]
            delta=jnp.sum(dot_[h*HD:(h+1)*HD],0,keepdims=True)
            if causal:
                keep=lax.broadcasted_iota(jnp.int32,(bq,bq),0)<=lax.broadcasted_iota(jnp.int32,(bq,bq),1)
                sd=jnp.where(keep,s[L-bq:],-1e30)
                s=jnp.concatenate([s[:L-bq],sd],0) if L>bq else sd
            p=jnp.exp(s-lse)
            ds=(p*(dp-delta)).astype(bf16)
            pb=p.astype(bf16)
            dv_acc[:L,:]+=lax.dot_general(pb,dm[h],NN,preferred_element_type=f32)
            dk_acc[:L,:]+=lax.dot_general(ds,qm[h],NN,preferred_element_type=f32)
            dqs.append(lax.dot_general(kt[h*HD:(h+1)*HD,:L],ds,NN,preferred_element_type=f32))
        dq_ref[rows,:]=(jnp.concatenate(dqs,0)*0.125).T.astype(bf16)
    dk_ref[...]=dk_acc[...].astype(bf16)
    dv_ref[...]=dv_acc[...].astype(bf16)

def att_bwd(q,k,v,o,do,lse,causal,bq=256,qo=0,ko=0,vo=0):
    n=q.shape[0]; nk=k.shape[0]; width=o.shape[1]; np_=width//128
    spec=lambda rows,off: pl.BlockSpec((rows,128),lambda p: (0,p+off))
    return pl.pallas_call(
        functools.partial(att_bwd_kernel,bq=bq,causal=causal),
        grid=(np_,),
        in_specs=[spec(n,qo),spec(nk,ko),spec(nk,vo),spec(n,0),spec(n,0),pl.BlockSpec((1,2,n),lambda p:(p,0,0))],
        out_specs=[spec(n,0),spec(nk,0),spec(nk,0)],
        out_shape=[jax.ShapeDtypeStruct((n,width),bf16),jax.ShapeDtypeStruct((nk,width),bf16),jax.ShapeDtypeStruct((nk,width),bf16)],
        scratch_shapes=[pltpu.VMEM((nk,128),f32)]*2,
        compiler_params=pltpu.CompilerParams(dimension_semantics=("arbitrary",),vmem_limit_bytes=56*2**20),
    )(q,k,v,o,do,lse)


ERFC_SLOPE = 0.44
ERFC_COEFS = (
    0.12411048270139104,
    0.12443557227306976,
    0.1086564621750582,
    0.10790840846971936,
    -0.01009671066483208,
    0.1483525285505606,
    -0.13897999621011298,
    0.03561334337852199,
)


def gelu_and_slope(u):
    a = jnp.abs(u) * 0.7071067811865476
    t = 1.0 / (1.0 + ERFC_SLOPE * a)
    q = jnp.full_like(t, ERFC_COEFS[-1])
    for c in ERFC_COEFS[-2::-1]:
        q = q * t + c
    e = jnp.exp(-(a * a))
    tail = e * (t * q)
    phi = jnp.where(u < 0, tail, 1.0 - tail)
    return u * phi, phi + u * (e * 0.3989422804014327)


def nn(a, b):
    return lax.dot_general(a, b, NN, preferred_element_type=f32)


def nt(a, b):
    return lax.dot_general(a, b, NT, preferred_element_type=f32)


def tn(a, b):
    return lax.dot_general(a, b, (((0,), (0,)), ((), ())), preferred_element_type=f32)


def norm_rows(r, gain, shift):
    center = r - jnp.mean(r, -1, keepdims=True)
    inv = lax.rsqrt(jnp.mean(center * center, -1, keepdims=True) + NORM_EPS)
    n = center * inv
    return n * gain + shift, n, inv


def norm_rows_back(e, n, inv, gain):
    eg = e * gain
    grad = inv * (eg - jnp.mean(eg, -1, keepdims=True) - n * jnp.mean(eg * n, -1, keepdims=True))
    return grad, jnp.sum(e * n, 0), jnp.sum(e, 0), jnp.sum(grad, 0)


def trade(x):
    return lax.ppermute(x, "tp", [(0, 1), (1, 0)])


def in_order(place, own, other, axis=0):
    return jnp.where(
        place == 0,
        jnp.concatenate([own, other], axis),
        jnp.concatenate([other, own], axis),
    )


def own_sequence(piece, place):
    own = lax.dynamic_index_in_dim(piece, place, 0, keepdims=False)
    away = lax.dynamic_index_in_dim(piece, 1 - place, 0, keepdims=False)
    return in_order(place, own, trade(away))


def to_pieces(rows, place):
    half = rows.shape[0] // 2
    halves = rows.reshape(2, half, rows.shape[1])
    own = lax.dynamic_index_in_dim(halves, place, 0, keepdims=True)
    away = lax.dynamic_index_in_dim(halves, 1 - place, 0, keepdims=True)
    return in_order(place, own, trade(away))


def sum_everywhere(x, fsdp_count):
    step = 1
    while step < fsdp_count:
        x = x + lax.ppermute(x, "fsdp", [(i, i ^ step) for i in range(fsdp_count)])
        step *= 2
    return x + trade(x)


def whole_sequences(
    layer_in,
    memory,
    out_grad,
    w_self_in,
    w_self_out,
    w_cross_in,
    w_cross_out,
    w_up,
    w_down,
    head_bias,
    up_bias,
    norm_gain,
    row_bias,
):
    place = lax.axis_index("tp")
    fsdp_count = lax.axis_size("fsdp")
    width = layer_in.shape[2]
    cols = w_self_in.shape[2]
    units = w_up.shape[1]
    shard = w_self_in.shape[0]
    gains = norm_gain.astype(f32)
    shifts = row_bias.astype(f32)

    def gather(*parts):
        mine = jnp.concatenate(parts, 1) if len(parts) > 1 else parts[0]
        both = lax.all_gather(mine, ("tp", "fsdp"), axis=0, tiled=True)
        return both.reshape(2, width, mine.shape[1])

    def scatter(parts):
        low = jnp.concatenate([p.astype(bf16) for p in parts], 0)
        return lax.psum_scatter(low, ("tp", "fsdp"), scatter_dimension=0, tiled=True).astype(f32)

    small = jnp.concatenate([head_bias.reshape(-1), up_bias])
    small = in_order(place, small[None], trade(small)[None])
    hb = small[:, : 4 * cols].reshape(2, 4, cols).astype(f32)
    ub = small[:, 4 * cols :].astype(f32)

    g_self = gather(w_self_in.reshape(shard, 3 * cols), w_self_out.T)
    g_cross = gather(w_cross_in.reshape(shard, 3 * cols), w_cross_out.T)
    g_ffn = gather(w_up, w_down.T)
    c3 = 3 * cols

    x = own_sequence(layer_in, place)
    mem = own_sequence(memory, place)
    cot = own_sequence(out_grad, place)
    xf = x.astype(f32)
    halves = (0, 1)
    zero = jnp.zeros((cols,), f32)
    scale3 = jnp.concatenate([zero + ATT_SCALE, zero + 1.0, zero + 1.0])
    blk = cols // 128

    sy, sa, sl = [], [], []
    for t in halves:
        bias = jnp.concatenate([hb[t, 0], zero, hb[t, 1]])
        y = ((nn(x, g_self[t, :, :c3]) + bias) * scale3).astype(bf16)
        o, lse = att_fwd(y, y, y, True, 512, 0, blk, 2 * blk, cols)
        sy.append(y)
        sa.append(o)
        sl.append(lse)
    r1 = xf + (nt(sa[0], g_self[0, :, c3:]) + nt(sa[1], g_self[1, :, c3:])) + shifts[0]
    h1, n1, i1 = norm_rows(r1, gains[0], shifts[3])
    h1b = h1.astype(bf16)

    cq, ckv, ca, cl = [], [], [], []
    for t in halves:
        kv = (nn(mem, g_cross[t, :, cols:c3]) + jnp.concatenate([zero, hb[t, 3]])).astype(bf16)
        q = ((nn(h1b, g_cross[t, :, :cols]) + hb[t, 2]) * ATT_SCALE).astype(bf16)
        o, lse = att_fwd(q, kv, kv, False, 512, 0, 0, blk, cols)
        cq.append(q)
        ckv.append(kv)
        ca.append(o)
        cl.append(lse)
    r2 = h1 + (nt(ca[0], g_cross[0, :, c3:]) + nt(ca[1], g_cross[1, :, c3:])) + shifts[1]
    h2, n2, i2 = norm_rows(r2, gains[1], shifts[4])
    h2b = h2.astype(bf16)

    act, slope = [], []
    for t in halves:
        g, d = gelu_and_slope(nn(h2b, g_ffn[t, :, :units]) + ub[t])
        act.append(g.astype(bf16))
        slope.append(d.astype(bf16))
    r3 = h2 + (nt(act[0], g_ffn[0, :, units:]) + nt(act[1], g_ffn[1, :, units:])) + shifts[2]
    h3, n3, i3 = norm_rows(r3, gains[2], shifts[5])
    mixed = to_pieces(h3.astype(bf16), place)

    dr3, gg3, gs3, gb3 = norm_rows_back(cot.astype(f32), n3, i3, gains[2])
    e3 = dr3.astype(bf16)
    du = [(nn(e3, g_ffn[t, :, units:]) * slope[t].astype(f32)).astype(bf16) for t in halves]
    s_ffn = scatter(
        [jnp.concatenate([tn(h2b, du[t]), tn(e3, act[t])], 1) for t in halves]
    )
    gu = jnp.stack([jnp.sum(du[t].astype(f32), 0) for t in halves])
    dh2 = dr3 + (nt(du[0], g_ffn[0, :, :units]) + nt(du[1], g_ffn[1, :, :units]))
    dr2, gg2, gs2, gb2 = norm_rows_back(dh2, n2, i2, gains[1])
    e2 = dr2.astype(bf16)

    dcq, dck, dcv = [], [], []
    for t in halves:
        da = nn(e2, g_cross[t, :, c3:]).astype(bf16)
        a, b, c = att_bwd(cq[t], ckv[t], ckv[t], ca[t], da, cl[t], False, 256, 0, 0, blk)
        dcq.append(a)
        dck.append(b)
        dcv.append(c)
    grad_cross = [
        jnp.concatenate(
            [tn(h1b, dcq[t]), tn(mem, dck[t]), tn(mem, dcv[t]), tn(e2, ca[t])], 1
        )
        for t in halves
    ]
    dmem = sum(
        nt(dck[t], g_cross[t, :, cols : 2 * cols]) + nt(dcv[t], g_cross[t, :, 2 * cols : c3])
        for t in halves
    )
    d_memory = to_pieces(dmem.astype(bf16), place)
    dh1 = dr2 + (nt(dcq[0], g_cross[0, :, :cols]) + nt(dcq[1], g_cross[1, :, :cols]))
    dr1, gg1, gs1, gb1 = norm_rows_back(dh1, n1, i1, gains[0])
    e1 = dr1.astype(bf16)

    dsq, dsk, dsv = [], [], []
    for t in halves:
        da = nn(e1, g_self[t, :, c3:]).astype(bf16)
        y = sy[t]
        a, b, c = att_bwd(y, y, y, sa[t], da, sl[t], True, 256, 0, blk, 2 * blk)
        dsq.append(a)
        dsk.append(b)
        dsv.append(c)
    grad_self = [
        jnp.concatenate([tn(x, dsq[t]), tn(x, dsk[t]), tn(x, dsv[t]), tn(e1, sa[t])], 1)
        for t in halves
    ]
    s_att = scatter([jnp.concatenate([grad_cross[t], grad_self[t]], 1) for t in halves])
    dx = dr1 + sum(
        nt(dsq[t], g_self[t, :, :cols])
        + nt(dsk[t], g_self[t, :, cols : 2 * cols])
        + nt(dsv[t], g_self[t, :, 2 * cols : c3])
        for t in halves
    )
    d_layer_in = to_pieces(dx.astype(bf16), place)

    def col_sums(pair):
        return jnp.stack([jnp.sum(p.astype(f32), 0) for p in pair])

    gh = jnp.stack([col_sums(dsq), col_sums(dsv), col_sums(dcq), col_sums(dcv)], 1)
    flat = jnp.concatenate(
        [
            v.reshape(-1)
            for v in (gh, gu, gg1, gg2, gg3, gb1, gb2, gb3, gs1, gs2, gs3)
        ]
    )
    flat = sum_everywhere(flat.reshape(-1, 128), fsdp_count).reshape(-1)
    head_sum = lax.dynamic_index_in_dim(flat[: 8 * cols].reshape(2, 4, cols), place, 0, False)
    unit_sum = lax.dynamic_index_in_dim(
        flat[8 * cols : 8 * cols + 2 * units].reshape(2, units), place, 0, False
    )
    rest = flat[8 * cols + 2 * units :].reshape(9, width)

    cross_part, self_part = s_att[:, : 4 * cols], s_att[:, 4 * cols :]
    return (
        mixed,
        d_layer_in,
        d_memory,
        self_part[:, :c3].reshape(shard, 3, cols),
        self_part[:, c3:].T,
        cross_part[:, :c3].reshape(shard, 3, cols),
        cross_part[:, c3:].T,
        s_ffn[:, :units],
        s_ffn[:, units:].T,
        head_sum,
        unit_sum,
        rest[:3],
        rest[3:],
    )


def on_device(layer_in, *rest):
    fsdp_count = lax.axis_size("fsdp")
    pair = lax.axis_size("tp") == 2 and layer_in.shape[0] == 2
    if pair and fsdp_count & (fsdp_count - 1) == 0:
        return whole_sequences(layer_in, *rest)
    return shared_sequences(layer_in, *rest)


def solution(mesh):
    return jax.shard_map(
        on_device,
        mesh=mesh,
        in_specs=(
            P("fsdp", "tp", None),
            P("fsdp", "tp", None),
            P("fsdp", "tp", None),
            P("fsdp", None, "tp"),
            P("tp", "fsdp"),
            P("fsdp", None, "tp"),
            P("tp", "fsdp"),
            P("fsdp", "tp"),
            P("tp", "fsdp"),
            P(None, "tp"),
            P("tp"),
            P(),
            P(),
        ),
        out_specs=(
            P("fsdp", "tp", None),
            P("fsdp", "tp", None),
            P("fsdp", "tp", None),
            P("fsdp", None, "tp"),
            P("tp", "fsdp"),
            P("fsdp", None, "tp"),
            P("tp", "fsdp"),
            P("fsdp", "tp"),
            P("tp", "fsdp"),
            P(None, "tp"),
            P("tp"),
            P(),
            P(),
        ),
        check_vma=False,
    )
```

```python
import functools

import jax
import jax.numpy as jnp
from jax import lax
from jax.experimental import pallas as pl
from jax.experimental.pallas import tpu as pltpu
from jax.sharding import PartitionSpec as P

HD = 64
NORM_EPS = 1e-05
ATT_SCALE = 0.125


def times_back(left, right):
    return lax.dot_general(
        left, right, (((1,), (1,)), ((), ())), preferred_element_type=jnp.float32
    )


def over_rows(left, right):
    return lax.dot_general(
        left, right, (((0,), (0,)), ((), ())), preferred_element_type=jnp.float32
    )


def whole_rows(piece):
    return lax.all_gather(piece, "tp", axis=1, tiled=True)


def whole_grads(piece):
    return lax.all_gather(piece, "tp", axis=1, tiled=True)


def branch_sum(term):
    return lax.psum_scatter(
        term.astype(jnp.bfloat16), "tp", scatter_dimension=1, tiled=True
    ).astype(jnp.float32)


def piece_sum(term):
    return lax.psum_scatter(
        term.astype(jnp.bfloat16), "tp", scatter_dimension=1, tiled=True
    ).astype(jnp.float32)


def norm_forward(resid, gain, shift):
    center = resid - jnp.mean(resid, -1, keepdims=True)
    spread = jnp.mean(center * center, -1, keepdims=True)
    inv_std = lax.rsqrt(spread + NORM_EPS)
    normed = center * inv_std
    return (normed * gain + shift, normed, inv_std)


def norm_backward(grad_out, normed, inv_std, gain):
    grad_normed = grad_out * gain
    grad_resid = inv_std * (
        grad_normed
        - jnp.mean(grad_normed, -1, keepdims=True)
        - normed * jnp.mean(grad_normed * normed, -1, keepdims=True)
    )
    return (grad_resid, jnp.sum(grad_out * normed, (0, 1)), jnp.sum(grad_out, (0, 1)))


def gelu_exact(pre_act):
    return jax.nn.gelu(pre_act, approximate=False)


def gelu_back(pre_act, grad_act):
    unused_out, pull_back = jax.vjp(gelu_exact, pre_act)
    return pull_back(grad_act)[0]


def masked_scores(query_blk, block_start, keys_seq, causal):
    scores = jnp.einsum("qhc,khc->hqk", query_blk, keys_seq, preferred_element_type=jnp.float32)
    if causal:
        row_pos = block_start + lax.broadcasted_iota(jnp.int32, scores.shape[1:], 0)
        col_pos = lax.broadcasted_iota(jnp.int32, scores.shape[1:], 1)
        scores = jnp.where(row_pos >= col_pos, scores, -1e30)
    return scores


def attend_forward(query, keys, values, causal):
    seq_count, length, heads_dev, depth = query.shape
    block_rows = min(512, length)
    block_count = length // block_rows
    block_starts = jnp.arange(block_count, dtype=jnp.int32) * block_rows

    def one_sequence(seq_item):
        query_seq, keys_seq, values_seq = seq_item

        def one_block(blk_item):
            query_blk, block_start = blk_item
            scores = masked_scores(query_blk, block_start, keys_seq, causal)
            row_max = jnp.max(scores, -1, keepdims=True)
            log_total = row_max + jnp.log(jnp.sum(jnp.exp(scores - row_max), -1, keepdims=True))
            probs = jnp.exp(scores - log_total).astype(jnp.bfloat16)
            block_out = jnp.einsum(
                "hqk,khc->qhc", probs, values_seq, preferred_element_type=jnp.float32
            )
            return (block_out.astype(jnp.bfloat16), log_total)

        block_outs, log_totals = lax.map(
            one_block, (query_seq.reshape(block_count, block_rows, heads_dev, depth), block_starts)
        )
        return (block_outs.reshape(length, heads_dev, depth), log_totals)

    return lax.map(one_sequence, (query, keys, values))


def attend_backward(query, keys, values, log_totals, grad_out, causal):
    seq_count, length, heads_dev, depth = query.shape
    block_rows = min(512, length)
    block_count = length // block_rows
    block_starts = jnp.arange(block_count, dtype=jnp.int32) * block_rows

    def one_sequence(seq_item):
        query_seq, keys_seq, values_seq, total_seq, grad_seq = seq_item

        def one_block(carry, blk_item):
            query_blk, grad_blk, total_blk, block_start = blk_item
            probs = jnp.exp(masked_scores(query_blk, block_start, keys_seq, causal) - total_blk)
            grad_probs = jnp.einsum(
                "qhc,khc->hqk", grad_blk, values_seq, preferred_element_type=jnp.float32
            )
            row_delta = jnp.sum(probs * grad_probs, -1, keepdims=True)
            grad_scores = (probs * (grad_probs - row_delta)).astype(jnp.bfloat16)
            grad_query = jnp.einsum(
                "hqk,khc->qhc", grad_scores, keys_seq, preferred_element_type=jnp.float32
            )
            grad_keys = carry[0] + jnp.einsum(
                "hqk,qhc->khc", grad_scores, query_blk, preferred_element_type=jnp.float32
            )
            grad_values = carry[1] + jnp.einsum(
                "hqk,qhc->khc",
                probs.astype(jnp.bfloat16),
                grad_blk,
                preferred_element_type=jnp.float32,
            )
            return ((grad_keys, grad_values), grad_query)

        zero_keys = jnp.zeros(keys_seq.shape, jnp.float32)
        blk_items = (
            query_seq.reshape(block_count, block_rows, heads_dev, depth),
            grad_seq.reshape(block_count, block_rows, heads_dev, depth),
            total_seq,
            block_starts,
        )
        (grad_keys, grad_values), grad_query = lax.scan(
            one_block, (zero_keys, zero_keys), blk_items
        )
        return (grad_query.reshape(length, heads_dev, depth), grad_keys, grad_values)

    return lax.map(one_sequence, (query, keys, values, log_totals, grad_out))


def shared_sequences(
    layer_in,
    memory,
    out_grad,
    w_self_in,
    w_self_out,
    w_cross_in,
    w_cross_out,
    w_up,
    w_down,
    head_bias,
    up_bias,
    norm_gain,
    row_bias,
):
    seq_count, piece_len, model_width = layer_in.shape
    head_cols = w_self_in.shape[2]
    unit_cols = w_up.shape[1]
    heads_dev = head_cols // HD
    tp_place = lax.axis_index("tp")
    tp_count = lax.axis_size("tp")
    zero_index = jnp.zeros((), jnp.int32)
    gains = norm_gain.astype(jnp.float32)
    shifts = row_bias.astype(jnp.float32)
    col_bias = head_bias.astype(jnp.float32)
    unit_bias = up_bias.astype(jnp.float32)
    self_in, self_out, cross_in, cross_out, up_full, down_full = (
        lax.all_gather(w_self_in, "fsdp", axis=0, tiled=True),
        lax.all_gather(w_self_out, "fsdp", axis=1, tiled=True),
        lax.all_gather(w_cross_in, "fsdp", axis=0, tiled=True),
        lax.all_gather(w_cross_out, "fsdp", axis=1, tiled=True),
        lax.all_gather(w_up, "fsdp", axis=0, tiled=True),
        lax.all_gather(w_down, "fsdp", axis=1, tiled=True),
    )
    layer_whole = whole_rows(layer_in)
    length = layer_whole.shape[1]
    row_count = seq_count * length
    token_rows = layer_whole.reshape(row_count, model_width)
    self_proj = jnp.einsum("rd,dkc->rkc", token_rows, self_in, preferred_element_type=jnp.float32)
    self_query = ((self_proj[:, 0] + col_bias[0]) * ATT_SCALE).astype(jnp.bfloat16)
    self_keys = self_proj[:, 1].astype(jnp.bfloat16)
    self_values = (self_proj[:, 2] + col_bias[1]).astype(jnp.bfloat16)
    head_shape = (seq_count, length, heads_dev, HD)
    self_att, self_totals = attend_forward(
        self_query.reshape(head_shape),
        self_keys.reshape(head_shape),
        self_values.reshape(head_shape),
        True,
    )
    self_rows = self_att.reshape(row_count, head_cols)
    self_term = jnp.dot(self_rows, self_out, preferred_element_type=jnp.float32).reshape(
        seq_count, length, model_width
    )
    resid_one = layer_in.astype(jnp.float32) + branch_sum(self_term) + shifts[0]
    normed_one, unit_one, inv_one = norm_forward(resid_one, gains[0], shifts[3])
    normed_rows = whole_rows(normed_one.astype(jnp.bfloat16)).reshape(row_count, model_width)
    cross_query = (
        (jnp.dot(normed_rows, cross_in[:, 0], preferred_element_type=jnp.float32) + col_bias[2])
        * ATT_SCALE
    ).astype(jnp.bfloat16)
    memory_whole = lax.all_gather(memory, "tp", axis=1, tiled=True)
    source_len = memory_whole.shape[1]
    source_rows = memory_whole.reshape(seq_count * source_len, model_width)
    cross_proj = jnp.einsum(
        "rd,dkc->rkc", source_rows, cross_in[:, 1:], preferred_element_type=jnp.float32
    )
    cross_keys = cross_proj[:, 0].astype(jnp.bfloat16)
    cross_values = (cross_proj[:, 1] + col_bias[3]).astype(jnp.bfloat16)
    source_shape = (seq_count, source_len, heads_dev, HD)
    cross_att, cross_totals = attend_forward(
        cross_query.reshape(head_shape),
        cross_keys.reshape(source_shape),
        cross_values.reshape(source_shape),
        False,
    )
    cross_rows = cross_att.reshape(row_count, head_cols)
    cross_term = jnp.dot(cross_rows, cross_out, preferred_element_type=jnp.float32).reshape(
        seq_count, length, model_width
    )
    resid_two = normed_one + branch_sum(cross_term) + shifts[1]
    normed_two, unit_two, inv_two = norm_forward(resid_two, gains[1], shifts[4])
    normed_two_low = normed_two.astype(jnp.bfloat16)
    ffn_rows = whole_rows(normed_two_low).reshape(row_count, model_width)
    pre_act = jnp.dot(ffn_rows, up_full, preferred_element_type=jnp.float32) + unit_bias
    hidden_act = gelu_exact(pre_act).astype(jnp.bfloat16)
    ffn_term = jnp.dot(hidden_act, down_full, preferred_element_type=jnp.float32).reshape(
        seq_count, length, model_width
    )
    ffn_out = branch_sum(ffn_term)
    resid_three = normed_two + ffn_out + shifts[2]
    mixed, unit_three, inv_three = norm_forward(resid_three, gains[2], shifts[5])
    grad_three, gain_grad_three, shift_grad_three = norm_backward(
        out_grad.astype(jnp.float32), unit_three, inv_three, gains[2]
    )
    bias_grad_three = jnp.sum(grad_three, (0, 1))
    grad_three_low = grad_three.astype(jnp.bfloat16)
    grad_rows = whole_grads(grad_three_low).reshape(row_count, model_width)
    grad_act = times_back(grad_rows, down_full)
    grad_pre = gelu_back(pre_act, grad_act).astype(jnp.bfloat16)
    d_up = over_rows(ffn_rows, grad_pre)
    d_down = over_rows(hidden_act, grad_rows)
    unit_grad = jnp.sum(grad_pre, 0, dtype=jnp.float32)
    grad_two_in = piece_sum(times_back(grad_pre, up_full).reshape(seq_count, length, model_width))
    grad_normed_two = grad_three + grad_two_in
    grad_two, gain_grad_two, shift_grad_two = norm_backward(
        grad_normed_two, unit_two, inv_two, gains[1]
    )
    bias_grad_two = jnp.sum(grad_two, (0, 1))
    grad_two_rows = whole_grads(grad_two.astype(jnp.bfloat16)).reshape(row_count, model_width)
    d_cross_out = over_rows(cross_rows, grad_two_rows)
    grad_cross_att = times_back(grad_two_rows, cross_out).astype(jnp.bfloat16)
    cq_grad, ck_grad, cv_grad = attend_backward(
        cross_query.reshape(head_shape),
        cross_keys.reshape(source_shape),
        cross_values.reshape(source_shape),
        cross_totals,
        grad_cross_att.reshape(head_shape),
        False,
    )
    cq_pre = cq_grad.reshape(row_count, head_cols).astype(jnp.bfloat16) * jnp.asarray(
        ATT_SCALE, jnp.bfloat16
    )
    ckv_low = jnp.stack(
        [
            ck_grad.reshape(seq_count * source_len, head_cols),
            cv_grad.reshape(seq_count * source_len, head_cols),
        ],
        1,
    ).astype(jnp.bfloat16)
    cross_q_grad = over_rows(normed_rows, cq_pre)
    cq_bias_grad = jnp.sum(cq_pre, 0, dtype=jnp.float32)
    normed_part = times_back(cq_pre, cross_in[:, 0]).reshape(seq_count, length, model_width)
    source_part = jnp.einsum(
        "rkc,dkc->rd", ckv_low, cross_in[:, 1:], preferred_element_type=jnp.float32
    ).reshape(seq_count, source_len, model_width)
    grad_one_in, memory_grad = (
        lax.psum_scatter(
            normed_part.astype(jnp.bfloat16), "tp", scatter_dimension=1, tiled=True
        ).astype(jnp.float32),
        lax.psum_scatter(
            source_part.astype(jnp.bfloat16), "tp", scatter_dimension=1, tiled=True
        ).astype(jnp.float32),
    )
    d_memory = memory_grad.astype(jnp.bfloat16)
    cross_kv_grad = jnp.einsum(
        "rd,rkc->dkc", source_rows, ckv_low, preferred_element_type=jnp.float32
    )
    cross_grad_term = jnp.concatenate([cross_q_grad[:, None, :], cross_kv_grad], 1)
    cv_own = jnp.sum(ckv_low[:, 1], 0, dtype=jnp.float32)
    cv_wide = lax.dynamic_update_slice(
        jnp.zeros((head_cols * tp_count,), jnp.float32), cv_own, (tp_place * head_cols,)
    )
    grad_normed_one = grad_two + grad_one_in
    grad_one, gain_grad_one, shift_grad_one = norm_backward(
        grad_normed_one, unit_one, inv_one, gains[0]
    )
    bias_grad_one = jnp.sum(grad_one, (0, 1))
    grad_one_rows = whole_grads(grad_one.astype(jnp.bfloat16)).reshape(row_count, model_width)
    d_self_out = over_rows(self_rows, grad_one_rows)
    grad_self_att = times_back(grad_one_rows, self_out).astype(jnp.bfloat16)
    sq_grad, sk_grad, sv_grad = attend_backward(
        self_query.reshape(head_shape),
        self_keys.reshape(head_shape),
        self_values.reshape(head_shape),
        self_totals,
        grad_self_att.reshape(head_shape),
        True,
    )
    sq_pre = sq_grad.reshape(row_count, head_cols).astype(jnp.bfloat16) * jnp.asarray(
        ATT_SCALE, jnp.bfloat16
    )
    sqkv_low = jnp.stack(
        [
            sq_pre,
            sk_grad.reshape(row_count, head_cols).astype(jnp.bfloat16),
            sv_grad.reshape(row_count, head_cols).astype(jnp.bfloat16),
        ],
        1,
    )
    d_self_in = jnp.einsum("rd,rkc->dkc", token_rows, sqkv_low, preferred_element_type=jnp.float32)
    sq_bias_grad = jnp.sum(sq_pre, 0, dtype=jnp.float32)
    sv_bias_grad = jnp.sum(sqkv_low[:, 2], 0, dtype=jnp.float32)
    layer_part = jnp.einsum(
        "rkc,dkc->rd", sqkv_low, self_in, preferred_element_type=jnp.float32
    ).reshape(seq_count, length, model_width)
    d_layer_in = (grad_one + piece_sum(layer_part)).astype(jnp.bfloat16)
    slot_grad = jnp.stack([sq_bias_grad, sv_bias_grad, cq_bias_grad])
    slot_wide = lax.dynamic_update_slice(
        jnp.zeros((3, head_cols * tp_count), jnp.float32),
        slot_grad,
        (zero_index, tp_place * head_cols),
    )
    head_wide = jnp.concatenate([slot_wide, cv_wide[None, :]], 0)
    unit_wide_grad = lax.dynamic_update_slice(
        jnp.zeros((unit_cols * tp_count,), jnp.float32), unit_grad, (tp_place * unit_cols,)
    )
    gain_grads = jnp.stack([gain_grad_one, gain_grad_two, gain_grad_three])
    shift_grads = jnp.stack(
        [
            bias_grad_one,
            bias_grad_two,
            bias_grad_three,
            shift_grad_one,
            shift_grad_two,
            shift_grad_three,
        ]
    )
    gain_total, shift_total, head_total, unit_total = lax.psum(
        (gain_grads, shift_grads, head_wide, unit_wide_grad), ("fsdp", "tp")
    )
    d_head_bias = lax.dynamic_slice(head_total, (zero_index, tp_place * head_cols), (4, head_cols))
    d_up_bias = lax.dynamic_slice(unit_total, (tp_place * unit_cols,), (unit_cols,))
    g_self_in, g_self_out, g_cross_part, g_cross_out, g_up, g_down = (
        lax.psum_scatter(
            d_self_in.astype(jnp.bfloat16), "fsdp", scatter_dimension=0, tiled=True
        ).astype(jnp.float32),
        lax.psum_scatter(
            d_self_out.astype(jnp.bfloat16), "fsdp", scatter_dimension=1, tiled=True
        ).astype(jnp.float32),
        lax.psum_scatter(
            cross_grad_term.astype(jnp.bfloat16), "fsdp", scatter_dimension=0, tiled=True
        ).astype(jnp.float32),
        lax.psum_scatter(
            d_cross_out.astype(jnp.bfloat16), "fsdp", scatter_dimension=1, tiled=True
        ).astype(jnp.float32),
        lax.psum_scatter(d_up.astype(jnp.bfloat16), "fsdp", scatter_dimension=0, tiled=True).astype(
            jnp.float32
        ),
        lax.psum_scatter(
            d_down.astype(jnp.bfloat16), "fsdp", scatter_dimension=1, tiled=True
        ).astype(jnp.float32),
    )
    return (
        mixed.astype(jnp.bfloat16),
        d_layer_in,
        d_memory,
        g_self_in,
        g_self_out,
        g_cross_part,
        g_cross_out,
        g_up,
        g_down,
        d_head_bias,
        d_up_bias,
        gain_total,
        shift_total,
    )


NT=(((1,),(1,)),((),()))
NN=(((1,),(0,)),((),()))
f32=jnp.float32
bf16=jnp.bfloat16

def scores_t(k_h,q,i,bq,causal):
    s=lax.dot_general(k_h,q,NT,preferred_element_type=f32)
    return s

def att_fwd_kernel(q_ref,k_ref,v_ref,o_ref,lse_ref,*,bq,causal):
    n=q_ref.shape[0]; nk=k_ref.shape[0]
    lane=lax.broadcasted_iota(jnp.int32,(nk,128),1)
    k=k_ref[...]; v=v_ref[...]
    zero=jnp.zeros((),bf16)
    kh=[jnp.where(lane<HD,k,zero),jnp.where(lane>=HD,k,zero)]
    vt=v.astype(f32).T.astype(bf16)
    ones=jnp.ones((8,nk),bf16)
    vh=[jnp.concatenate([vt[h*HD:(h+1)*HD],ones],0) for h in range(2)]
    for i in range(n//bq):
        q=q_ref[i*bq:(i+1)*bq,:]
        L=(i+1)*bq if causal else nk
        outs=[];lses=[]
        for h in range(2):
            s=lax.dot_general(kh[h][:L],q,NT,preferred_element_type=f32)
            if causal:
                keep=lax.broadcasted_iota(jnp.int32,(bq,bq),0)<=lax.broadcasted_iota(jnp.int32,(bq,bq),1)
                sd=jnp.where(keep,s[L-bq:],-1e30)
                s=jnp.concatenate([s[:L-bq],sd],0) if L>bq else sd
            m=jnp.max(s,0,keepdims=True)
            p=jnp.exp(s-m).astype(bf16)
            ol=lax.dot_general(vh[h][:,:L],p,NN,preferred_element_type=f32)
            l=ol[HD:HD+1]
            outs.append(ol[:HD]*(1.0/l))
            lses.append(m+jnp.log(l))
        ot=jnp.concatenate(outs,0)
        o_ref[i*bq:(i+1)*bq,:]=ot.T.astype(bf16)
        lse_ref[0,:,i*bq:(i+1)*bq]=jnp.concatenate(lses,0)

def att_fwd(q,k,v,causal,bq=256,qo=0,ko=0,vo=0,width=None):
    n=q.shape[0]; nk=k.shape[0]; width=width or q.shape[1]; np_=width//128
    spec=lambda rows,off: pl.BlockSpec((rows,128),lambda p: (0,p+off))
    return pl.pallas_call(
        functools.partial(att_fwd_kernel,bq=bq,causal=causal),
        grid=(np_,),
        in_specs=[spec(n,qo),spec(nk,ko),spec(nk,vo)],
        out_specs=[spec(n,0),pl.BlockSpec((1,2,n),lambda p:(p,0,0))],
        out_shape=[jax.ShapeDtypeStruct((n,width),bf16),jax.ShapeDtypeStruct((np_,2,n),f32)],
        compiler_params=pltpu.CompilerParams(dimension_semantics=("arbitrary",),vmem_limit_bytes=56*2**20),
    )(q,k,v)

def att_bwd_kernel(q_ref,k_ref,v_ref,o_ref,do_ref,lse_ref,dq_ref,dk_ref,dv_ref,dk_acc,dv_acc,*,bq,causal):
    n=q_ref.shape[0]; nk=k_ref.shape[0]
    lane=lax.broadcasted_iota(jnp.int32,(nk,128),1)
    lq=lax.broadcasted_iota(jnp.int32,(bq,128),1)
    k=k_ref[...]; v=v_ref[...]
    zero=jnp.zeros((),bf16)
    kh=[jnp.where(lane<HD,k,zero),jnp.where(lane>=HD,k,zero)]
    vh=[jnp.where(lane<HD,v,zero),jnp.where(lane>=HD,v,zero)]
    kt=k.astype(f32).T.astype(bf16)
    dk_acc[...]=jnp.zeros_like(dk_acc); dv_acc[...]=jnp.zeros_like(dv_acc)
    for i in range(n//bq):
        rows=slice(i*bq,(i+1)*bq)
        q=q_ref[rows,:]; do=do_ref[rows,:]
        L=(i+1)*bq if causal else nk
        dot_=(do.astype(f32)*o_ref[rows,:].astype(f32)).T
        qm=[jnp.where(lq<HD,q,zero),jnp.where(lq>=HD,q,zero)]
        dm=[jnp.where(lq<HD,do,zero),jnp.where(lq>=HD,do,zero)]
        dqs=[]
        for h in range(2):
            s=lax.dot_general(kh[h][:L],q,NT,preferred_element_type=f32)
            dp=lax.dot_general(vh[h][:L],do,NT,preferred_element_type=f32)
            lse=lse_ref[0,h:h+1,rows]
            delta=jnp.sum(dot_[h*HD:(h+1)*HD],0,keepdims=True)
            if causal:
                keep=lax.broadcasted_iota(jnp.int32,(bq,bq),0)<=lax.broadcasted_iota(jnp.int32,(bq,bq),1)
                sd=jnp.where(keep,s[L-bq:],-1e30)
                s=jnp.concatenate([s[:L-bq],sd],0) if L>bq else sd
            p=jnp.exp(s-lse)
            ds=(p*(dp-delta)).astype(bf16)
            pb=p.astype(bf16)
            dv_acc[:L,:]+=lax.dot_general(pb,dm[h],NN,preferred_element_type=f32)
            dk_acc[:L,:]+=lax.dot_general(ds,qm[h],NN,preferred_element_type=f32)
            dqs.append(lax.dot_general(kt[h*HD:(h+1)*HD,:L],ds,NN,preferred_element_type=f32))
        dq_ref[rows,:]=(jnp.concatenate(dqs,0)*0.125).T.astype(bf16)
    dk_ref[...]=dk_acc[...].astype(bf16)
    dv_ref[...]=dv_acc[...].astype(bf16)

def att_bwd(q,k,v,o,do,lse,causal,bq=256,qo=0,ko=0,vo=0):
    n=q.shape[0]; nk=k.shape[0]; width=o.shape[1]; np_=width//128
    spec=lambda rows,off: pl.BlockSpec((rows,128),lambda p: (0,p+off))
    return pl.pallas_call(
        functools.partial(att_bwd_kernel,bq=bq,causal=causal),
        grid=(np_,),
        in_specs=[spec(n,qo),spec(nk,ko),spec(nk,vo),spec(n,0),spec(n,0),pl.BlockSpec((1,2,n),lambda p:(p,0,0))],
        out_specs=[spec(n,0),spec(nk,0),spec(nk,0)],
        out_shape=[jax.ShapeDtypeStruct((n,width),bf16),jax.ShapeDtypeStruct((nk,width),bf16),jax.ShapeDtypeStruct((nk,width),bf16)],
        scratch_shapes=[pltpu.VMEM((nk,128),f32)]*2,
        compiler_params=pltpu.CompilerParams(dimension_semantics=("arbitrary",),vmem_limit_bytes=56*2**20),
    )(q,k,v,o,do,lse)


MESH = pl.DeviceIdType.MESH
LINKS = ("z1", "z2", "y", "x", "c")


def partners():
    t = lax.axis_index("tp")
    f = lax.axis_index("fsdp")
    z, y, c = f // 4, (f // 2) % 2, f % 2

    def at(z_, y_, c_, t_):
        return (z_ * 4 + y_ * 2 + c_, t_)

    ids = dict(
        z1=at(z + 1 - 2 * (z % 2), y, c, t),
        z2=at((z + 2) % 4, y, c, t),
        y=at(z, 1 - y, c, t),
        x=at(z, y, c, 1 - t),
        c=at(z, y, 1 - c, t),
    )
    return (t, z, y, c), ids


def greet(ids):
    barrier = pltpu.get_barrier_semaphore()
    for name in LINKS:
        pl.semaphore_signal(barrier, inc=1, device_id=ids[name], device_id_type=MESH)
    pl.semaphore_wait(barrier, len(LINKS))


def pipeline(chunks, stages, begin):
    started = {}
    for step in range(chunks + stages):
        for s in range(stages, -1, -1):
            k = step - s
            if 0 <= k < chunks:
                if s > 0:
                    for copy in started[k, s - 1]:
                        copy.wait_recv()
                started[k, s] = begin(k, s)
    for copies in started.values():
        for copy in copies:
            copy.wait_send()


def gather_kernel(shard_ref, w_ref, send, recv, own, *, cw, chunks):
    (t, z, y, c), ids = partners()
    mine = pltpu.make_async_copy(shard_ref, w_ref.at[t, z, y, c], own)
    mine.start()
    greet(ids)
    pair = (z // 2) * 2
    h = cw // 2

    def begin(k, s):
        both, a, b = pl.ds(k * cw, cw), pl.ds(k * cw, h), pl.ds(k * cw + h, h)
        if s == 0:
            moves = [(shard_ref.at[:, both], w_ref.at[t, z, y, c, :, both], "z1", 0)]
        elif s == 1:
            if k == 0:
                mine.wait()
            r = w_ref.at[t, pl.ds(pair, 2), y, c, :, both]
            moves = [(r, r, "z2", 1)]
        elif s == 2:
            ra, rb = w_ref.at[t, :, y, c, :, a], w_ref.at[t, :, y, c, :, b]
            moves = [(ra, ra, "y", 2), (rb, rb, "x", 3)]
        elif s == 3:
            ra, rb = w_ref.at[t, :, :, c, :, a], w_ref.at[:, :, y, c, :, b]
            moves = [(ra, ra, "x", 4), (rb, rb, "y", 5)]
        elif s == 4:
            r = w_ref.at[:, :, :, c, :, both]
            moves = [(r, r, "c", 6)]
        else:
            moves = []
        copies = []
        for src, dst, to, j in moves:
            copy = pltpu.make_async_remote_copy(
                src_ref=src,
                dst_ref=dst,
                send_sem=send.at[k, j],
                recv_sem=recv.at[k, j],
                device_id=ids[to],
                device_id_type=MESH,
            )
            copy.start()
            copies.append(copy)
        return copies

    pipeline(chunks, 5, begin)


def gather_weights(shard, cid, chunks):
    rows, cols = shard.shape
    whole = pl.pallas_call(
        functools.partial(gather_kernel, cw=cols // chunks, chunks=chunks),
        in_specs=[pl.BlockSpec(memory_space=pltpu.VMEM)],
        out_specs=pl.BlockSpec(memory_space=pl.ANY),
        out_shape=jax.ShapeDtypeStruct((2, 4, 2, 2, rows, cols), shard.dtype),
        scratch_shapes=[
            pltpu.SemaphoreType.DMA((chunks, 7)),
            pltpu.SemaphoreType.DMA((chunks, 7)),
            pltpu.SemaphoreType.DMA,
        ],
        compiler_params=pltpu.CompilerParams(collective_id=cid, has_side_effects=True),
        cost_estimate=pl.CostEstimate(
            flops=0, bytes_accessed=32 * rows * cols * 20, transcendentals=0
        ),
    )(shard)
    return whole.reshape(2, 16 * rows, cols)


def scatter_kernel(*refs, chunks):
    g_refs, refs = refs[: 2 * chunks], refs[2 * chunks :]
    small_ref, out_ref, small_out, own, r1, s2, r2, k2, s3, r3, k3, s4, r4, k4, s5, r5 = refs[:16]
    sm, rm, send, recv, own_sem, small_send, small_recv = refs[16:]
    (t, z, y, c), ids = partners()
    pair = (z // 2) * 2
    away = 2 - pair
    other = 1 - z % 2
    rows = own.shape[3]
    cw = own.shape[4] // chunks
    h = cw // 2

    def loc(k, half):
        return pltpu.make_async_copy(
            g_refs[2 * k + half].at[:, :, c],
            own.at[half, :, :, :, pl.ds(k * cw, cw)],
            own_sem.at[k, half],
        )

    for k in range(chunks):
        loc(k, 0).start()
        loc(k, 1).start()
    greet(ids)

    def go(k, j, src, dst, to):
        copy = pltpu.make_async_remote_copy(
            src_ref=src,
            dst_ref=dst,
            send_sem=send.at[k, j],
            recv_sem=recv.at[k, j],
            device_id=ids[to],
            device_id_type=MESH,
        )
        copy.start()
        return copy

    def small_go(j):
        copy = pltpu.make_async_remote_copy(
            src_ref=sm.at[j],
            dst_ref=rm.at[j],
            send_sem=small_send.at[j],
            recv_sem=small_recv.at[j],
            device_id=ids[("c", "x", "y", "z2", "z1")[j]],
            device_id_type=MESH,
        )
        copy.start()
        return copy

    def up(v):
        return v.astype(f32)

    def begin(k, s):
        ca = slice(k * cw, k * cw + h)
        cb = slice(k * cw + h, (k + 1) * cw)
        if s == 0:
            cols = pl.ds(k * cw, cw)
            return [
                go(k, 7 * half, g_refs[2 * k + half].at[:, :, 1 - c], r1.at[half, :, :, :, cols], "c")
                for half in (0, 1)
            ]
        if s == 1:
            loc(k, 0).wait()
            loc(k, 1).wait()
            shape = (8, rows, h)
            sent = up(own[1 - t, :, :, :, ca]) + up(r1[1 - t, :, :, :, ca])
            s2[k, 0] = sent.astype(bf16).reshape(shape)
            da = go(k, 1, s2.at[k, 0], r2.at[k, 0], "x")
            sent = up(own[:, :, 1 - y, :, cb]) + up(r1[:, :, 1 - y, :, cb])
            s2[k, 1] = sent.astype(bf16).reshape(shape)
            db = go(k, 2, s2.at[k, 1], r2.at[k, 1], "y")
            k2[k, 0] = (up(own[t, :, :, :, ca]) + up(r1[t, :, :, :, ca])).reshape(shape)
            k2[k, 1] = (up(own[:, :, y, :, cb]) + up(r1[:, :, y, :, cb])).reshape(shape)
            return [da, db]
        if s == 2:
            for i in range(4):
                j = 2 * i + 1 - y
                s3[k, 0, i] = (k2[k, 0, j] + up(r2[k, 0, j])).astype(bf16)
            da = go(k, 3, s3.at[k, 0], r3.at[k, 0], "y")
            for i in range(4):
                j = 4 * (1 - t) + i
                s3[k, 1, i] = (k2[k, 1, j] + up(r2[k, 1, j])).astype(bf16)
            db = go(k, 4, s3.at[k, 1], r3.at[k, 1], "x")
            for i in range(4):
                k3[k, 0, i] = k2[k, 0, 2 * i + y] + up(r2[k, 0, 2 * i + y])
                k3[k, 1, i] = k2[k, 1, 4 * t + i] + up(r2[k, 1, 4 * t + i])
            return [da, db]
        if s == 3:
            for j in range(2):
                for i in range(2):
                    s4[k, j, i] = (k3[k, j, away + i] + up(r3[k, j, away + i])).astype(bf16)
            d = go(k, 5, s4.at[k], r4.at[k], "z2")
            for j in range(2):
                for i in range(2):
                    k4[k, j, i] = k3[k, j, pair + i] + up(r3[k, j, pair + i])
            return [d]
        if s == 4:
            for j in range(2):
                s5[k, j] = (k4[k, j, other] + up(r4[k, j, other])).astype(bf16)
            return [go(k, 6, s5.at[k], r5.at[k], "z1")]
        for j in range(2):
            mine = k4[k, j, z % 2] + up(r4[k, j, z % 2]) + up(r5[k, j])
            out_ref[:, k * cw + j * h : k * cw + (j + 1) * h] = mine
        return []

    smalls = []

    def begin_with_small(k, s):
        if k == 0:
            if s == 0:
                sm[0] = small_ref[...]
            else:
                smalls[s - 1].wait_recv()
                total = sm[s - 1] + rm[s - 1]
                if s < 5:
                    sm[s] = total
                else:
                    small_out[...] = total
            if s < 5:
                smalls.append(small_go(s))
        return begin(k, s)

    pipeline(chunks, 5, begin_with_small)
    for copy in smalls:
        copy.wait_send()


def scatter_grads(pairs, small, cid):
    chunks = len(pairs)
    width, cw = pairs[0][0].shape
    rows, h, cols = width // 16, cw // 2, cw * chunks
    V = pltpu.VMEM
    dma = pltpu.SemaphoreType.DMA
    flat = [g.reshape(4, 2, 2, rows, cw) for pair in pairs for g in pair]
    whole = pl.BlockSpec(memory_space=pltpu.VMEM)
    return pl.pallas_call(
        functools.partial(scatter_kernel, chunks=chunks),
        in_specs=[pl.BlockSpec(memory_space=pl.ANY)] * len(flat) + [whole],
        out_specs=[whole, whole],
        out_shape=[
            jax.ShapeDtypeStruct((rows, cols), f32),
            jax.ShapeDtypeStruct(small.shape, f32),
        ],
        scratch_shapes=[
            V((2, 4, 2, rows, cols), bf16),
            V((2, 4, 2, rows, cols), bf16),
            V((chunks, 2, 8, rows, h), bf16),
            V((chunks, 2, 8, rows, h), bf16),
            V((chunks, 2, 8, rows, h), f32),
            V((chunks, 2, 4, rows, h), bf16),
            V((chunks, 2, 4, rows, h), bf16),
            V((chunks, 2, 4, rows, h), f32),
            V((chunks, 2, 2, rows, h), bf16),
            V((chunks, 2, 2, rows, h), bf16),
            V((chunks, 2, 2, rows, h), f32),
            V((chunks, 2, rows, h), bf16),
            V((chunks, 2, rows, h), bf16),
            V((5,) + small.shape, f32),
            V((5,) + small.shape, f32),
            dma((chunks, 8)),
            dma((chunks, 8)),
            dma((chunks, 2)),
            dma((5,)),
            dma((5,)),
        ],
        compiler_params=pltpu.CompilerParams(
            collective_id=cid, has_side_effects=True, vmem_limit_bytes=60 * 2**20
        ),
        cost_estimate=pl.CostEstimate(
            flops=0, bytes_accessed=32 * rows * cols * 20, transcendentals=0
        ),
    )(*flat, small)


ERFC_SLOPE = 0.44
ERFC_COEFS = (
    0.12411048270139104,
    0.12443557227306976,
    0.1086564621750582,
    0.10790840846971936,
    -0.01009671066483208,
    0.1483525285505606,
    -0.13897999621011298,
    0.03561334337852199,
)


def gelu_and_slope(u):
    a = jnp.abs(u) * 0.7071067811865476
    t = 1.0 / (1.0 + ERFC_SLOPE * a)
    q = jnp.full_like(t, ERFC_COEFS[-1])
    for c in ERFC_COEFS[-2::-1]:
        q = q * t + c
    e = jnp.exp(-(a * a))
    tail = e * (t * q)
    phi = jnp.where(u < 0, tail, 1.0 - tail)
    return u * phi, phi + u * (e * 0.3989422804014327)


def up_kernel(x_ref, w_ref, b_ref, act_ref, slope_ref):
    for i in range(4):
        rows = slice(256 * i, 256 * (i + 1))
        u = lax.dot_general(x_ref[rows, :], w_ref[0], NN, preferred_element_type=f32) + b_ref[...]
        g, d = gelu_and_slope(u)
        act_ref[rows, :] = g.astype(bf16)
        slope_ref[rows, :] = d.astype(bf16)


def hidden_units(x, w, bias, tile):
    rows, width = x.shape
    units = w.shape[2] // 2
    per = units // tile
    col = pl.BlockSpec((rows, tile), lambda j: (0, j))
    return pl.pallas_call(
        up_kernel,
        grid=(2 * per,),
        in_specs=[
            pl.BlockSpec((rows, width), lambda j: (0, 0)),
            pl.BlockSpec((1, width, tile), lambda j: (j // per, 0, j % per)),
            pl.BlockSpec((1, tile), lambda j: (0, j)),
        ],
        out_specs=[col, col],
        out_shape=[jax.ShapeDtypeStruct((rows, 2 * units), bf16)] * 2,
        compiler_params=pltpu.CompilerParams(vmem_limit_bytes=56 * 2**20),
    )(x, w, bias)


def units_back_kernel(e_ref, w_ref, slope_ref, du_ref, sum_ref):
    total = 0.0
    for i in range(4):
        rows = slice(256 * i, 256 * (i + 1))
        d = lax.dot_general(e_ref[rows, :], w_ref[0], NN, preferred_element_type=f32)
        du = (d * slope_ref[rows, :].astype(f32)).astype(bf16)
        du_ref[rows, :] = du
        total = total + jnp.sum(du.astype(f32), 0, keepdims=True)
    sum_ref[...] = total


def hidden_units_back(e, w, slope, tile):
    rows, width = e.shape
    units = w.shape[2] // 2
    per = units // tile
    col = pl.BlockSpec((rows, tile), lambda j: (0, j))
    return pl.pallas_call(
        units_back_kernel,
        grid=(2 * per,),
        in_specs=[
            pl.BlockSpec((rows, width), lambda j: (0, 0)),
            pl.BlockSpec((1, width, tile), lambda j: (j // per, 0, per + j % per)),
            col,
        ],
        out_specs=[col, pl.BlockSpec((1, tile), lambda j: (0, j))],
        out_shape=[
            jax.ShapeDtypeStruct((rows, 2 * units), bf16),
            jax.ShapeDtypeStruct((1, 2 * units), f32),
        ],
        compiler_params=pltpu.CompilerParams(vmem_limit_bytes=56 * 2**20),
    )(e, w, slope)


def weight_grads_kernel(a_ref,b_ref,da_ref,db_ref,out_ref,at,bt,*,tiles):
    j=pl.program_id(0)
    @pl.when(j==0)
    def _():
        at[...]=a_ref[...].T
        bt[...]=b_ref[...].T
    kind=(j//tiles)%2
    @pl.when(kind==0)
    def _():
        out_ref[0]=lax.dot_general(at[...],da_ref[...],NN,preferred_element_type=f32).astype(bf16)
    @pl.when(kind==1)
    def _():
        out_ref[0]=lax.dot_general(bt[...],db_ref[...],NN,preferred_element_type=f32).astype(bf16)

def weight_grads(a,b,da,db,tile=512):
    rows,width=a.shape; half=da.shape[1]//2; tiles=half//tile
    whole=pl.BlockSpec((rows,width),lambda j:(0,0))
    t=lambda j: j//(2*tiles)
    kind=lambda j:(j//tiles)%2
    i=lambda j: j%tiles
    return pl.pallas_call(
        functools.partial(weight_grads_kernel,tiles=tiles),
        grid=(4*tiles,),
        in_specs=[whole,whole,
          pl.BlockSpec((rows,tile),lambda j:(0,t(j)*tiles+jnp.where(kind(j)==0,i(j),tiles-1))),
          pl.BlockSpec((rows,tile),lambda j:(0,t(j)*tiles+jnp.where(kind(j)==1,i(j),0)))],
        out_specs=pl.BlockSpec((1,width,tile),lambda j:(t(j),0,kind(j)*tiles+i(j))),
        out_shape=jax.ShapeDtypeStruct((2,width,2*half),bf16),
        scratch_shapes=[pltpu.VMEM((width,rows),bf16)]*2,
        compiler_params=pltpu.CompilerParams(vmem_limit_bytes=56*2**20),
    )(a,b,da,db)


def nn(a, b):
    return lax.dot_general(a, b, NN, preferred_element_type=f32)


def nt(a, b):
    return lax.dot_general(a, b, NT, preferred_element_type=f32)


def tn(a, b):
    return lax.dot_general(a, b, (((0,), (0,)), ((), ())), preferred_element_type=f32)


def norm_rows(r, gain, shift):
    center = r - jnp.mean(r, -1, keepdims=True)
    inv = lax.rsqrt(jnp.mean(center * center, -1, keepdims=True) + NORM_EPS)
    n = center * inv
    return n * gain + shift, n, inv


def norm_rows_back(e, n, inv, gain):
    eg = e * gain
    grad = inv * (eg - jnp.mean(eg, -1, keepdims=True) - n * jnp.mean(eg * n, -1, keepdims=True))
    return grad, jnp.sum(e * n, 0), jnp.sum(e, 0), jnp.sum(grad, 0)


def trade(x):
    return lax.ppermute(x, "tp", [(0, 1), (1, 0)])


def in_order(place, own, other, axis=0):
    return jnp.where(
        place == 0,
        jnp.concatenate([own, other], axis),
        jnp.concatenate([other, own], axis),
    )


def own_sequence(piece, place):
    own = lax.dynamic_index_in_dim(piece, place, 0, keepdims=False)
    away = lax.dynamic_index_in_dim(piece, 1 - place, 0, keepdims=False)
    return in_order(place, own, trade(away))


def to_pieces(rows, place):
    half = rows.shape[0] // 2
    halves = rows.reshape(2, half, rows.shape[1])
    own = lax.dynamic_index_in_dim(halves, place, 0, keepdims=True)
    away = lax.dynamic_index_in_dim(halves, 1 - place, 0, keepdims=True)
    return in_order(place, own, trade(away))


def whole_sequences(
    layer_in,
    memory,
    out_grad,
    w_self_in,
    w_self_out,
    w_cross_in,
    w_cross_out,
    w_up,
    w_down,
    head_bias,
    up_bias,
    norm_gain,
    row_bias,
):
    place = lax.axis_index("tp")
    width = layer_in.shape[2]
    cols = w_self_in.shape[2]
    units = w_up.shape[1]
    shard = w_self_in.shape[0]
    gains = norm_gain.astype(f32)
    shifts = row_bias.astype(f32)

    def gather(*parts):
        mine = jnp.concatenate(parts, 1)
        both = lax.all_gather(mine, ("tp", "fsdp"), axis=0, tiled=True)
        return both.reshape(2, width, mine.shape[1])

    small = jnp.concatenate([head_bias.reshape(-1), up_bias])
    small = in_order(place, small[None], trade(small)[None])
    hb = small[:, : 4 * cols].reshape(2, 4, cols).astype(f32)
    ub = small[:, 4 * cols :].astype(f32)

    g_self = gather_weights(
        jnp.concatenate([w_self_in.reshape(shard, 3 * cols), w_self_out.T], 1), 1, 4
    )
    g_cross = gather(w_cross_in.reshape(shard, 3 * cols), w_cross_out.T)
    g_ffn = gather(w_up, w_down.T)
    c3 = 3 * cols

    x = own_sequence(layer_in, place)
    mem = own_sequence(memory, place)
    cot = own_sequence(out_grad, place)
    xf = x.astype(f32)
    halves = (0, 1)
    zero = jnp.zeros((cols,), f32)
    scale3 = jnp.concatenate([zero + ATT_SCALE, zero + 1.0, zero + 1.0])
    blk = cols // 128

    sy, sa, sl = [], [], []
    for t in halves:
        bias = jnp.concatenate([hb[t, 0], zero, hb[t, 1]])
        y = ((nn(x, g_self[t, :, :c3]) + bias) * scale3).astype(bf16)
        o, lse = att_fwd(y, y, y, True, 512, 0, blk, 2 * blk, cols)
        sy.append(y)
        sa.append(o)
        sl.append(lse)
    r1 = xf + (nt(sa[0], g_self[0, :, c3:]) + nt(sa[1], g_self[1, :, c3:])) + shifts[0]
    h1, n1, i1 = norm_rows(r1, gains[0], shifts[3])
    h1b = h1.astype(bf16)

    cq, ckv, ca, cl = [], [], [], []
    for t in halves:
        kv = (nn(mem, g_cross[t, :, cols:c3]) + jnp.concatenate([zero, hb[t, 3]])).astype(bf16)
        q = ((nn(h1b, g_cross[t, :, :cols]) + hb[t, 2]) * ATT_SCALE).astype(bf16)
        o, lse = att_fwd(q, kv, kv, False, 512, 0, 0, blk, cols)
        cq.append(q)
        ckv.append(kv)
        ca.append(o)
        cl.append(lse)
    r2 = h1 + (nt(ca[0], g_cross[0, :, c3:]) + nt(ca[1], g_cross[1, :, c3:])) + shifts[1]
    h2, n2, i2 = norm_rows(r2, gains[1], shifts[4])
    h2b = h2.astype(bf16)

    act, slope = hidden_units(h2b, g_ffn, ub.reshape(1, 2 * units), 512)
    r3 = (
        h2
        + (nt(act[:, :units], g_ffn[0, :, units:]) + nt(act[:, units:], g_ffn[1, :, units:]))
        + shifts[2]
    )
    h3, n3, i3 = norm_rows(r3, gains[2], shifts[5])
    mixed = to_pieces(h3.astype(bf16), place)

    dr3, gg3, gs3, gb3 = norm_rows_back(cot.astype(f32), n3, i3, gains[2])
    e3 = dr3.astype(bf16)
    du, gu = hidden_units_back(e3, g_ffn, slope, 512)
    grad_ffn = weight_grads(h2b, e3, du, act, 1024)
    grad_ffn, du = lax.optimization_barrier((grad_ffn, du))
    s_ffn = lax.psum_scatter(
        grad_ffn.reshape(2 * width, 2 * units), ("tp", "fsdp"), scatter_dimension=0, tiled=True
    ).astype(f32)
    dh2 = dr3 + (nt(du[:, :units], g_ffn[0, :, :units]) + nt(du[:, units:], g_ffn[1, :, :units]))
    dr2, gg2, gs2, gb2 = norm_rows_back(dh2, n2, i2, gains[1])
    e2 = dr2.astype(bf16)

    dcq, dck, dcv = [], [], []
    for t in halves:
        da = nn(e2, g_cross[t, :, c3:]).astype(bf16)
        a, b, c = att_bwd(cq[t], ckv[t], ckv[t], ca[t], da, cl[t], False, 256, 0, 0, blk)
        dcq.append(a)
        dck.append(b)
        dcv.append(c)
    low = lambda v: v.astype(bf16)
    grads = [
        tuple(low(tn(h1b, dcq[t])) for t in halves),
        tuple(low(tn(mem, dck[t])) for t in halves),
        tuple(low(tn(mem, dcv[t])) for t in halves),
        tuple(low(tn(e2, ca[t])) for t in halves),
    ]
    dmem = sum(
        nt(dck[t], g_cross[t, :, cols : 2 * cols]) + nt(dcv[t], g_cross[t, :, 2 * cols : c3])
        for t in halves
    )
    d_memory = to_pieces(dmem.astype(bf16), place)
    dh1 = dr2 + (nt(dcq[0], g_cross[0, :, :cols]) + nt(dcq[1], g_cross[1, :, :cols]))
    dr1, gg1, gs1, gb1 = norm_rows_back(dh1, n1, i1, gains[0])
    e1 = dr1.astype(bf16)

    dsq, dsk, dsv = [], [], []
    for t in halves:
        da = nn(e1, g_self[t, :, c3:]).astype(bf16)
        y = sy[t]
        a, b, c = att_bwd(y, y, y, sa[t], da, sl[t], True, 256, 0, blk, 2 * blk)
        dsq.append(a)
        dsk.append(b)
        dsv.append(c)
    grads += [
        tuple(low(tn(x, dsq[t])) for t in halves),
        tuple(low(tn(x, dsk[t])) for t in halves),
        tuple(low(tn(x, dsv[t])) for t in halves),
        tuple(low(tn(e1, sa[t])) for t in halves),
    ]
    dx = dr1 + sum(
        nt(dsq[t], g_self[t, :, :cols])
        + nt(dsk[t], g_self[t, :, cols : 2 * cols])
        + nt(dsv[t], g_self[t, :, 2 * cols : c3])
        for t in halves
    )
    d_layer_in = to_pieces(dx.astype(bf16), place)

    def col_sums(pair):
        return jnp.stack([jnp.sum(p.astype(f32), 0) for p in pair])

    gh = jnp.stack([col_sums(dsq), col_sums(dsv), col_sums(dcq), col_sums(dcv)], 1)
    flat = jnp.concatenate(
        [
            v.reshape(-1)
            for v in (gh, gu, gg1, gg2, gg3, gb1, gb2, gb3, gs1, gs2, gs3)
        ]
    )
    s_att, flat = scatter_grads(grads, flat.reshape(-1, 128), 2)
    flat = flat.reshape(-1)
    head_sum = lax.dynamic_index_in_dim(flat[: 8 * cols].reshape(2, 4, cols), place, 0, False)
    unit_sum = lax.dynamic_index_in_dim(
        flat[8 * cols : 8 * cols + 2 * units].reshape(2, units), place, 0, False
    )
    rest = flat[8 * cols + 2 * units :].reshape(9, width)

    cross_part, self_part = s_att[:, : 4 * cols], s_att[:, 4 * cols :]
    return (
        mixed,
        d_layer_in,
        d_memory,
        self_part[:, :c3].reshape(shard, 3, cols),
        self_part[:, c3:].T,
        cross_part[:, :c3].reshape(shard, 3, cols),
        cross_part[:, c3:].T,
        s_ffn[:, :units],
        s_ffn[:, units:].T,
        head_sum,
        unit_sum,
        rest[:3],
        rest[3:],
    )


def on_device(layer_in, *rest):
    paired = lax.axis_size("tp") == 2 and layer_in.shape[0] == 2
    if paired and lax.axis_size("fsdp") == 16:
        return whole_sequences(layer_in, *rest)
    return shared_sequences(layer_in, *rest)


def solution(mesh):
    return jax.shard_map(
        on_device,
        mesh=mesh,
        in_specs=(
            P("fsdp", "tp", None),
            P("fsdp", "tp", None),
            P("fsdp", "tp", None),
            P("fsdp", None, "tp"),
            P("tp", "fsdp"),
            P("fsdp", None, "tp"),
            P("tp", "fsdp"),
            P("fsdp", "tp"),
            P("tp", "fsdp"),
            P(None, "tp"),
            P("tp"),
            P(),
            P(),
        ),
        out_specs=(
            P("fsdp", "tp", None),
            P("fsdp", "tp", None),
            P("fsdp", "tp", None),
            P("fsdp", None, "tp"),
            P("tp", "fsdp"),
            P("fsdp", None, "tp"),
            P("tp", "fsdp"),
            P("fsdp", "tp"),
            P("tp", "fsdp"),
            P(None, "tp"),
            P("tp"),
            P(),
            P(),
        ),
        check_vma=False,
    )
```

```python
import functools

import jax
import jax.numpy as jnp
from jax import lax
from jax.experimental import pallas as pl
from jax.experimental.pallas import tpu as pltpu
from jax.sharding import PartitionSpec as P

HD = 64
NORM_EPS = 1e-05
ATT_SCALE = 0.125


def times_back(left, right):
    return lax.dot_general(
        left, right, (((1,), (1,)), ((), ())), preferred_element_type=jnp.float32
    )


def over_rows(left, right):
    return lax.dot_general(
        left, right, (((0,), (0,)), ((), ())), preferred_element_type=jnp.float32
    )


def whole_rows(piece):
    return lax.all_gather(piece, "tp", axis=1, tiled=True)


def whole_grads(piece):
    return lax.all_gather(piece, "tp", axis=1, tiled=True)


def branch_sum(term):
    return lax.psum_scatter(
        term.astype(jnp.bfloat16), "tp", scatter_dimension=1, tiled=True
    ).astype(jnp.float32)


def piece_sum(term):
    return lax.psum_scatter(
        term.astype(jnp.bfloat16), "tp", scatter_dimension=1, tiled=True
    ).astype(jnp.float32)


def norm_forward(resid, gain, shift):
    center = resid - jnp.mean(resid, -1, keepdims=True)
    spread = jnp.mean(center * center, -1, keepdims=True)
    inv_std = lax.rsqrt(spread + NORM_EPS)
    normed = center * inv_std
    return (normed * gain + shift, normed, inv_std)


def norm_backward(grad_out, normed, inv_std, gain):
    grad_normed = grad_out * gain
    grad_resid = inv_std * (
        grad_normed
        - jnp.mean(grad_normed, -1, keepdims=True)
        - normed * jnp.mean(grad_normed * normed, -1, keepdims=True)
    )
    return (grad_resid, jnp.sum(grad_out * normed, (0, 1)), jnp.sum(grad_out, (0, 1)))


def gelu_exact(pre_act):
    return jax.nn.gelu(pre_act, approximate=False)


def gelu_back(pre_act, grad_act):
    unused_out, pull_back = jax.vjp(gelu_exact, pre_act)
    return pull_back(grad_act)[0]


def masked_scores(query_blk, block_start, keys_seq, causal):
    scores = jnp.einsum("qhc,khc->hqk", query_blk, keys_seq, preferred_element_type=jnp.float32)
    if causal:
        row_pos = block_start + lax.broadcasted_iota(jnp.int32, scores.shape[1:], 0)
        col_pos = lax.broadcasted_iota(jnp.int32, scores.shape[1:], 1)
        scores = jnp.where(row_pos >= col_pos, scores, -1e30)
    return scores


def attend_forward(query, keys, values, causal):
    seq_count, length, heads_dev, depth = query.shape
    block_rows = min(512, length)
    block_count = length // block_rows
    block_starts = jnp.arange(block_count, dtype=jnp.int32) * block_rows

    def one_sequence(seq_item):
        query_seq, keys_seq, values_seq = seq_item

        def one_block(blk_item):
            query_blk, block_start = blk_item
            scores = masked_scores(query_blk, block_start, keys_seq, causal)
            row_max = jnp.max(scores, -1, keepdims=True)
            log_total = row_max + jnp.log(jnp.sum(jnp.exp(scores - row_max), -1, keepdims=True))
            probs = jnp.exp(scores - log_total).astype(jnp.bfloat16)
            block_out = jnp.einsum(
                "hqk,khc->qhc", probs, values_seq, preferred_element_type=jnp.float32
            )
            return (block_out.astype(jnp.bfloat16), log_total)

        block_outs, log_totals = lax.map(
            one_block, (query_seq.reshape(block_count, block_rows, heads_dev, depth), block_starts)
        )
        return (block_outs.reshape(length, heads_dev, depth), log_totals)

    return lax.map(one_sequence, (query, keys, values))


def attend_backward(query, keys, values, log_totals, grad_out, causal):
    seq_count, length, heads_dev, depth = query.shape
    block_rows = min(512, length)
    block_count = length // block_rows
    block_starts = jnp.arange(block_count, dtype=jnp.int32) * block_rows

    def one_sequence(seq_item):
        query_seq, keys_seq, values_seq, total_seq, grad_seq = seq_item

        def one_block(carry, blk_item):
            query_blk, grad_blk, total_blk, block_start = blk_item
            probs = jnp.exp(masked_scores(query_blk, block_start, keys_seq, causal) - total_blk)
            grad_probs = jnp.einsum(
                "qhc,khc->hqk", grad_blk, values_seq, preferred_element_type=jnp.float32
            )
            row_delta = jnp.sum(probs * grad_probs, -1, keepdims=True)
            grad_scores = (probs * (grad_probs - row_delta)).astype(jnp.bfloat16)
            grad_query = jnp.einsum(
                "hqk,khc->qhc", grad_scores, keys_seq, preferred_element_type=jnp.float32
            )
            grad_keys = carry[0] + jnp.einsum(
                "hqk,qhc->khc", grad_scores, query_blk, preferred_element_type=jnp.float32
            )
            grad_values = carry[1] + jnp.einsum(
                "hqk,qhc->khc",
                probs.astype(jnp.bfloat16),
                grad_blk,
                preferred_element_type=jnp.float32,
            )
            return ((grad_keys, grad_values), grad_query)

        zero_keys = jnp.zeros(keys_seq.shape, jnp.float32)
        blk_items = (
            query_seq.reshape(block_count, block_rows, heads_dev, depth),
            grad_seq.reshape(block_count, block_rows, heads_dev, depth),
            total_seq,
            block_starts,
        )
        (grad_keys, grad_values), grad_query = lax.scan(
            one_block, (zero_keys, zero_keys), blk_items
        )
        return (grad_query.reshape(length, heads_dev, depth), grad_keys, grad_values)

    return lax.map(one_sequence, (query, keys, values, log_totals, grad_out))


def shared_sequences(
    layer_in,
    memory,
    out_grad,
    w_self_in,
    w_self_out,
    w_cross_in,
    w_cross_out,
    w_up,
    w_down,
    head_bias,
    up_bias,
    norm_gain,
    row_bias,
):
    seq_count, piece_len, model_width = layer_in.shape
    head_cols = w_self_in.shape[2]
    unit_cols = w_up.shape[1]
    heads_dev = head_cols // HD
    tp_place = lax.axis_index("tp")
    tp_count = lax.axis_size("tp")
    zero_index = jnp.zeros((), jnp.int32)
    gains = norm_gain.astype(jnp.float32)
    shifts = row_bias.astype(jnp.float32)
    col_bias = head_bias.astype(jnp.float32)
    unit_bias = up_bias.astype(jnp.float32)
    self_in, self_out, cross_in, cross_out, up_full, down_full = (
        lax.all_gather(w_self_in, "fsdp", axis=0, tiled=True),
        lax.all_gather(w_self_out, "fsdp", axis=1, tiled=True),
        lax.all_gather(w_cross_in, "fsdp", axis=0, tiled=True),
        lax.all_gather(w_cross_out, "fsdp", axis=1, tiled=True),
        lax.all_gather(w_up, "fsdp", axis=0, tiled=True),
        lax.all_gather(w_down, "fsdp", axis=1, tiled=True),
    )
    layer_whole = whole_rows(layer_in)
    length = layer_whole.shape[1]
    row_count = seq_count * length
    token_rows = layer_whole.reshape(row_count, model_width)
    self_proj = jnp.einsum("rd,dkc->rkc", token_rows, self_in, preferred_element_type=jnp.float32)
    self_query = ((self_proj[:, 0] + col_bias[0]) * ATT_SCALE).astype(jnp.bfloat16)
    self_keys = self_proj[:, 1].astype(jnp.bfloat16)
    self_values = (self_proj[:, 2] + col_bias[1]).astype(jnp.bfloat16)
    head_shape = (seq_count, length, heads_dev, HD)
    self_att, self_totals = attend_forward(
        self_query.reshape(head_shape),
        self_keys.reshape(head_shape),
        self_values.reshape(head_shape),
        True,
    )
    self_rows = self_att.reshape(row_count, head_cols)
    self_term = jnp.dot(self_rows, self_out, preferred_element_type=jnp.float32).reshape(
        seq_count, length, model_width
    )
    resid_one = layer_in.astype(jnp.float32) + branch_sum(self_term) + shifts[0]
    normed_one, unit_one, inv_one = norm_forward(resid_one, gains[0], shifts[3])
    normed_rows = whole_rows(normed_one.astype(jnp.bfloat16)).reshape(row_count, model_width)
    cross_query = (
        (jnp.dot(normed_rows, cross_in[:, 0], preferred_element_type=jnp.float32) + col_bias[2])
        * ATT_SCALE
    ).astype(jnp.bfloat16)
    memory_whole = lax.all_gather(memory, "tp", axis=1, tiled=True)
    source_len = memory_whole.shape[1]
    source_rows = memory_whole.reshape(seq_count * source_len, model_width)
    cross_proj = jnp.einsum(
        "rd,dkc->rkc", source_rows, cross_in[:, 1:], preferred_element_type=jnp.float32
    )
    cross_keys = cross_proj[:, 0].astype(jnp.bfloat16)
    cross_values = (cross_proj[:, 1] + col_bias[3]).astype(jnp.bfloat16)
    source_shape = (seq_count, source_len, heads_dev, HD)
    cross_att, cross_totals = attend_forward(
        cross_query.reshape(head_shape),
        cross_keys.reshape(source_shape),
        cross_values.reshape(source_shape),
        False,
    )
    cross_rows = cross_att.reshape(row_count, head_cols)
    cross_term = jnp.dot(cross_rows, cross_out, preferred_element_type=jnp.float32).reshape(
        seq_count, length, model_width
    )
    resid_two = normed_one + branch_sum(cross_term) + shifts[1]
    normed_two, unit_two, inv_two = norm_forward(resid_two, gains[1], shifts[4])
    normed_two_low = normed_two.astype(jnp.bfloat16)
    ffn_rows = whole_rows(normed_two_low).reshape(row_count, model_width)
    pre_act = jnp.dot(ffn_rows, up_full, preferred_element_type=jnp.float32) + unit_bias
    hidden_act = gelu_exact(pre_act).astype(jnp.bfloat16)
    ffn_term = jnp.dot(hidden_act, down_full, preferred_element_type=jnp.float32).reshape(
        seq_count, length, model_width
    )
    ffn_out = branch_sum(ffn_term)
    resid_three = normed_two + ffn_out + shifts[2]
    mixed, unit_three, inv_three = norm_forward(resid_three, gains[2], shifts[5])
    grad_three, gain_grad_three, shift_grad_three = norm_backward(
        out_grad.astype(jnp.float32), unit_three, inv_three, gains[2]
    )
    bias_grad_three = jnp.sum(grad_three, (0, 1))
    grad_three_low = grad_three.astype(jnp.bfloat16)
    grad_rows = whole_grads(grad_three_low).reshape(row_count, model_width)
    grad_act = times_back(grad_rows, down_full)
    grad_pre = gelu_back(pre_act, grad_act).astype(jnp.bfloat16)
    d_up = over_rows(ffn_rows, grad_pre)
    d_down = over_rows(hidden_act, grad_rows)
    unit_grad = jnp.sum(grad_pre, 0, dtype=jnp.float32)
    grad_two_in = piece_sum(times_back(grad_pre, up_full).reshape(seq_count, length, model_width))
    grad_normed_two = grad_three + grad_two_in
    grad_two, gain_grad_two, shift_grad_two = norm_backward(
        grad_normed_two, unit_two, inv_two, gains[1]
    )
    bias_grad_two = jnp.sum(grad_two, (0, 1))
    grad_two_rows = whole_grads(grad_two.astype(jnp.bfloat16)).reshape(row_count, model_width)
    d_cross_out = over_rows(cross_rows, grad_two_rows)
    grad_cross_att = times_back(grad_two_rows, cross_out).astype(jnp.bfloat16)
    cq_grad, ck_grad, cv_grad = attend_backward(
        cross_query.reshape(head_shape),
        cross_keys.reshape(source_shape),
        cross_values.reshape(source_shape),
        cross_totals,
        grad_cross_att.reshape(head_shape),
        False,
    )
    cq_pre = cq_grad.reshape(row_count, head_cols).astype(jnp.bfloat16) * jnp.asarray(
        ATT_SCALE, jnp.bfloat16
    )
    ckv_low = jnp.stack(
        [
            ck_grad.reshape(seq_count * source_len, head_cols),
            cv_grad.reshape(seq_count * source_len, head_cols),
        ],
        1,
    ).astype(jnp.bfloat16)
    cross_q_grad = over_rows(normed_rows, cq_pre)
    cq_bias_grad = jnp.sum(cq_pre, 0, dtype=jnp.float32)
    normed_part = times_back(cq_pre, cross_in[:, 0]).reshape(seq_count, length, model_width)
    source_part = jnp.einsum(
        "rkc,dkc->rd", ckv_low, cross_in[:, 1:], preferred_element_type=jnp.float32
    ).reshape(seq_count, source_len, model_width)
    grad_one_in, memory_grad = (
        lax.psum_scatter(
            normed_part.astype(jnp.bfloat16), "tp", scatter_dimension=1, tiled=True
        ).astype(jnp.float32),
        lax.psum_scatter(
            source_part.astype(jnp.bfloat16), "tp", scatter_dimension=1, tiled=True
        ).astype(jnp.float32),
    )
    d_memory = memory_grad.astype(jnp.bfloat16)
    cross_kv_grad = jnp.einsum(
        "rd,rkc->dkc", source_rows, ckv_low, preferred_element_type=jnp.float32
    )
    cross_grad_term = jnp.concatenate([cross_q_grad[:, None, :], cross_kv_grad], 1)
    cv_own = jnp.sum(ckv_low[:, 1], 0, dtype=jnp.float32)
    cv_wide = lax.dynamic_update_slice(
        jnp.zeros((head_cols * tp_count,), jnp.float32), cv_own, (tp_place * head_cols,)
    )
    grad_normed_one = grad_two + grad_one_in
    grad_one, gain_grad_one, shift_grad_one = norm_backward(
        grad_normed_one, unit_one, inv_one, gains[0]
    )
    bias_grad_one = jnp.sum(grad_one, (0, 1))
    grad_one_rows = whole_grads(grad_one.astype(jnp.bfloat16)).reshape(row_count, model_width)
    d_self_out = over_rows(self_rows, grad_one_rows)
    grad_self_att = times_back(grad_one_rows, self_out).astype(jnp.bfloat16)
    sq_grad, sk_grad, sv_grad = attend_backward(
        self_query.reshape(head_shape),
        self_keys.reshape(head_shape),
        self_values.reshape(head_shape),
        self_totals,
        grad_self_att.reshape(head_shape),
        True,
    )
    sq_pre = sq_grad.reshape(row_count, head_cols).astype(jnp.bfloat16) * jnp.asarray(
        ATT_SCALE, jnp.bfloat16
    )
    sqkv_low = jnp.stack(
        [
            sq_pre,
            sk_grad.reshape(row_count, head_cols).astype(jnp.bfloat16),
            sv_grad.reshape(row_count, head_cols).astype(jnp.bfloat16),
        ],
        1,
    )
    d_self_in = jnp.einsum("rd,rkc->dkc", token_rows, sqkv_low, preferred_element_type=jnp.float32)
    sq_bias_grad = jnp.sum(sq_pre, 0, dtype=jnp.float32)
    sv_bias_grad = jnp.sum(sqkv_low[:, 2], 0, dtype=jnp.float32)
    layer_part = jnp.einsum(
        "rkc,dkc->rd", sqkv_low, self_in, preferred_element_type=jnp.float32
    ).reshape(seq_count, length, model_width)
    d_layer_in = (grad_one + piece_sum(layer_part)).astype(jnp.bfloat16)
    slot_grad = jnp.stack([sq_bias_grad, sv_bias_grad, cq_bias_grad])
    slot_wide = lax.dynamic_update_slice(
        jnp.zeros((3, head_cols * tp_count), jnp.float32),
        slot_grad,
        (zero_index, tp_place * head_cols),
    )
    head_wide = jnp.concatenate([slot_wide, cv_wide[None, :]], 0)
    unit_wide_grad = lax.dynamic_update_slice(
        jnp.zeros((unit_cols * tp_count,), jnp.float32), unit_grad, (tp_place * unit_cols,)
    )
    gain_grads = jnp.stack([gain_grad_one, gain_grad_two, gain_grad_three])
    shift_grads = jnp.stack(
        [
            bias_grad_one,
            bias_grad_two,
            bias_grad_three,
            shift_grad_one,
            shift_grad_two,
            shift_grad_three,
        ]
    )
    gain_total, shift_total, head_total, unit_total = lax.psum(
        (gain_grads, shift_grads, head_wide, unit_wide_grad), ("fsdp", "tp")
    )
    d_head_bias = lax.dynamic_slice(head_total, (zero_index, tp_place * head_cols), (4, head_cols))
    d_up_bias = lax.dynamic_slice(unit_total, (tp_place * unit_cols,), (unit_cols,))
    g_self_in, g_self_out, g_cross_part, g_cross_out, g_up, g_down = (
        lax.psum_scatter(
            d_self_in.astype(jnp.bfloat16), "fsdp", scatter_dimension=0, tiled=True
        ).astype(jnp.float32),
        lax.psum_scatter(
            d_self_out.astype(jnp.bfloat16), "fsdp", scatter_dimension=1, tiled=True
        ).astype(jnp.float32),
        lax.psum_scatter(
            cross_grad_term.astype(jnp.bfloat16), "fsdp", scatter_dimension=0, tiled=True
        ).astype(jnp.float32),
        lax.psum_scatter(
            d_cross_out.astype(jnp.bfloat16), "fsdp", scatter_dimension=1, tiled=True
        ).astype(jnp.float32),
        lax.psum_scatter(d_up.astype(jnp.bfloat16), "fsdp", scatter_dimension=0, tiled=True).astype(
            jnp.float32
        ),
        lax.psum_scatter(
            d_down.astype(jnp.bfloat16), "fsdp", scatter_dimension=1, tiled=True
        ).astype(jnp.float32),
    )
    return (
        mixed.astype(jnp.bfloat16),
        d_layer_in,
        d_memory,
        g_self_in,
        g_self_out,
        g_cross_part,
        g_cross_out,
        g_up,
        g_down,
        d_head_bias,
        d_up_bias,
        gain_total,
        shift_total,
    )


NT=(((1,),(1,)),((),()))
NN=(((1,),(0,)),((),()))
f32=jnp.float32
bf16=jnp.bfloat16

def scores_t(k_h,q,i,bq,causal):
    s=lax.dot_general(k_h,q,NT,preferred_element_type=f32)
    return s

def att_fwd_kernel(q_ref,k_ref,v_ref,o_ref,lse_ref,*,bq,causal):
    n=q_ref.shape[0]; nk=k_ref.shape[0]
    lane=lax.broadcasted_iota(jnp.int32,(nk,128),1)
    k=k_ref[...]; v=v_ref[...]
    zero=jnp.zeros((),bf16)
    kh=[jnp.where(lane<HD,k,zero),jnp.where(lane>=HD,k,zero)]
    vt=v.astype(f32).T.astype(bf16)
    ones=jnp.ones((8,nk),bf16)
    vh=[jnp.concatenate([vt[h*HD:(h+1)*HD],ones],0) for h in range(2)]
    for i in range(n//bq):
        q=q_ref[i*bq:(i+1)*bq,:]
        L=(i+1)*bq if causal else nk
        outs=[];lses=[]
        for h in range(2):
            s=lax.dot_general(kh[h][:L],q,NT,preferred_element_type=f32)
            if causal:
                keep=lax.broadcasted_iota(jnp.int32,(bq,bq),0)<=lax.broadcasted_iota(jnp.int32,(bq,bq),1)
                sd=jnp.where(keep,s[L-bq:],-1e30)
                s=jnp.concatenate([s[:L-bq],sd],0) if L>bq else sd
            m=jnp.max(s,0,keepdims=True)
            p=jnp.exp(s-m).astype(bf16)
            ol=lax.dot_general(vh[h][:,:L],p,NN,preferred_element_type=f32)
            l=ol[HD:HD+1]
            outs.append(ol[:HD]*(1.0/l))
            lses.append(m+jnp.log(l))
        ot=jnp.concatenate(outs,0)
        o_ref[i*bq:(i+1)*bq,:]=ot.T.astype(bf16)
        lse_ref[0,:,i*bq:(i+1)*bq]=jnp.concatenate(lses,0)

def att_fwd(q,k,v,causal,bq=256,qo=0,ko=0,vo=0,width=None):
    n=q.shape[0]; nk=k.shape[0]; width=width or q.shape[1]; np_=width//128
    spec=lambda rows,off: pl.BlockSpec((rows,128),lambda p: (0,p+off))
    return pl.pallas_call(
        functools.partial(att_fwd_kernel,bq=bq,causal=causal),
        grid=(np_,),
        in_specs=[spec(n,qo),spec(nk,ko),spec(nk,vo)],
        out_specs=[spec(n,0),pl.BlockSpec((1,2,n),lambda p:(p,0,0))],
        out_shape=[jax.ShapeDtypeStruct((n,width),bf16),jax.ShapeDtypeStruct((np_,2,n),f32)],
        compiler_params=pltpu.CompilerParams(dimension_semantics=("arbitrary",),vmem_limit_bytes=56*2**20),
    )(q,k,v)

def att_bwd_kernel(q_ref,k_ref,v_ref,o_ref,do_ref,lse_ref,dq_ref,dk_ref,dv_ref,dk_acc,dv_acc,*,bq,causal):
    n=q_ref.shape[0]; nk=k_ref.shape[0]
    lane=lax.broadcasted_iota(jnp.int32,(nk,128),1)
    lq=lax.broadcasted_iota(jnp.int32,(bq,128),1)
    k=k_ref[...]; v=v_ref[...]
    zero=jnp.zeros((),bf16)
    kh=[jnp.where(lane<HD,k,zero),jnp.where(lane>=HD,k,zero)]
    vh=[jnp.where(lane<HD,v,zero),jnp.where(lane>=HD,v,zero)]
    kt=k.astype(f32).T.astype(bf16)
    dk_acc[...]=jnp.zeros_like(dk_acc); dv_acc[...]=jnp.zeros_like(dv_acc)
    for i in range(n//bq):
        rows=slice(i*bq,(i+1)*bq)
        q=q_ref[rows,:]; do=do_ref[rows,:]
        L=(i+1)*bq if causal else nk
        dot_=(do.astype(f32)*o_ref[rows,:].astype(f32)).T
        qm=[jnp.where(lq<HD,q,zero),jnp.where(lq>=HD,q,zero)]
        dm=[jnp.where(lq<HD,do,zero),jnp.where(lq>=HD,do,zero)]
        dqs=[]
        for h in range(2):
            s=lax.dot_general(kh[h][:L],q,NT,preferred_element_type=f32)
            dp=lax.dot_general(vh[h][:L],do,NT,preferred_element_type=f32)
            lse=lse_ref[0,h:h+1,rows]
            delta=jnp.sum(dot_[h*HD:(h+1)*HD],0,keepdims=True)
            if causal:
                keep=lax.broadcasted_iota(jnp.int32,(bq,bq),0)<=lax.broadcasted_iota(jnp.int32,(bq,bq),1)
                sd=jnp.where(keep,s[L-bq:],-1e30)
                s=jnp.concatenate([s[:L-bq],sd],0) if L>bq else sd
            p=jnp.exp(s-lse)
            ds=(p*(dp-delta)).astype(bf16)
            pb=p.astype(bf16)
            dv_acc[:L,:]+=lax.dot_general(pb,dm[h],NN,preferred_element_type=f32)
            dk_acc[:L,:]+=lax.dot_general(ds,qm[h],NN,preferred_element_type=f32)
            dqs.append(lax.dot_general(kt[h*HD:(h+1)*HD,:L],ds,NN,preferred_element_type=f32))
        dq_ref[rows,:]=(jnp.concatenate(dqs,0)*0.125).T.astype(bf16)
    dk_ref[...]=dk_acc[...].astype(bf16)
    dv_ref[...]=dv_acc[...].astype(bf16)

def att_bwd(q,k,v,o,do,lse,causal,bq=256,qo=0,ko=0,vo=0):
    n=q.shape[0]; nk=k.shape[0]; width=o.shape[1]; np_=width//128
    spec=lambda rows,off: pl.BlockSpec((rows,128),lambda p: (0,p+off))
    return pl.pallas_call(
        functools.partial(att_bwd_kernel,bq=bq,causal=causal),
        grid=(np_,),
        in_specs=[spec(n,qo),spec(nk,ko),spec(nk,vo),spec(n,0),spec(n,0),pl.BlockSpec((1,2,n),lambda p:(p,0,0))],
        out_specs=[spec(n,0),spec(nk,0),spec(nk,0)],
        out_shape=[jax.ShapeDtypeStruct((n,width),bf16),jax.ShapeDtypeStruct((nk,width),bf16),jax.ShapeDtypeStruct((nk,width),bf16)],
        scratch_shapes=[pltpu.VMEM((nk,128),f32)]*2,
        compiler_params=pltpu.CompilerParams(dimension_semantics=("arbitrary",),vmem_limit_bytes=56*2**20),
    )(q,k,v,o,do,lse)


MESH = pl.DeviceIdType.MESH
LINKS = ("z1", "z2", "y", "x", "c")


def partners():
    t = lax.axis_index("tp")
    f = lax.axis_index("fsdp")
    z, y, c = f // 4, (f // 2) % 2, f % 2

    def at(z_, y_, c_, t_):
        return (z_ * 4 + y_ * 2 + c_, t_)

    ids = dict(
        z1=at(z + 1 - 2 * (z % 2), y, c, t),
        z2=at((z + 2) % 4, y, c, t),
        y=at(z, 1 - y, c, t),
        x=at(z, y, c, 1 - t),
        c=at(z, y, 1 - c, t),
    )
    return (t, z, y, c), ids


def greet(ids):
    barrier = pltpu.get_barrier_semaphore()
    for name in LINKS:
        pl.semaphore_signal(barrier, inc=1, device_id=ids[name], device_id_type=MESH)
    pl.semaphore_wait(barrier, len(LINKS))


def pipeline(chunks, stages, begin):
    started = {}
    for step in range(chunks + stages):
        for s in range(stages + 1):
            k = step - s
            if 0 <= k < chunks:
                if s > 0:
                    for copy in started[k, s - 1]:
                        copy.wait_recv()
                started[k, s] = begin(k, s)
    for copies in started.values():
        for copy in copies:
            copy.wait_send()


def start_copy(src, dst, send, recv, to):
    copy = pltpu.make_async_remote_copy(
        src_ref=src,
        dst_ref=dst,
        send_sem=send,
        recv_sem=recv,
        device_id=to,
        device_id_type=MESH,
    )
    copy.start()
    return copy


def gather_kernel(shard_ref, *refs, cw, chunks, swaps):
    ins, outs = refs[:swaps], refs[swaps + 1 : 2 * swaps + 1]
    w_ref = refs[swaps]
    send, recv, own, swap_send, swap_recv, swap_own = refs[2 * swaps + 1 :]
    (t, z, y, c), ids = partners()
    mine = pltpu.make_async_copy(shard_ref, w_ref.at[t, z, y, c], own)
    mine.start()
    kept = [
        pltpu.make_async_copy(ins[i].at[t], outs[i].at[t], swap_own.at[i]) for i in range(swaps)
    ]
    for copy in kept:
        copy.start()
    greet(ids)
    pair = (z // 2) * 2
    traded = []

    def begin(k, s):
        cols = pl.ds(k * cw, cw)
        if s == 0:
            r, to = w_ref.at[t, z, y, c, :, cols], "z1"
            copies = [start_copy(shard_ref.at[:, cols], r, send.at[k, 0], recv.at[k, 0], ids[to])]
            for i in range(swaps):
                part = ins[i].shape[1] // chunks
                rows = pl.ds(k * part, part)
                traded.append(
                    start_copy(
                        ins[i].at[1 - t, rows],
                        outs[i].at[t, rows],
                        swap_send.at[i, k],
                        swap_recv.at[i, k],
                        ids["x"],
                    )
                )
            return copies
        if s == 5:
            return []
        if s == 1:
            if k == 0:
                mine.wait()
            r, to = w_ref.at[t, pl.ds(pair, 2), y, c, :, cols], "z2"
        elif s == 2:
            r, to = w_ref.at[t, :, y, c, :, cols], "x"
        elif s == 3:
            r, to = w_ref.at[:, :, y, c, :, cols], "y"
        else:
            r, to = w_ref.at[:, :, :, c, :, cols], "c"
        return [start_copy(r, r, send.at[k, s], recv.at[k, s], ids[to])]

    pipeline(chunks, 5, begin)
    for copy in traded:
        copy.wait()
    for copy in kept:
        copy.wait()


def gather_weights(shard, pieces, cid, chunks):
    rows, cols = shard.shape
    swaps = len(pieces)
    anywhere = pl.BlockSpec(memory_space=pl.ANY)
    dma = pltpu.SemaphoreType.DMA
    outs = pl.pallas_call(
        functools.partial(gather_kernel, cw=cols // chunks, chunks=chunks, swaps=swaps),
        in_specs=[pl.BlockSpec(memory_space=pltpu.VMEM)] + [anywhere] * swaps,
        out_specs=[anywhere] * (1 + swaps),
        out_shape=[jax.ShapeDtypeStruct((2, 4, 2, 2, rows, cols), shard.dtype)]
        + [jax.ShapeDtypeStruct(p.shape, p.dtype) for p in pieces],
        scratch_shapes=[
            dma((chunks, 5)),
            dma((chunks, 5)),
            dma,
            dma((swaps, chunks)),
            dma((swaps, chunks)),
            dma((swaps,)),
        ],
        compiler_params=pltpu.CompilerParams(collective_id=cid, has_side_effects=True),
        cost_estimate=pl.CostEstimate(
            flops=0, bytes_accessed=32 * rows * cols * 20, transcendentals=0
        ),
    )(shard, *pieces)
    whole = outs[0].reshape(2, 16 * rows, cols)
    return whole, [p.reshape(p.shape[0] * p.shape[1], p.shape[2]) for p in outs[1:]]


def scatter_kernel(*refs, chunks, ahead):
    g_refs, refs = refs[: 2 * chunks], refs[2 * chunks + ahead :]
    rows_ref, small_ref, out_ref, small_out, pieces_ref, own, r1 = refs[:7]
    s2, r2, k2, s3, r3, k3, s4, r4, k4, s5, r5 = refs[7:18]
    sm, rm, send, recv, own_sem, small_send, small_recv, swap_send, swap_recv, swap_own = refs[18:]
    (t, z, y, c), ids = partners()
    pair = (z // 2) * 2
    away = 2 - pair
    other = 1 - z % 2
    rows = own.shape[3]
    cw = own.shape[4] // chunks
    h = cw // 2

    def loc(k, half):
        return pltpu.make_async_copy(
            g_refs[2 * k + half].at[:, :, c],
            own.at[half, :, :, :, pl.ds(k * cw, cw)],
            own_sem.at[k, half],
        )

    for k in range(chunks):
        loc(k, 0).start()
        loc(k, 1).start()
    kept = pltpu.make_async_copy(rows_ref.at[t], pieces_ref.at[t], swap_own)
    kept.start()
    greet(ids)
    traded = []

    def go(k, j, src, dst, to):
        return start_copy(src, dst, send.at[k, j], recv.at[k, j], ids[to])

    def small_go(j):
        to = ids[("c", "x", "y", "z2", "z1")[j]]
        return start_copy(sm.at[j], rm.at[j], small_send.at[j], small_recv.at[j], to)

    def up(v):
        return v.astype(f32)

    def begin(k, s):
        ca = slice(k * cw, k * cw + h)
        cb = slice(k * cw + h, (k + 1) * cw)
        if s == 0:
            cols = pl.ds(k * cw, cw)
            return [
                go(k, 7 * half, g_refs[2 * k + half].at[:, :, 1 - c], r1.at[half, :, :, :, cols], "c")
                for half in (0, 1)
            ]
        if s == 1:
            loc(k, 0).wait()
            loc(k, 1).wait()
            shape = (8, rows, h)
            sent = up(own[1 - t, :, :, :, ca]) + up(r1[1 - t, :, :, :, ca])
            s2[k, 0] = sent.astype(bf16).reshape(shape)
            da = go(k, 1, s2.at[k, 0], r2.at[k, 0], "x")
            sent = up(own[:, :, 1 - y, :, cb]) + up(r1[:, :, 1 - y, :, cb])
            s2[k, 1] = sent.astype(bf16).reshape(shape)
            db = go(k, 2, s2.at[k, 1], r2.at[k, 1], "y")
            k2[k, 0] = (up(own[t, :, :, :, ca]) + up(r1[t, :, :, :, ca])).reshape(shape)
            k2[k, 1] = (up(own[:, :, y, :, cb]) + up(r1[:, :, y, :, cb])).reshape(shape)
            return [da, db]
        if s == 2:
            for i in range(4):
                j = 2 * i + 1 - y
                s3[k, 0, i] = (k2[k, 0, j] + up(r2[k, 0, j])).astype(bf16)
            da = go(k, 3, s3.at[k, 0], r3.at[k, 0], "y")
            for i in range(4):
                j = 4 * (1 - t) + i
                s3[k, 1, i] = (k2[k, 1, j] + up(r2[k, 1, j])).astype(bf16)
            db = go(k, 4, s3.at[k, 1], r3.at[k, 1], "x")
            for i in range(4):
                k3[k, 0, i] = k2[k, 0, 2 * i + y] + up(r2[k, 0, 2 * i + y])
                k3[k, 1, i] = k2[k, 1, 4 * t + i] + up(r2[k, 1, 4 * t + i])
            return [da, db]
        if s == 3:
            for j in range(2):
                for i in range(2):
                    s4[k, j, i] = (k3[k, j, away + i] + up(r3[k, j, away + i])).astype(bf16)
            d = go(k, 5, s4.at[k], r4.at[k], "z2")
            for j in range(2):
                for i in range(2):
                    k4[k, j, i] = k3[k, j, pair + i] + up(r3[k, j, pair + i])
            return [d]
        if s == 4:
            for j in range(2):
                s5[k, j] = (k4[k, j, other] + up(r4[k, j, other])).astype(bf16)
            return [go(k, 6, s5.at[k], r5.at[k], "z1")]
        for j in range(2):
            mine = k4[k, j, z % 2] + up(r4[k, j, z % 2]) + up(r5[k, j])
            out_ref[:, k * cw + j * h : k * cw + (j + 1) * h] = mine
        return []

    smalls = []

    def begin_with_small(k, s):
        if s == 0:
            part = rows_ref.shape[1] // chunks
            some = pl.ds(k * part, part)
            src, dst = rows_ref.at[1 - t, some], pieces_ref.at[t, some]
            traded.append(start_copy(src, dst, swap_send.at[k], swap_recv.at[k], ids["x"]))
        if k == 0:
            if s == 0:
                sm[0] = small_ref[...]
            else:
                smalls[s - 1].wait_recv()
                total = sm[s - 1] + rm[s - 1]
                if s < 5:
                    sm[s] = total
                else:
                    small_out[...] = total
            if s < 5:
                smalls.append(small_go(s))
        return begin(k, s)

    pipeline(chunks, 5, begin_with_small)
    for copy in smalls:
        copy.wait_send()
    for copy in traded:
        copy.wait()
    kept.wait()


def scatter_grads(pairs, ahead, seq_rows, small, cid):
    chunks = len(pairs)
    width, cw = pairs[0][0].shape
    rows, h, cols = width // 16, cw // 2, cw * chunks
    V = pltpu.VMEM
    dma = pltpu.SemaphoreType.DMA
    flat = [g.reshape(4, 2, 2, rows, cw) for pair in pairs for g in pair]
    seq_rows = seq_rows.reshape(2, seq_rows.shape[0] // 2, seq_rows.shape[1])
    whole = pl.BlockSpec(memory_space=pltpu.VMEM)
    anywhere = pl.BlockSpec(memory_space=pl.ANY)
    return pl.pallas_call(
        functools.partial(scatter_kernel, chunks=chunks, ahead=len(ahead)),
        in_specs=[anywhere] * (len(flat) + len(ahead) + 1) + [whole],
        out_specs=[whole, whole, anywhere],
        out_shape=[
            jax.ShapeDtypeStruct((rows, cols), f32),
            jax.ShapeDtypeStruct(small.shape, f32),
            jax.ShapeDtypeStruct(seq_rows.shape, seq_rows.dtype),
        ],
        scratch_shapes=[
            V((2, 4, 2, rows, cols), bf16),
            V((2, 4, 2, rows, cols), bf16),
            V((chunks, 2, 8, rows, h), bf16),
            V((chunks, 2, 8, rows, h), bf16),
            V((chunks, 2, 8, rows, h), f32),
            V((chunks, 2, 4, rows, h), bf16),
            V((chunks, 2, 4, rows, h), bf16),
            V((chunks, 2, 4, rows, h), f32),
            V((chunks, 2, 2, rows, h), bf16),
            V((chunks, 2, 2, rows, h), bf16),
            V((chunks, 2, 2, rows, h), f32),
            V((chunks, 2, rows, h), bf16),
            V((chunks, 2, rows, h), bf16),
            V((5,) + small.shape, f32),
            V((5,) + small.shape, f32),
            dma((chunks, 8)),
            dma((chunks, 8)),
            dma((chunks, 2)),
            dma((5,)),
            dma((5,)),
            dma((chunks,)),
            dma((chunks,)),
            dma,
        ],
        compiler_params=pltpu.CompilerParams(
            collective_id=cid, has_side_effects=True, vmem_limit_bytes=60 * 2**20
        ),
        cost_estimate=pl.CostEstimate(
            flops=0, bytes_accessed=32 * rows * cols * 20, transcendentals=0
        ),
    )(*flat, *ahead, seq_rows, small)


ERFC_SLOPE = 0.44
ERFC_COEFS = (
    0.12411048270139104,
    0.12443557227306976,
    0.1086564621750582,
    0.10790840846971936,
    -0.01009671066483208,
    0.1483525285505606,
    -0.13897999621011298,
    0.03561334337852199,
)


def gelu_and_slope(u):
    a = jnp.abs(u) * 0.7071067811865476
    t = 1.0 / (1.0 + ERFC_SLOPE * a)
    q = jnp.full_like(t, ERFC_COEFS[-1])
    for c in ERFC_COEFS[-2::-1]:
        q = q * t + c
    e = jnp.exp(-(a * a))
    tail = e * (t * q)
    phi = jnp.where(u < 0, tail, 1.0 - tail)
    return u * phi, phi + u * (e * 0.3989422804014327)


def up_kernel(x_ref, w_ref, b_ref, act_ref, slope_ref):
    for i in range(4):
        rows = slice(256 * i, 256 * (i + 1))
        u = lax.dot_general(x_ref[rows, :], w_ref[0], NN, preferred_element_type=f32) + b_ref[...]
        g, d = gelu_and_slope(u)
        act_ref[rows, :] = g.astype(bf16)
        slope_ref[rows, :] = d.astype(bf16)


def hidden_units(x, w, bias, tile):
    rows, width = x.shape
    units = w.shape[2] // 2
    per = units // tile
    col = pl.BlockSpec((rows, tile), lambda j: (0, j))
    return pl.pallas_call(
        up_kernel,
        grid=(2 * per,),
        in_specs=[
            pl.BlockSpec((rows, width), lambda j: (0, 0)),
            pl.BlockSpec((1, width, tile), lambda j: (j // per, 0, j % per)),
            pl.BlockSpec((1, tile), lambda j: (0, j)),
        ],
        out_specs=[col, col],
        out_shape=[jax.ShapeDtypeStruct((rows, 2 * units), bf16)] * 2,
        compiler_params=pltpu.CompilerParams(vmem_limit_bytes=56 * 2**20),
    )(x, w, bias)


def units_back_kernel(e_ref, w_ref, slope_ref, du_ref, sum_ref):
    total = 0.0
    for i in range(4):
        rows = slice(256 * i, 256 * (i + 1))
        d = lax.dot_general(e_ref[rows, :], w_ref[0], NN, preferred_element_type=f32)
        du = (d * slope_ref[rows, :].astype(f32)).astype(bf16)
        du_ref[rows, :] = du
        total = total + jnp.sum(du.astype(f32), 0, keepdims=True)
    sum_ref[...] = total


def hidden_units_back(e, w, slope, tile):
    rows, width = e.shape
    units = w.shape[2] // 2
    per = units // tile
    col = pl.BlockSpec((rows, tile), lambda j: (0, j))
    return pl.pallas_call(
        units_back_kernel,
        grid=(2 * per,),
        in_specs=[
            pl.BlockSpec((rows, width), lambda j: (0, 0)),
            pl.BlockSpec((1, width, tile), lambda j: (j // per, 0, per + j % per)),
            col,
        ],
        out_specs=[col, pl.BlockSpec((1, tile), lambda j: (0, j))],
        out_shape=[
            jax.ShapeDtypeStruct((rows, 2 * units), bf16),
            jax.ShapeDtypeStruct((1, 2 * units), f32),
        ],
        compiler_params=pltpu.CompilerParams(vmem_limit_bytes=56 * 2**20),
    )(e, w, slope)


def down_kernel(act_ref, w_ref, h_ref, cot_ref, vec_ref, mixed_ref, dr_ref, e_ref, sum_ref):
    units = w_ref.shape[2]
    r = h_ref[...] + vec_ref[0:1]
    for t in range(2):
        part = act_ref[:, t * units : (t + 1) * units]
        r = r + lax.dot_general(part, w_ref[t], NT, preferred_element_type=f32)
    gain = vec_ref[1:2]
    h, n, inv = norm_rows(r, gain, vec_ref[2:3])
    mixed_ref[...] = h.astype(bf16)
    rows_back(cot_ref[...].astype(f32), n, inv, gain, dr_ref, e_ref, sum_ref)


def rows_back(e, n, inv, gain, dr_ref, e_ref, sum_ref):
    dr, gg, gs, gb = norm_rows_back(e, n, inv, gain)
    dr_ref[...] = dr
    e_ref[...] = dr.astype(bf16)

    @pl.when(pl.program_id(0) == 0)
    def _():
        sum_ref[...] = jnp.zeros_like(sum_ref)

    sum_ref[0:3] += jnp.concatenate([gg[None], gs[None], gb[None]], 0)


def down_and_norms(act, w, h, cot, vecs, block):
    rows, width = h.shape
    units = w.shape[2] // 2
    row = pl.BlockSpec((block, width), lambda i: (i, 0))
    top = pl.BlockSpec((8, width), lambda i: (0, 0))
    return pl.pallas_call(
        down_kernel,
        grid=(rows // block,),
        in_specs=[
            pl.BlockSpec((block, 2 * units), lambda i: (i, 0)),
            pl.BlockSpec((2, width, units), lambda i: (0, 0, 1), pipeline_mode=pl.Buffered(1)),
            row,
            row,
            top,
        ],
        out_specs=[row, row, row, top],
        out_shape=[
            jax.ShapeDtypeStruct((rows, width), bf16),
            jax.ShapeDtypeStruct((rows, width), f32),
            jax.ShapeDtypeStruct((rows, width), bf16),
            jax.ShapeDtypeStruct((8, width), f32),
        ],
        compiler_params=pltpu.CompilerParams(vmem_limit_bytes=56 * 2**20),
    )(act, w, h, cot, vecs)


def up_back_kernel(du_ref, w_ref, dr3_ref, n_ref, inv_ref, vec_ref, dr_ref, e_ref, sum_ref):
    units = w_ref.shape[2]
    e = dr3_ref[...]
    for t in range(2):
        part = du_ref[:, t * units : (t + 1) * units]
        e = e + lax.dot_general(part, w_ref[t], NT, preferred_element_type=f32)
    rows_back(e, n_ref[...], inv_ref[...], vec_ref[0:1], dr_ref, e_ref, sum_ref)


def up_back_and_norm(du, w, dr3, n, inv, vecs, block):
    rows, width = dr3.shape
    units = w.shape[2] // 2
    row = pl.BlockSpec((block, width), lambda i: (i, 0))
    top = pl.BlockSpec((8, width), lambda i: (0, 0))
    return pl.pallas_call(
        up_back_kernel,
        grid=(rows // block,),
        in_specs=[
            pl.BlockSpec((block, 2 * units), lambda i: (i, 0)),
            pl.BlockSpec((2, width, units), lambda i: (0, 0, 0), pipeline_mode=pl.Buffered(1)),
            row,
            row,
            pl.BlockSpec((block, 1), lambda i: (i, 0)),
            top,
        ],
        out_specs=[row, row, top],
        out_shape=[
            jax.ShapeDtypeStruct((rows, width), f32),
            jax.ShapeDtypeStruct((rows, width), bf16),
            jax.ShapeDtypeStruct((8, width), f32),
        ],
        compiler_params=pltpu.CompilerParams(vmem_limit_bytes=56 * 2**20),
    )(du, w, dr3, n, inv, vecs)


def weight_grads_kernel(a_ref,b_ref,da_ref,db_ref,out_ref,at,bt,*,tiles):
    j=pl.program_id(0)
    @pl.when(j==0)
    def _():
        at[...]=a_ref[...].T
        bt[...]=b_ref[...].T
    kind=(j//tiles)%2
    @pl.when(kind==0)
    def _():
        out_ref[0]=lax.dot_general(at[...],da_ref[...],NN,preferred_element_type=f32).astype(bf16)
    @pl.when(kind==1)
    def _():
        out_ref[0]=lax.dot_general(bt[...],db_ref[...],NN,preferred_element_type=f32).astype(bf16)

def weight_grads(a,b,da,db,tile=512):
    rows,width=a.shape; half=da.shape[1]//2; tiles=half//tile
    whole=pl.BlockSpec((rows,width),lambda j:(0,0))
    t=lambda j: j//(2*tiles)
    kind=lambda j:(j//tiles)%2
    i=lambda j: j%tiles
    return pl.pallas_call(
        functools.partial(weight_grads_kernel,tiles=tiles),
        grid=(4*tiles,),
        in_specs=[whole,whole,
          pl.BlockSpec((rows,tile),lambda j:(0,t(j)*tiles+jnp.where(kind(j)==0,i(j),tiles-1))),
          pl.BlockSpec((rows,tile),lambda j:(0,t(j)*tiles+jnp.where(kind(j)==1,i(j),0)))],
        out_specs=pl.BlockSpec((1,width,tile),lambda j:(t(j),0,kind(j)*tiles+i(j))),
        out_shape=jax.ShapeDtypeStruct((2,width,2*half),bf16),
        scratch_shapes=[pltpu.VMEM((width,rows),bf16)]*2,
        compiler_params=pltpu.CompilerParams(vmem_limit_bytes=56*2**20),
    )(a,b,da,db)


def nn(a, b):
    return lax.dot_general(a, b, NN, preferred_element_type=f32)


def nt(a, b):
    return lax.dot_general(a, b, NT, preferred_element_type=f32)


def tn(a, b):
    return lax.dot_general(a, b, (((0,), (0,)), ((), ())), preferred_element_type=f32)


def norm_rows(r, gain, shift):
    center = r - jnp.mean(r, -1, keepdims=True)
    inv = lax.rsqrt(jnp.mean(center * center, -1, keepdims=True) + NORM_EPS)
    n = center * inv
    return n * gain + shift, n, inv


def norm_rows_back(e, n, inv, gain):
    eg = e * gain
    grad = inv * (eg - jnp.mean(eg, -1, keepdims=True) - n * jnp.mean(eg * n, -1, keepdims=True))
    return grad, jnp.sum(e * n, 0), jnp.sum(e, 0), jnp.sum(grad, 0)


def trade(x):
    return lax.ppermute(x, "tp", [(0, 1), (1, 0)])


def in_order(place, own, other, axis=0):
    return jnp.where(
        place == 0,
        jnp.concatenate([own, other], axis),
        jnp.concatenate([other, own], axis),
    )


def own_sequence(piece, place):
    own = lax.dynamic_index_in_dim(piece, place, 0, keepdims=False)
    away = lax.dynamic_index_in_dim(piece, 1 - place, 0, keepdims=False)
    return in_order(place, own, trade(away))


def to_pieces(rows, place):
    half = rows.shape[0] // 2
    halves = rows.reshape(2, half, rows.shape[1])
    own = lax.dynamic_index_in_dim(halves, place, 0, keepdims=True)
    away = lax.dynamic_index_in_dim(halves, 1 - place, 0, keepdims=True)
    return in_order(place, own, trade(away))


def whole_sequences(
    layer_in,
    memory,
    out_grad,
    w_self_in,
    w_self_out,
    w_cross_in,
    w_cross_out,
    w_up,
    w_down,
    head_bias,
    up_bias,
    norm_gain,
    row_bias,
):
    place = lax.axis_index("tp")
    width = layer_in.shape[2]
    cols = w_self_in.shape[2]
    units = w_up.shape[1]
    shard = w_self_in.shape[0]
    gains = norm_gain.astype(f32)
    shifts = row_bias.astype(f32)

    def gather(*parts):
        mine = jnp.concatenate(parts, 1)
        both = lax.all_gather(mine, ("tp", "fsdp"), axis=0, tiled=True)
        return both.reshape(2, width, mine.shape[1])

    small = jnp.concatenate([head_bias.reshape(-1), up_bias])
    small = in_order(place, small[None], trade(small)[None])
    hb = small[:, : 4 * cols].reshape(2, 4, cols).astype(f32)
    ub = small[:, 4 * cols :].astype(f32)

    c3, c4 = 3 * cols, 4 * cols
    g_att, (x, mem) = gather_weights(
        jnp.concatenate(
            [
                w_self_in.reshape(shard, c3),
                w_self_out.T,
                w_cross_in.reshape(shard, c3),
                w_cross_out.T,
            ],
            1,
        ),
        (layer_in, memory),
        1,
        8,
    )
    g_att, w_up, w_down = lax.optimization_barrier((g_att, w_up, w_down))
    g_self, g_cross = g_att[:, :, :c4], g_att[:, :, c4:]
    g_ffn = gather(w_up, w_down.T)
    g_ffn, out_grad = lax.optimization_barrier((g_ffn, out_grad))
    cot = own_sequence(out_grad, place)
    xf = x.astype(f32)
    halves = (0, 1)
    zero = jnp.zeros((cols,), f32)
    scale3 = jnp.concatenate([zero + ATT_SCALE, zero + 1.0, zero + 1.0])
    blk = cols // 128

    sy, sa, sl = [], [], []
    for t in halves:
        bias = jnp.concatenate([hb[t, 0], zero, hb[t, 1]])
        y = ((nn(x, g_self[t, :, :c3]) + bias) * scale3).astype(bf16)
        o, lse = att_fwd(y, y, y, True, 512, 0, blk, 2 * blk, cols)
        sy.append(y)
        sa.append(o)
        sl.append(lse)
    r1 = xf + (nt(sa[0], g_self[0, :, c3:]) + nt(sa[1], g_self[1, :, c3:])) + shifts[0]
    h1, n1, i1 = norm_rows(r1, gains[0], shifts[3])
    h1b = h1.astype(bf16)

    cq, ckv, ca, cl = [], [], [], []
    for t in halves:
        kv = (nn(mem, g_cross[t, :, cols:c3]) + jnp.concatenate([zero, hb[t, 3]])).astype(bf16)
        q = ((nn(h1b, g_cross[t, :, :cols]) + hb[t, 2]) * ATT_SCALE).astype(bf16)
        o, lse = att_fwd(q, kv, kv, False, 512, 0, 0, blk, cols)
        cq.append(q)
        ckv.append(kv)
        ca.append(o)
        cl.append(lse)
    r2 = h1 + (nt(ca[0], g_cross[0, :, c3:]) + nt(ca[1], g_cross[1, :, c3:])) + shifts[1]
    h2, n2, i2 = norm_rows(r2, gains[1], shifts[4])
    h2b = h2.astype(bf16)

    act, slope = hidden_units(h2b, g_ffn, ub.reshape(1, 2 * units), 512)
    none = jnp.zeros((5, width), f32)
    mixed_rows, dr3, e3, sums3 = down_and_norms(
        act,
        g_ffn,
        h2,
        cot,
        jnp.concatenate([shifts[2:3], gains[2:3], shifts[5:6], none], 0),
        256,
    )
    gg3, gs3, gb3 = sums3[0], sums3[1], sums3[2]
    mixed = to_pieces(mixed_rows, place)

    du, gu = hidden_units_back(e3, g_ffn, slope, 512)
    grad_ffn = weight_grads(h2b, e3, du, act, 1024)
    grad_ffn, du = lax.optimization_barrier((grad_ffn, du))
    s_ffn = lax.psum_scatter(
        grad_ffn.reshape(2 * width, 2 * units), ("tp", "fsdp"), scatter_dimension=0, tiled=True
    ).astype(f32)
    dr2, e2, sums2 = up_back_and_norm(
        du,
        g_ffn,
        dr3,
        n2,
        i2,
        jnp.concatenate([gains[1:2], none, none[:2]], 0),
        256,
    )
    gg2, gs2, gb2 = sums2[0], sums2[1], sums2[2]

    dcq, dck, dcv = [], [], []
    for t in halves:
        da = nn(e2, g_cross[t, :, c3:]).astype(bf16)
        a, b, c = att_bwd(cq[t], ckv[t], ckv[t], ca[t], da, cl[t], False, 256, 0, 0, blk)
        dcq.append(a)
        dck.append(b)
        dcv.append(c)
    low = lambda v: v.astype(bf16)
    grads = [
        tuple(low(tn(h1b, dcq[t])) for t in halves),
        tuple(low(tn(mem, dck[t])) for t in halves),
        tuple(low(tn(mem, dcv[t])) for t in halves),
        tuple(low(tn(e2, ca[t])) for t in halves),
    ]
    dmem = sum(
        nt(dck[t], g_cross[t, :, cols : 2 * cols]) + nt(dcv[t], g_cross[t, :, 2 * cols : c3])
        for t in halves
    )
    d_memory = to_pieces(dmem.astype(bf16), place)
    dh1 = dr2 + (nt(dcq[0], g_cross[0, :, :cols]) + nt(dcq[1], g_cross[1, :, :cols]))
    dr1, gg1, gs1, gb1 = norm_rows_back(dh1, n1, i1, gains[0])
    e1 = dr1.astype(bf16)

    dsq, dsk, dsv = [], [], []
    for t in halves:
        da = nn(e1, g_self[t, :, c3:]).astype(bf16)
        y = sy[t]
        a, b, c = att_bwd(y, y, y, sa[t], da, sl[t], True, 256, 0, blk, 2 * blk)
        dsq.append(a)
        dsk.append(b)
        dsv.append(c)
    grads += [
        tuple(low(tn(x, dsq[t])) for t in halves),
        tuple(low(tn(x, dsk[t])) for t in halves),
        tuple(low(tn(x, dsv[t])) for t in halves),
        tuple(low(tn(e1, sa[t])) for t in halves),
    ]
    dx = dr1 + sum(
        nt(dsq[t], g_self[t, :, :cols])
        + nt(dsk[t], g_self[t, :, cols : 2 * cols])
        + nt(dsv[t], g_self[t, :, 2 * cols : c3])
        for t in halves
    )

    def col_sums(pair):
        return jnp.stack([jnp.sum(p.astype(f32), 0) for p in pair])

    gh = jnp.stack([col_sums(dsq), col_sums(dsv), col_sums(dcq), col_sums(dcv)], 1)
    flat = jnp.concatenate(
        [
            v.reshape(-1)
            for v in (gh, gu, gg1, gg2, gg3, gb1, gb2, gb3, gs1, gs2, gs3)
        ]
    )
    s_att, flat, d_layer_in = scatter_grads(
        grads, (mixed, d_memory), dx.astype(bf16), flat.reshape(-1, 128), 2
    )
    flat = flat.reshape(-1)
    head_sum = lax.dynamic_index_in_dim(flat[: 8 * cols].reshape(2, 4, cols), place, 0, False)
    unit_sum = lax.dynamic_index_in_dim(
        flat[8 * cols : 8 * cols + 2 * units].reshape(2, units), place, 0, False
    )
    rest = flat[8 * cols + 2 * units :].reshape(9, width)

    cross_part, self_part = s_att[:, : 4 * cols], s_att[:, 4 * cols :]
    return (
        mixed,
        d_layer_in,
        d_memory,
        self_part[:, :c3].reshape(shard, 3, cols),
        self_part[:, c3:].T,
        cross_part[:, :c3].reshape(shard, 3, cols),
        cross_part[:, c3:].T,
        s_ffn[:, :units],
        s_ffn[:, units:].T,
        head_sum,
        unit_sum,
        rest[:3],
        rest[3:],
    )


def on_device(layer_in, *rest):
    paired = lax.axis_size("tp") == 2 and layer_in.shape[0] == 2
    if paired and lax.axis_size("fsdp") == 16:
        return whole_sequences(layer_in, *rest)
    return shared_sequences(layer_in, *rest)


def solution(mesh):
    return jax.shard_map(
        on_device,
        mesh=mesh,
        in_specs=(
            P("fsdp", "tp", None),
            P("fsdp", "tp", None),
            P("fsdp", "tp", None),
            P("fsdp", None, "tp"),
            P("tp", "fsdp"),
            P("fsdp", None, "tp"),
            P("tp", "fsdp"),
            P("fsdp", "tp"),
            P("tp", "fsdp"),
            P(None, "tp"),
            P("tp"),
            P(),
            P(),
        ),
        out_specs=(
            P("fsdp", "tp", None),
            P("fsdp", "tp", None),
            P("fsdp", "tp", None),
            P("fsdp", None, "tp"),
            P("tp", "fsdp"),
            P("fsdp", None, "tp"),
            P("tp", "fsdp"),
            P("fsdp", "tp"),
            P("tp", "fsdp"),
            P(None, "tp"),
            P("tp"),
            P(),
            P(),
        ),
        check_vma=False,
    )
```

```python
import functools

import jax
import jax.numpy as jnp
from jax import lax
from jax.experimental import pallas as pl
from jax.experimental.pallas import tpu as pltpu
from jax.sharding import PartitionSpec as P

HD = 64
NORM_EPS = 1e-05
ATT_SCALE = 0.125


def times_back(left, right):
    return lax.dot_general(
        left, right, (((1,), (1,)), ((), ())), preferred_element_type=jnp.float32
    )


def over_rows(left, right):
    return lax.dot_general(
        left, right, (((0,), (0,)), ((), ())), preferred_element_type=jnp.float32
    )


def whole_rows(piece):
    return lax.all_gather(piece, "tp", axis=1, tiled=True)


def whole_grads(piece):
    return lax.all_gather(piece, "tp", axis=1, tiled=True)


def branch_sum(term):
    return lax.psum_scatter(
        term.astype(jnp.bfloat16), "tp", scatter_dimension=1, tiled=True
    ).astype(jnp.float32)


def piece_sum(term):
    return lax.psum_scatter(
        term.astype(jnp.bfloat16), "tp", scatter_dimension=1, tiled=True
    ).astype(jnp.float32)


def norm_forward(resid, gain, shift):
    center = resid - jnp.mean(resid, -1, keepdims=True)
    spread = jnp.mean(center * center, -1, keepdims=True)
    inv_std = lax.rsqrt(spread + NORM_EPS)
    normed = center * inv_std
    return (normed * gain + shift, normed, inv_std)


def norm_backward(grad_out, normed, inv_std, gain):
    grad_normed = grad_out * gain
    grad_resid = inv_std * (
        grad_normed
        - jnp.mean(grad_normed, -1, keepdims=True)
        - normed * jnp.mean(grad_normed * normed, -1, keepdims=True)
    )
    return (grad_resid, jnp.sum(grad_out * normed, (0, 1)), jnp.sum(grad_out, (0, 1)))


def gelu_exact(pre_act):
    return jax.nn.gelu(pre_act, approximate=False)


def gelu_back(pre_act, grad_act):
    unused_out, pull_back = jax.vjp(gelu_exact, pre_act)
    return pull_back(grad_act)[0]


def masked_scores(query_blk, block_start, keys_seq, causal):
    scores = jnp.einsum("qhc,khc->hqk", query_blk, keys_seq, preferred_element_type=jnp.float32)
    if causal:
        row_pos = block_start + lax.broadcasted_iota(jnp.int32, scores.shape[1:], 0)
        col_pos = lax.broadcasted_iota(jnp.int32, scores.shape[1:], 1)
        scores = jnp.where(row_pos >= col_pos, scores, -1e30)
    return scores


def attend_forward(query, keys, values, causal):
    seq_count, length, heads_dev, depth = query.shape
    block_rows = min(512, length)
    block_count = length // block_rows
    block_starts = jnp.arange(block_count, dtype=jnp.int32) * block_rows

    def one_sequence(seq_item):
        query_seq, keys_seq, values_seq = seq_item

        def one_block(blk_item):
            query_blk, block_start = blk_item
            scores = masked_scores(query_blk, block_start, keys_seq, causal)
            row_max = jnp.max(scores, -1, keepdims=True)
            log_total = row_max + jnp.log(jnp.sum(jnp.exp(scores - row_max), -1, keepdims=True))
            probs = jnp.exp(scores - log_total).astype(jnp.bfloat16)
            block_out = jnp.einsum(
                "hqk,khc->qhc", probs, values_seq, preferred_element_type=jnp.float32
            )
            return (block_out.astype(jnp.bfloat16), log_total)

        block_outs, log_totals = lax.map(
            one_block, (query_seq.reshape(block_count, block_rows, heads_dev, depth), block_starts)
        )
        return (block_outs.reshape(length, heads_dev, depth), log_totals)

    return lax.map(one_sequence, (query, keys, values))


def attend_backward(query, keys, values, log_totals, grad_out, causal):
    seq_count, length, heads_dev, depth = query.shape
    block_rows = min(512, length)
    block_count = length // block_rows
    block_starts = jnp.arange(block_count, dtype=jnp.int32) * block_rows

    def one_sequence(seq_item):
        query_seq, keys_seq, values_seq, total_seq, grad_seq = seq_item

        def one_block(carry, blk_item):
            query_blk, grad_blk, total_blk, block_start = blk_item
            probs = jnp.exp(masked_scores(query_blk, block_start, keys_seq, causal) - total_blk)
            grad_probs = jnp.einsum(
                "qhc,khc->hqk", grad_blk, values_seq, preferred_element_type=jnp.float32
            )
            row_delta = jnp.sum(probs * grad_probs, -1, keepdims=True)
            grad_scores = (probs * (grad_probs - row_delta)).astype(jnp.bfloat16)
            grad_query = jnp.einsum(
                "hqk,khc->qhc", grad_scores, keys_seq, preferred_element_type=jnp.float32
            )
            grad_keys = carry[0] + jnp.einsum(
                "hqk,qhc->khc", grad_scores, query_blk, preferred_element_type=jnp.float32
            )
            grad_values = carry[1] + jnp.einsum(
                "hqk,qhc->khc",
                probs.astype(jnp.bfloat16),
                grad_blk,
                preferred_element_type=jnp.float32,
            )
            return ((grad_keys, grad_values), grad_query)

        zero_keys = jnp.zeros(keys_seq.shape, jnp.float32)
        blk_items = (
            query_seq.reshape(block_count, block_rows, heads_dev, depth),
            grad_seq.reshape(block_count, block_rows, heads_dev, depth),
            total_seq,
            block_starts,
        )
        (grad_keys, grad_values), grad_query = lax.scan(
            one_block, (zero_keys, zero_keys), blk_items
        )
        return (grad_query.reshape(length, heads_dev, depth), grad_keys, grad_values)

    return lax.map(one_sequence, (query, keys, values, log_totals, grad_out))


def shared_sequences(
    layer_in,
    memory,
    out_grad,
    w_self_in,
    w_self_out,
    w_cross_in,
    w_cross_out,
    w_up,
    w_down,
    head_bias,
    up_bias,
    norm_gain,
    row_bias,
):
    seq_count, piece_len, model_width = layer_in.shape
    head_cols = w_self_in.shape[2]
    unit_cols = w_up.shape[1]
    heads_dev = head_cols // HD
    tp_place = lax.axis_index("tp")
    tp_count = lax.axis_size("tp")
    zero_index = jnp.zeros((), jnp.int32)
    gains = norm_gain.astype(jnp.float32)
    shifts = row_bias.astype(jnp.float32)
    col_bias = head_bias.astype(jnp.float32)
    unit_bias = up_bias.astype(jnp.float32)
    self_in, self_out, cross_in, cross_out, up_full, down_full = (
        lax.all_gather(w_self_in, "fsdp", axis=0, tiled=True),
        lax.all_gather(w_self_out, "fsdp", axis=1, tiled=True),
        lax.all_gather(w_cross_in, "fsdp", axis=0, tiled=True),
        lax.all_gather(w_cross_out, "fsdp", axis=1, tiled=True),
        lax.all_gather(w_up, "fsdp", axis=0, tiled=True),
        lax.all_gather(w_down, "fsdp", axis=1, tiled=True),
    )
    layer_whole = whole_rows(layer_in)
    length = layer_whole.shape[1]
    row_count = seq_count * length
    token_rows = layer_whole.reshape(row_count, model_width)
    self_proj = jnp.einsum("rd,dkc->rkc", token_rows, self_in, preferred_element_type=jnp.float32)
    self_query = ((self_proj[:, 0] + col_bias[0]) * ATT_SCALE).astype(jnp.bfloat16)
    self_keys = self_proj[:, 1].astype(jnp.bfloat16)
    self_values = (self_proj[:, 2] + col_bias[1]).astype(jnp.bfloat16)
    head_shape = (seq_count, length, heads_dev, HD)
    self_att, self_totals = attend_forward(
        self_query.reshape(head_shape),
        self_keys.reshape(head_shape),
        self_values.reshape(head_shape),
        True,
    )
    self_rows = self_att.reshape(row_count, head_cols)
    self_term = jnp.dot(self_rows, self_out, preferred_element_type=jnp.float32).reshape(
        seq_count, length, model_width
    )
    resid_one = layer_in.astype(jnp.float32) + branch_sum(self_term) + shifts[0]
    normed_one, unit_one, inv_one = norm_forward(resid_one, gains[0], shifts[3])
    normed_rows = whole_rows(normed_one.astype(jnp.bfloat16)).reshape(row_count, model_width)
    cross_query = (
        (jnp.dot(normed_rows, cross_in[:, 0], preferred_element_type=jnp.float32) + col_bias[2])
        * ATT_SCALE
    ).astype(jnp.bfloat16)
    memory_whole = lax.all_gather(memory, "tp", axis=1, tiled=True)
    source_len = memory_whole.shape[1]
    source_rows = memory_whole.reshape(seq_count * source_len, model_width)
    cross_proj = jnp.einsum(
        "rd,dkc->rkc", source_rows, cross_in[:, 1:], preferred_element_type=jnp.float32
    )
    cross_keys = cross_proj[:, 0].astype(jnp.bfloat16)
    cross_values = (cross_proj[:, 1] + col_bias[3]).astype(jnp.bfloat16)
    source_shape = (seq_count, source_len, heads_dev, HD)
    cross_att, cross_totals = attend_forward(
        cross_query.reshape(head_shape),
        cross_keys.reshape(source_shape),
        cross_values.reshape(source_shape),
        False,
    )
    cross_rows = cross_att.reshape(row_count, head_cols)
    cross_term = jnp.dot(cross_rows, cross_out, preferred_element_type=jnp.float32).reshape(
        seq_count, length, model_width
    )
    resid_two = normed_one + branch_sum(cross_term) + shifts[1]
    normed_two, unit_two, inv_two = norm_forward(resid_two, gains[1], shifts[4])
    normed_two_low = normed_two.astype(jnp.bfloat16)
    ffn_rows = whole_rows(normed_two_low).reshape(row_count, model_width)
    pre_act = jnp.dot(ffn_rows, up_full, preferred_element_type=jnp.float32) + unit_bias
    hidden_act = gelu_exact(pre_act).astype(jnp.bfloat16)
    ffn_term = jnp.dot(hidden_act, down_full, preferred_element_type=jnp.float32).reshape(
        seq_count, length, model_width
    )
    ffn_out = branch_sum(ffn_term)
    resid_three = normed_two + ffn_out + shifts[2]
    mixed, unit_three, inv_three = norm_forward(resid_three, gains[2], shifts[5])
    grad_three, gain_grad_three, shift_grad_three = norm_backward(
        out_grad.astype(jnp.float32), unit_three, inv_three, gains[2]
    )
    bias_grad_three = jnp.sum(grad_three, (0, 1))
    grad_three_low = grad_three.astype(jnp.bfloat16)
    grad_rows = whole_grads(grad_three_low).reshape(row_count, model_width)
    grad_act = times_back(grad_rows, down_full)
    grad_pre = gelu_back(pre_act, grad_act).astype(jnp.bfloat16)
    d_up = over_rows(ffn_rows, grad_pre)
    d_down = over_rows(hidden_act, grad_rows)
    unit_grad = jnp.sum(grad_pre, 0, dtype=jnp.float32)
    grad_two_in = piece_sum(times_back(grad_pre, up_full).reshape(seq_count, length, model_width))
    grad_normed_two = grad_three + grad_two_in
    grad_two, gain_grad_two, shift_grad_two = norm_backward(
        grad_normed_two, unit_two, inv_two, gains[1]
    )
    bias_grad_two = jnp.sum(grad_two, (0, 1))
    grad_two_rows = whole_grads(grad_two.astype(jnp.bfloat16)).reshape(row_count, model_width)
    d_cross_out = over_rows(cross_rows, grad_two_rows)
    grad_cross_att = times_back(grad_two_rows, cross_out).astype(jnp.bfloat16)
    cq_grad, ck_grad, cv_grad = attend_backward(
        cross_query.reshape(head_shape),
        cross_keys.reshape(source_shape),
        cross_values.reshape(source_shape),
        cross_totals,
        grad_cross_att.reshape(head_shape),
        False,
    )
    cq_pre = cq_grad.reshape(row_count, head_cols).astype(jnp.bfloat16) * jnp.asarray(
        ATT_SCALE, jnp.bfloat16
    )
    ckv_low = jnp.stack(
        [
            ck_grad.reshape(seq_count * source_len, head_cols),
            cv_grad.reshape(seq_count * source_len, head_cols),
        ],
        1,
    ).astype(jnp.bfloat16)
    cross_q_grad = over_rows(normed_rows, cq_pre)
    cq_bias_grad = jnp.sum(cq_pre, 0, dtype=jnp.float32)
    normed_part = times_back(cq_pre, cross_in[:, 0]).reshape(seq_count, length, model_width)
    source_part = jnp.einsum(
        "rkc,dkc->rd", ckv_low, cross_in[:, 1:], preferred_element_type=jnp.float32
    ).reshape(seq_count, source_len, model_width)
    grad_one_in, memory_grad = (
        lax.psum_scatter(
            normed_part.astype(jnp.bfloat16), "tp", scatter_dimension=1, tiled=True
        ).astype(jnp.float32),
        lax.psum_scatter(
            source_part.astype(jnp.bfloat16), "tp", scatter_dimension=1, tiled=True
        ).astype(jnp.float32),
    )
    d_memory = memory_grad.astype(jnp.bfloat16)
    cross_kv_grad = jnp.einsum(
        "rd,rkc->dkc", source_rows, ckv_low, preferred_element_type=jnp.float32
    )
    cross_grad_term = jnp.concatenate([cross_q_grad[:, None, :], cross_kv_grad], 1)
    cv_own = jnp.sum(ckv_low[:, 1], 0, dtype=jnp.float32)
    cv_wide = lax.dynamic_update_slice(
        jnp.zeros((head_cols * tp_count,), jnp.float32), cv_own, (tp_place * head_cols,)
    )
    grad_normed_one = grad_two + grad_one_in
    grad_one, gain_grad_one, shift_grad_one = norm_backward(
        grad_normed_one, unit_one, inv_one, gains[0]
    )
    bias_grad_one = jnp.sum(grad_one, (0, 1))
    grad_one_rows = whole_grads(grad_one.astype(jnp.bfloat16)).reshape(row_count, model_width)
    d_self_out = over_rows(self_rows, grad_one_rows)
    grad_self_att = times_back(grad_one_rows, self_out).astype(jnp.bfloat16)
    sq_grad, sk_grad, sv_grad = attend_backward(
        self_query.reshape(head_shape),
        self_keys.reshape(head_shape),
        self_values.reshape(head_shape),
        self_totals,
        grad_self_att.reshape(head_shape),
        True,
    )
    sq_pre = sq_grad.reshape(row_count, head_cols).astype(jnp.bfloat16) * jnp.asarray(
        ATT_SCALE, jnp.bfloat16
    )
    sqkv_low = jnp.stack(
        [
            sq_pre,
            sk_grad.reshape(row_count, head_cols).astype(jnp.bfloat16),
            sv_grad.reshape(row_count, head_cols).astype(jnp.bfloat16),
        ],
        1,
    )
    d_self_in = jnp.einsum("rd,rkc->dkc", token_rows, sqkv_low, preferred_element_type=jnp.float32)
    sq_bias_grad = jnp.sum(sq_pre, 0, dtype=jnp.float32)
    sv_bias_grad = jnp.sum(sqkv_low[:, 2], 0, dtype=jnp.float32)
    layer_part = jnp.einsum(
        "rkc,dkc->rd", sqkv_low, self_in, preferred_element_type=jnp.float32
    ).reshape(seq_count, length, model_width)
    d_layer_in = (grad_one + piece_sum(layer_part)).astype(jnp.bfloat16)
    slot_grad = jnp.stack([sq_bias_grad, sv_bias_grad, cq_bias_grad])
    slot_wide = lax.dynamic_update_slice(
        jnp.zeros((3, head_cols * tp_count), jnp.float32),
        slot_grad,
        (zero_index, tp_place * head_cols),
    )
    head_wide = jnp.concatenate([slot_wide, cv_wide[None, :]], 0)
    unit_wide_grad = lax.dynamic_update_slice(
        jnp.zeros((unit_cols * tp_count,), jnp.float32), unit_grad, (tp_place * unit_cols,)
    )
    gain_grads = jnp.stack([gain_grad_one, gain_grad_two, gain_grad_three])
    shift_grads = jnp.stack(
        [
            bias_grad_one,
            bias_grad_two,
            bias_grad_three,
            shift_grad_one,
            shift_grad_two,
            shift_grad_three,
        ]
    )
    gain_total, shift_total, head_total, unit_total = lax.psum(
        (gain_grads, shift_grads, head_wide, unit_wide_grad), ("fsdp", "tp")
    )
    d_head_bias = lax.dynamic_slice(head_total, (zero_index, tp_place * head_cols), (4, head_cols))
    d_up_bias = lax.dynamic_slice(unit_total, (tp_place * unit_cols,), (unit_cols,))
    g_self_in, g_self_out, g_cross_part, g_cross_out, g_up, g_down = (
        lax.psum_scatter(
            d_self_in.astype(jnp.bfloat16), "fsdp", scatter_dimension=0, tiled=True
        ).astype(jnp.float32),
        lax.psum_scatter(
            d_self_out.astype(jnp.bfloat16), "fsdp", scatter_dimension=1, tiled=True
        ).astype(jnp.float32),
        lax.psum_scatter(
            cross_grad_term.astype(jnp.bfloat16), "fsdp", scatter_dimension=0, tiled=True
        ).astype(jnp.float32),
        lax.psum_scatter(
            d_cross_out.astype(jnp.bfloat16), "fsdp", scatter_dimension=1, tiled=True
        ).astype(jnp.float32),
        lax.psum_scatter(d_up.astype(jnp.bfloat16), "fsdp", scatter_dimension=0, tiled=True).astype(
            jnp.float32
        ),
        lax.psum_scatter(
            d_down.astype(jnp.bfloat16), "fsdp", scatter_dimension=1, tiled=True
        ).astype(jnp.float32),
    )
    return (
        mixed.astype(jnp.bfloat16),
        d_layer_in,
        d_memory,
        g_self_in,
        g_self_out,
        g_cross_part,
        g_cross_out,
        g_up,
        g_down,
        d_head_bias,
        d_up_bias,
        gain_total,
        shift_total,
    )


NT=(((1,),(1,)),((),()))
NN=(((1,),(0,)),((),()))
f32=jnp.float32
bf16=jnp.bfloat16

LN2 = 0.6931471805599453
LOG2E = 1.4426950408889634


def att_fwd_kernel(q_ref,k_ref,v_ref,o_ref,lse_ref,*,bq,causal):
    n=q_ref.shape[0]; nk=k_ref.shape[0]
    lane=lax.broadcasted_iota(jnp.int32,(nk,128),1)
    k=k_ref[...]
    zero=jnp.zeros((),bf16)
    kh=[jnp.where(lane<HD,k,zero),jnp.where(lane>=HD,k,zero)]
    vt=v_ref[...].T
    ones=jnp.ones((8,nk),bf16)
    vh=[jnp.concatenate([vt[h*HD:(h+1)*HD],ones],0) for h in range(2)]
    for i in range(n//bq):
        q=q_ref[i*bq:(i+1)*bq,:]
        L=(i+1)*bq if causal else nk
        S=[]
        for h in range(2):
            s=lax.dot_general(kh[h][:L],q,NT,preferred_element_type=f32)
            if causal:
                keep=lax.broadcasted_iota(jnp.int32,(bq,bq),0)<=lax.broadcasted_iota(jnp.int32,(bq,bq),1)
                sd=jnp.where(keep,s[L-bq:],-1e30)
                s=jnp.concatenate([s[:L-bq],sd],0) if L>bq else sd
            S.append(s)
        M=[jnp.max(s,0,keepdims=True) for s in S]
        outs=[];lses=[]
        for h in range(2):
            p=jnp.exp2(S[h]-M[h]).astype(bf16)
            ol=lax.dot_general(vh[h][:,:L],p,NN,preferred_element_type=f32)
            l=ol[HD:HD+1]
            outs.append(ol[:HD]*(1.0/l)); lses.append(M[h]+jnp.log2(l))
        o_ref[i*bq:(i+1)*bq,:]=jnp.concatenate(outs,0).T.astype(bf16)
        lse_ref[0,:,i*bq:(i+1)*bq]=jnp.concatenate(lses,0)

def att_fwd(q,k,v,causal,bq=256,qo=0,ko=0,vo=0,width=None):
    n=q.shape[0]; nk=k.shape[0]; width=width or q.shape[1]; np_=width//128
    spec=lambda rows,off: pl.BlockSpec((rows,128),lambda p: (0,p+off))
    return pl.pallas_call(
        functools.partial(att_fwd_kernel,bq=bq,causal=causal),
        grid=(np_,),
        in_specs=[spec(n,qo),spec(nk,ko),spec(nk,vo)],
        out_specs=[spec(n,0),pl.BlockSpec((1,2,n),lambda p:(p,0,0))],
        out_shape=[jax.ShapeDtypeStruct((n,width),bf16),jax.ShapeDtypeStruct((np_,2,n),f32)],
        compiler_params=pltpu.CompilerParams(dimension_semantics=("arbitrary",),vmem_limit_bytes=56*2**20),
    )(q,k,v)

def att_bwd_kernel(q_ref,k_ref,v_ref,o_ref,do_ref,lse_ref,*refs,bq,causal):
    dq_ref,dk_ref,dv_ref,dk_acc,dv_acc=refs[-5:]
    n=q_ref.shape[0]; nk=k_ref.shape[0]
    lane=lax.broadcasted_iota(jnp.int32,(nk,128),1)
    lq=lax.broadcasted_iota(jnp.int32,(bq,128),1)
    k=k_ref[...]; v=v_ref[...]
    zero=jnp.zeros((),bf16)
    kh=[jnp.where(lane<HD,k,zero),jnp.where(lane>=HD,k,zero)]
    vh=[jnp.where(lane<HD,v,zero),jnp.where(lane>=HD,v,zero)]
    kt=k.T
    dk_acc[...]=jnp.zeros_like(dk_acc); dv_acc[...]=jnp.zeros_like(dv_acc)
    for i in range(n//bq):
        rows=slice(i*bq,(i+1)*bq)
        q=q_ref[rows,:]; do=do_ref[rows,:]
        L=(i+1)*bq if causal else nk
        dot_=(do.astype(f32)*o_ref[rows,:].astype(f32)).T
        qm=[jnp.where(lq<HD,q,zero),jnp.where(lq>=HD,q,zero)]
        dm=[jnp.where(lq<HD,do,zero),jnp.where(lq>=HD,do,zero)]
        dqs=[]
        for h in range(2):
            s=lax.dot_general(kh[h][:L],q,NT,preferred_element_type=f32)
            dp=lax.dot_general(vh[h][:L],do,NT,preferred_element_type=f32)
            lse=lse_ref[0,h:h+1,rows]
            delta=jnp.sum(dot_[h*HD:(h+1)*HD],0,keepdims=True)
            if causal:
                keep=lax.broadcasted_iota(jnp.int32,(bq,bq),0)<=lax.broadcasted_iota(jnp.int32,(bq,bq),1)
                sd=jnp.where(keep,s[L-bq:],-1e30)
                s=jnp.concatenate([s[:L-bq],sd],0) if L>bq else sd
            p=jnp.exp2(s-lse)
            ds=(p*(dp-delta)).astype(bf16)
            pb=p.astype(bf16)
            dv_acc[:L,:]+=lax.dot_general(pb,dm[h],NN,preferred_element_type=f32)
            dk_acc[:L,:]+=lax.dot_general(ds,qm[h],NN,preferred_element_type=f32)
            dqs.append(lax.dot_general(kt[h*HD:(h+1)*HD,:L],ds,NN,preferred_element_type=f32))
        dq_ref[rows,:]=(jnp.concatenate(dqs,0)*0.125).T.astype(bf16)
    dk_ref[...]=(dk_acc[...]*LN2).astype(bf16)
    dv_ref[...]=dv_acc[...].astype(bf16)

def att_bwd(q,k,v,o,do,lse,causal,bq=256,qo=0,ko=0,vo=0,ahead=()):
    n=q.shape[0]; nk=k.shape[0]; width=o.shape[1]; np_=width//128
    spec=lambda rows,off: pl.BlockSpec((rows,128),lambda p: (0,p+off))
    return pl.pallas_call(
        functools.partial(att_bwd_kernel,bq=bq,causal=causal),
        grid=(np_,),
        in_specs=[spec(n,qo),spec(nk,ko),spec(nk,vo),spec(n,0),spec(n,0),pl.BlockSpec((1,2,n),lambda p:(p,0,0))]+[pl.BlockSpec(memory_space=pl.ANY)]*len(ahead),
        out_specs=[spec(n,0),spec(nk,0),spec(nk,0)],
        out_shape=[jax.ShapeDtypeStruct((n,width),bf16),jax.ShapeDtypeStruct((nk,width),bf16),jax.ShapeDtypeStruct((nk,width),bf16)],
        scratch_shapes=[pltpu.VMEM((nk,128),f32)]*2,
        compiler_params=pltpu.CompilerParams(dimension_semantics=("arbitrary",),vmem_limit_bytes=56*2**20),
    )(q,k,v,o,do,lse,*ahead)


MESH = pl.DeviceIdType.MESH
LINKS = ("z1", "z2", "y", "x", "c")


def partners():
    t = lax.axis_index("tp")
    f = lax.axis_index("fsdp")
    z, y, c = f // 4, (f // 2) % 2, f % 2

    def at(z_, y_, c_, t_):
        return (z_ * 4 + y_ * 2 + c_, t_)

    ids = dict(
        z1=at(z + 1 - 2 * (z % 2), y, c, t),
        z2=at((z + 2) % 4, y, c, t),
        y=at(z, 1 - y, c, t),
        x=at(z, y, c, 1 - t),
        c=at(z, y, 1 - c, t),
    )
    return (t, z, y, c), ids


def greet(ids):
    barrier = pltpu.get_barrier_semaphore()
    for name in LINKS:
        pl.semaphore_signal(barrier, inc=1, device_id=ids[name], device_id_type=MESH)
    pl.semaphore_wait(barrier, len(LINKS))


def pipeline(chunks, stages, begin, after_step=None):
    started = {}
    for step in range(chunks + stages):
        for s in range(stages + 1):
            k = step - s
            if 0 <= k < chunks:
                if s > 0:
                    for copy in started[k, s - 1]:
                        copy.wait_recv()
                started[k, s] = begin(k, s)
        if after_step is not None:
            after_step(step)
    for copies in started.values():
        for copy in copies:
            copy.wait_send()


def start_copy(src, dst, send, recv, to):
    copy = pltpu.make_async_remote_copy(
        src_ref=src,
        dst_ref=dst,
        send_sem=send,
        recv_sem=recv,
        device_id=to,
        device_id_type=MESH,
    )
    copy.start()
    return copy


def gather_kernel(shard_ref, *refs, cw, chunks, swaps):
    ins, outs = refs[:swaps], refs[swaps + 1 : 2 * swaps + 1]
    w_ref = refs[swaps]
    send, recv, own, swap_send, swap_recv, swap_own = refs[2 * swaps + 1 :]
    (t, z, y, c), ids = partners()
    mine = pltpu.make_async_copy(shard_ref, w_ref.at[t, z, y, c], own)
    mine.start()
    kept = [
        pltpu.make_async_copy(ins[i].at[t], outs[i].at[t], swap_own.at[i]) for i in range(swaps)
    ]
    for copy in kept:
        copy.start()
    greet(ids)
    pair = (z // 2) * 2
    traded = []

    def begin(k, s):
        cols = pl.ds(k * cw, cw)
        if s == 0:
            r, to = w_ref.at[t, z, y, c, :, cols], "z1"
            copies = [start_copy(shard_ref.at[:, cols], r, send.at[k, 0], recv.at[k, 0], ids[to])]
            for i in range(swaps):
                part = ins[i].shape[1] // chunks
                rows = pl.ds(k * part, part)
                traded.append(
                    start_copy(
                        ins[i].at[1 - t, rows],
                        outs[i].at[t, rows],
                        swap_send.at[i, k],
                        swap_recv.at[i, k],
                        ids["x"],
                    )
                )
            return copies
        if s == 5:
            return []
        if s == 1:
            if k == 0:
                mine.wait()
            r, to = w_ref.at[t, pl.ds(pair, 2), y, c, :, cols], "z2"
        elif s == 2:
            r, to = w_ref.at[t, :, y, c, :, cols], "x"
        elif s == 3:
            r, to = w_ref.at[:, :, y, c, :, cols], "y"
        else:
            r, to = w_ref.at[:, :, :, c, :, cols], "c"
        return [start_copy(r, r, send.at[k, s], recv.at[k, s], ids[to])]

    pipeline(chunks, 5, begin)
    for copy in traded:
        copy.wait()
    for copy in kept:
        copy.wait()


def gather_weights(shard, pieces, cid, chunks):
    rows, cols = shard.shape
    swaps = len(pieces)
    anywhere = pl.BlockSpec(memory_space=pl.ANY)
    dma = pltpu.SemaphoreType.DMA
    outs = pl.pallas_call(
        functools.partial(gather_kernel, cw=cols // chunks, chunks=chunks, swaps=swaps),
        in_specs=[pl.BlockSpec(memory_space=pltpu.VMEM)] + [anywhere] * swaps,
        out_specs=[anywhere] * (1 + swaps),
        out_shape=[jax.ShapeDtypeStruct((2, 4, 2, 2, rows, cols), shard.dtype)]
        + [jax.ShapeDtypeStruct(p.shape, p.dtype) for p in pieces],
        scratch_shapes=[
            dma((chunks, 5)),
            dma((chunks, 5)),
            dma,
            dma((swaps, chunks)),
            dma((swaps, chunks)),
            dma((swaps,)),
        ],
        compiler_params=pltpu.CompilerParams(collective_id=cid, has_side_effects=True),
        cost_estimate=pl.CostEstimate(
            flops=0, bytes_accessed=32 * rows * cols * 20, transcendentals=0
        ),
    )(shard, *pieces)
    whole = outs[0].reshape(2, 16 * rows, cols)
    return whole, [p.reshape(p.shape[0] * p.shape[1], p.shape[2]) for p in outs[1:]]


def scatter_kernel(*refs, given, ahead, wa):
    g_refs, refs = refs[: 2 * given], refs[2 * given :]
    made = 4
    lefts, rights, refs = refs[:2], refs[2 : 2 + 2 * made], refs[2 + 2 * made + ahead :]
    rows_ref, small_ref, out_ref, small_out, pieces_ref = refs[:5]
    own, far, turned, r1, s2, r2, s3, r3, s4, r4, s5, r5, sm, rm = refs[5:19]
    send, recv, own_sem, small_send, small_recv, swap_send, swap_recv, swap_own = refs[19:]
    chunks = given + made
    (t, z, y, c), ids = partners()
    pair = (z // 2) * 2
    away = 2 - pair
    other = 1 - z % 2
    rows, cw = r5.shape[1:]
    sides = (slice(0, wa), slice(wa, cw))

    def loc(k, half):
        return pltpu.make_async_copy(
            g_refs[2 * k + half].at[:, :, c], own.at[k, half], own_sem.at[k, half]
        )

    for k in range(given):
        loc(k, 0).start()
        loc(k, 1).start()
    kept = pltpu.make_async_copy(rows_ref.at[t], pieces_ref.at[t], swap_own)
    kept.start()
    greet(ids)
    traded = []

    def go(k, j, src, dst, to):
        return start_copy(src, dst, send.at[k, j], recv.at[k, j], ids[to])

    def small_go(j):
        to = ids[("c", "x", "y", "z2", "z1")[j]]
        return start_copy(sm.at[j], rm.at[j], small_send.at[j], small_recv.at[j], to)

    def up(v):
        return v.astype(f32)

    def after_core(k, t_, z_, y_, cols):
        return up(own[k, t_, z_, y_, :, cols]) + up(r1[k, t_, z_, y_, :, cols])

    def after_two(k, z_, y_, t_, j):
        at = 2 * z_ + y_ if j == 0 else 4 * t_ + z_
        return after_core(k, t_, z_, y_, sides[j]) + up(r2[k, at, :, sides[j]])

    def after_three(k, z_, j):
        return after_two(k, z_, y, t, j) + up(r3[k, z_, :, sides[j]])

    def begin(k, s):
        a, b = sides
        if s == 0:
            copies = []
            for half in (0, 1):
                src = g_refs[2 * k + half].at[:, :, 1 - c] if k < given else far.at[k - given, half]
                copies.append(go(k, 6 + half, src, r1.at[k, half], "c"))
            return copies
        if s == 1:
            if k < given:
                loc(k, 0).wait()
                loc(k, 1).wait()
            for z_ in range(4):
                for i in range(2):
                    s2[k, 2 * z_ + i, :, a] = after_core(k, 1 - t, z_, i, a).astype(bf16)
            da = go(k, 0, s2.at[k, :, :, pl.ds(0, wa)], r2.at[k, :, :, pl.ds(0, wa)], "x")
            for z_ in range(4):
                for i in range(2):
                    s2[k, 4 * i + z_, :, b] = after_core(k, i, z_, 1 - y, b).astype(bf16)
            side = pl.ds(wa, cw - wa)
            return [da, go(k, 1, s2.at[k, :, :, side], r2.at[k, :, :, side], "y")]
        if s == 2:
            for z_ in range(4):
                s3[k, z_, :, a] = after_two(k, z_, 1 - y, t, 0).astype(bf16)
            da = go(k, 2, s3.at[k, :, :, pl.ds(0, wa)], r3.at[k, :, :, pl.ds(0, wa)], "y")
            for z_ in range(4):
                s3[k, z_, :, b] = after_two(k, z_, y, 1 - t, 1).astype(bf16)
            side = pl.ds(wa, cw - wa)
            return [da, go(k, 3, s3.at[k, :, :, side], r3.at[k, :, :, side], "x")]
        if s == 3:
            for i in range(2):
                for j in range(2):
                    s4[k, i, :, sides[j]] = after_three(k, away + i, j).astype(bf16)
            return [go(k, 4, s4.at[k], r4.at[k], "z2")]
        for j in range(2):
            if s == 4:
                sent = after_three(k, pair + other, j) + up(r4[k, other, :, sides[j]])
                s5[k, :, sides[j]] = sent.astype(bf16)
            else:
                mine = after_three(k, z, j) + up(r4[k, z % 2, :, sides[j]])
                cols = slice(k * cw + sides[j].start, k * cw + sides[j].stop)
                out_ref[:, cols] = mine + up(r5[k, :, sides[j]])
        return [go(k, 5, s5.at[k], r5.at[k], "z1")] if s == 4 else []

    smalls = []

    def begin_with_small(k, s):
        if s == 0:
            part = rows_ref.shape[1] // chunks
            some = pl.ds(k * part, part)
            src, dst = rows_ref.at[1 - t, some], pieces_ref.at[t, some]
            traded.append(start_copy(src, dst, swap_send.at[k], swap_recv.at[k], ids["x"]))
        if k == 0:
            if s == 0:
                sm[0] = small_ref[...]
            else:
                smalls[s - 1].wait_recv()
                total = sm[s - 1] + rm[s - 1]
                if s < 5:
                    sm[s] = total
                else:
                    small_out[...] = total
            if s < 5:
                smalls.append(small_go(s))
        return begin(k, s)

    def make(step):
        if step == 1:
            turned[...] = lefts[0][...].T
        elif step == made + 2:
            turned[...] = lefts[1][...].T
        ready = {2: [(0, 0)], 3: [(0, 1)]}
        for i in range(1, made):
            ready[3 + i] = [(i, 0), (i, 1)]
        for i, half in ready.get(step, []):
            d = rights[2 * i + half][...]
            g = lax.dot_general(turned[...], d, NN, preferred_element_type=f32)
            g = g.astype(bf16).reshape(4, 2, 2, rows, cw)
            own[given + i, half] = jnp.where(c == 0, g[:, :, 0], g[:, :, 1])
            far[i, half] = jnp.where(c == 0, g[:, :, 1], g[:, :, 0])

    pipeline(chunks, 5, begin_with_small, make)
    for copy in smalls:
        copy.wait_send()
    for copy in traded:
        copy.wait()
    kept.wait()


def scatter_grads(pairs, lefts, rights, ahead, seq_rows, small, cid):
    given = len(pairs)
    chunks = given + 4
    tokens, width = lefts[0].shape
    cw = pairs[0][0].shape[1]
    rows, cols = width // 16, cw * chunks
    V = pltpu.VMEM
    dma = pltpu.SemaphoreType.DMA
    flat = [g.reshape(4, 2, 2, rows, cw) for pair in pairs for g in pair]
    seq_rows = seq_rows.reshape(2, seq_rows.shape[0] // 2, seq_rows.shape[1])
    whole = pl.BlockSpec(memory_space=pltpu.VMEM)
    anywhere = pl.BlockSpec(memory_space=pl.ANY)
    return pl.pallas_call(
        functools.partial(scatter_kernel, given=given, ahead=len(ahead), wa=cw // 4),
        in_specs=[anywhere] * len(flat)
        + [whole] * (2 + len(rights))
        + [anywhere] * (len(ahead) + 1)
        + [whole],
        out_specs=[whole, whole, anywhere],
        out_shape=[
            jax.ShapeDtypeStruct((rows, cols), f32),
            jax.ShapeDtypeStruct(small.shape, f32),
            jax.ShapeDtypeStruct(seq_rows.shape, seq_rows.dtype),
        ],
        scratch_shapes=[
            V((chunks, 2, 4, 2, rows, cw), bf16),
            V((4, 2, 4, 2, rows, cw), bf16),
            V((width, tokens), bf16),
            V((chunks, 2, 4, 2, rows, cw), bf16),
            V((chunks, 8, rows, cw), bf16),
            V((chunks, 8, rows, cw), bf16),
            V((chunks, 4, rows, cw), bf16),
            V((chunks, 4, rows, cw), bf16),
            V((chunks, 2, rows, cw), bf16),
            V((chunks, 2, rows, cw), bf16),
            V((chunks, rows, cw), bf16),
            V((chunks, rows, cw), bf16),
            V((5,) + small.shape, f32),
            V((5,) + small.shape, f32),
            dma((chunks, 8)),
            dma((chunks, 8)),
            dma((given, 2)),
            dma((5,)),
            dma((5,)),
            dma((chunks,)),
            dma((chunks,)),
            dma,
        ],
        compiler_params=pltpu.CompilerParams(
            collective_id=cid, has_side_effects=True, vmem_limit_bytes=62 * 2**20
        ),
        cost_estimate=pl.CostEstimate(
            flops=0, bytes_accessed=32 * rows * cols * 20, transcendentals=0
        ),
    )(*flat, *lefts, *rights, *ahead, seq_rows, small)


ERFC_SLOPE = 0.44
ERFC_COEFS = (
    0.12411048270139104,
    0.12443557227306976,
    0.1086564621750582,
    0.10790840846971936,
    -0.01009671066483208,
    0.1483525285505606,
    -0.13897999621011298,
    0.03561334337852199,
)


def gelu_and_slope(u):
    a = jnp.abs(u) * 0.7071067811865476
    t = 1.0 / (1.0 + ERFC_SLOPE * a)
    q = jnp.full_like(t, ERFC_COEFS[-1])
    for c in ERFC_COEFS[-2::-1]:
        q = q * t + c
    e = jnp.exp(-(a * a))
    tail = e * (t * q)
    phi = jnp.where(u < 0, tail, 1.0 - tail)
    return u * phi, phi + u * (e * 0.3989422804014327)


def up_kernel(x_ref, w_ref, b_ref, act_ref, slope_ref):
    for i in range(8):
        rows = slice(128 * i, 128 * (i + 1))
        u = lax.dot_general(x_ref[rows, :], w_ref[0], NN, preferred_element_type=f32) + b_ref[...]
        g, d = gelu_and_slope(u)
        act_ref[rows, :] = g.astype(bf16)
        slope_ref[rows, :] = d.astype(bf16)


def hidden_units(x, w, bias, tile):
    rows, width = x.shape
    units = w.shape[2] // 2
    per = units // tile
    col = pl.BlockSpec((rows, tile), lambda j: (0, j))
    return pl.pallas_call(
        up_kernel,
        grid=(2 * per,),
        in_specs=[
            pl.BlockSpec((rows, width), lambda j: (0, 0)),
            pl.BlockSpec((1, width, tile), lambda j: (j // per, 0, j % per)),
            pl.BlockSpec((1, tile), lambda j: (0, j)),
        ],
        out_specs=[col, col],
        out_shape=[jax.ShapeDtypeStruct((rows, 2 * units), bf16)] * 2,
        compiler_params=pltpu.CompilerParams(vmem_limit_bytes=56 * 2**20),
    )(x, w, bias)


def units_back_kernel(e_ref, w_ref, slope_ref, du_ref, sum_ref):
    total = 0.0
    for i in range(4):
        rows = slice(256 * i, 256 * (i + 1))
        d = lax.dot_general(e_ref[rows, :], w_ref[0], NN, preferred_element_type=f32)
        du = (d * slope_ref[rows, :].astype(f32)).astype(bf16)
        du_ref[rows, :] = du
        total = total + jnp.sum(du.astype(f32), 0, keepdims=True)
    sum_ref[...] = total


def hidden_units_back(e, w, slope, tile):
    rows, width = e.shape
    units = w.shape[2] // 2
    per = units // tile
    col = pl.BlockSpec((rows, tile), lambda j: (0, j))
    return pl.pallas_call(
        units_back_kernel,
        grid=(2 * per,),
        in_specs=[
            pl.BlockSpec((rows, width), lambda j: (0, 0)),
            pl.BlockSpec((1, width, tile), lambda j: (j // per, 0, per + j % per)),
            col,
        ],
        out_specs=[col, pl.BlockSpec((1, tile), lambda j: (0, j))],
        out_shape=[
            jax.ShapeDtypeStruct((rows, 2 * units), bf16),
            jax.ShapeDtypeStruct((1, 2 * units), f32),
        ],
        compiler_params=pltpu.CompilerParams(vmem_limit_bytes=56 * 2**20),
    )(e, w, slope)


def down_kernel(act_ref, w_ref, h_ref, cot_ref, vec_ref, mixed_ref, dr_ref, e_ref, sum_ref):
    units = w_ref.shape[2]
    r = h_ref[...] + vec_ref[0:1]
    for t in range(2):
        part = act_ref[:, t * units : (t + 1) * units]
        r = r + lax.dot_general(part, w_ref[t], NT, preferred_element_type=f32)
    gain = vec_ref[1:2]
    h, n, inv = norm_rows(r, gain, vec_ref[2:3])
    mixed_ref[...] = h.astype(bf16)
    rows_back(cot_ref[...].astype(f32), n, inv, gain, dr_ref, e_ref, sum_ref)


def rows_back(e, n, inv, gain, dr_ref, e_ref, sum_ref):
    dr, gg, gs, gb = norm_rows_back(e, n, inv, gain)
    dr_ref[...] = dr
    e_ref[...] = dr.astype(bf16)

    @pl.when(pl.program_id(0) == 0)
    def _():
        sum_ref[...] = jnp.zeros_like(sum_ref)

    sum_ref[0:3] += jnp.concatenate([gg[None], gs[None], gb[None]], 0)


def down_and_norms(act, w, h, cot, vecs, block):
    rows, width = h.shape
    units = w.shape[2] // 2
    row = pl.BlockSpec((block, width), lambda i: (i, 0))
    top = pl.BlockSpec((8, width), lambda i: (0, 0))
    return pl.pallas_call(
        down_kernel,
        grid=(rows // block,),
        in_specs=[
            pl.BlockSpec((block, 2 * units), lambda i: (i, 0)),
            pl.BlockSpec((2, width, units), lambda i: (0, 0, 1), pipeline_mode=pl.Buffered(1)),
            row,
            row,
            top,
        ],
        out_specs=[row, row, row, top],
        out_shape=[
            jax.ShapeDtypeStruct((rows, width), bf16),
            jax.ShapeDtypeStruct((rows, width), f32),
            jax.ShapeDtypeStruct((rows, width), bf16),
            jax.ShapeDtypeStruct((8, width), f32),
        ],
        compiler_params=pltpu.CompilerParams(vmem_limit_bytes=56 * 2**20),
    )(act, w, h, cot, vecs)


def up_back_kernel(du_ref, w_ref, dr3_ref, n_ref, inv_ref, vec_ref, dr_ref, e_ref, sum_ref):
    units = w_ref.shape[2]
    e = dr3_ref[...]
    for t in range(2):
        part = du_ref[:, t * units : (t + 1) * units]
        e = e + lax.dot_general(part, w_ref[t], NT, preferred_element_type=f32)
    rows_back(e, n_ref[...], inv_ref[...], vec_ref[0:1], dr_ref, e_ref, sum_ref)


def up_back_and_norm(du, w, dr3, n, inv, vecs, block):
    rows, width = dr3.shape
    units = w.shape[2] // 2
    row = pl.BlockSpec((block, width), lambda i: (i, 0))
    top = pl.BlockSpec((8, width), lambda i: (0, 0))
    return pl.pallas_call(
        up_back_kernel,
        grid=(rows // block,),
        in_specs=[
            pl.BlockSpec((block, 2 * units), lambda i: (i, 0)),
            pl.BlockSpec((2, width, units), lambda i: (0, 0, 0), pipeline_mode=pl.Buffered(1)),
            row,
            row,
            pl.BlockSpec((block, 1), lambda i: (i, 0)),
            top,
        ],
        out_specs=[row, row, top],
        out_shape=[
            jax.ShapeDtypeStruct((rows, width), f32),
            jax.ShapeDtypeStruct((rows, width), bf16),
            jax.ShapeDtypeStruct((8, width), f32),
        ],
        compiler_params=pltpu.CompilerParams(vmem_limit_bytes=56 * 2**20),
    )(du, w, dr3, n, inv, vecs)


def products_kernel(*refs, count, based):
    total = refs[2 * count][...] if based else 0.0
    for i in range(count):
        total = total + lax.dot_general(
            refs[i][...], refs[count + i][0], NT, preferred_element_type=f32
        )
    refs[-1][...] = total.astype(refs[-1].dtype)


def sum_of_products(lefts, w, places, base, block):
    rows, cols = lefts[0].shape
    width = w.shape[1]
    row = pl.BlockSpec((block, width), lambda i: (i, 0))
    left = pl.BlockSpec((block, cols), lambda i: (i, 0))

    def weight(t, j):
        return pl.BlockSpec((1, width, cols), lambda i: (t, 0, j), pipeline_mode=pl.Buffered(1))

    based = [] if base is None else [base]
    return pl.pallas_call(
        functools.partial(products_kernel, count=len(lefts), based=len(based)),
        grid=(rows // block,),
        in_specs=[left] * len(lefts) + [weight(t, j) for t, j in places] + [row] * len(based),
        out_specs=row,
        out_shape=jax.ShapeDtypeStruct((rows, width), bf16),
        compiler_params=pltpu.CompilerParams(vmem_limit_bytes=40 * 2**20),
    )(*lefts, *([w] * len(lefts)), *based)


def weight_grads_kernel(a_ref,b_ref,da_ref,db_ref,out_ref,at,bt,*,tiles):
    j=pl.program_id(0)
    @pl.when(j==0)
    def _():
        at[...]=a_ref[...].T
        bt[...]=b_ref[...].T
    kind=(j//tiles)%2
    @pl.when(kind==0)
    def _():
        out_ref[0]=lax.dot_general(at[...],da_ref[...],NN,preferred_element_type=f32).astype(bf16)
    @pl.when(kind==1)
    def _():
        out_ref[0]=lax.dot_general(bt[...],db_ref[...],NN,preferred_element_type=f32).astype(bf16)

def weight_grads(a,b,da,db,tile=512):
    rows,width=a.shape; half=da.shape[1]//2; tiles=half//tile
    whole=pl.BlockSpec((rows,width),lambda j:(0,0))
    t=lambda j: j//(2*tiles)
    kind=lambda j:(j//tiles)%2
    i=lambda j: j%tiles
    return pl.pallas_call(
        functools.partial(weight_grads_kernel,tiles=tiles),
        grid=(4*tiles,),
        in_specs=[whole,whole,
          pl.BlockSpec((rows,tile),lambda j:(0,t(j)*tiles+jnp.where(kind(j)==0,i(j),tiles-1))),
          pl.BlockSpec((rows,tile),lambda j:(0,t(j)*tiles+jnp.where(kind(j)==1,i(j),0)))],
        out_specs=pl.BlockSpec((1,width,tile),lambda j:(t(j),0,kind(j)*tiles+i(j))),
        out_shape=jax.ShapeDtypeStruct((2,width,2*half),bf16),
        scratch_shapes=[pltpu.VMEM((width,rows),bf16)]*2,
        compiler_params=pltpu.CompilerParams(vmem_limit_bytes=56*2**20),
    )(a,b,da,db)


def nn(a, b):
    return lax.dot_general(a, b, NN, preferred_element_type=f32)


def nt(a, b):
    return lax.dot_general(a, b, NT, preferred_element_type=f32)


def tn(a, b):
    return lax.dot_general(a, b, (((0,), (0,)), ((), ())), preferred_element_type=f32)


def norm_rows(r, gain, shift):
    center = r - jnp.mean(r, -1, keepdims=True)
    inv = lax.rsqrt(jnp.mean(center * center, -1, keepdims=True) + NORM_EPS)
    n = center * inv
    return n * gain + shift, n, inv


def norm_rows_back(e, n, inv, gain):
    eg = e * gain
    grad = inv * (eg - jnp.mean(eg, -1, keepdims=True) - n * jnp.mean(eg * n, -1, keepdims=True))
    return grad, jnp.sum(e * n, 0), jnp.sum(e, 0), jnp.sum(grad, 0)


def trade(x):
    return lax.ppermute(x, "tp", [(0, 1), (1, 0)])


def in_order(place, own, other, axis=0):
    return jnp.where(
        place == 0,
        jnp.concatenate([own, other], axis),
        jnp.concatenate([other, own], axis),
    )


def own_sequence(piece, place):
    own = lax.dynamic_index_in_dim(piece, place, 0, keepdims=False)
    away = lax.dynamic_index_in_dim(piece, 1 - place, 0, keepdims=False)
    return in_order(place, own, trade(away))


def to_pieces(rows, place):
    half = rows.shape[0] // 2
    halves = rows.reshape(2, half, rows.shape[1])
    own = lax.dynamic_index_in_dim(halves, place, 0, keepdims=True)
    away = lax.dynamic_index_in_dim(halves, 1 - place, 0, keepdims=True)
    return in_order(place, own, trade(away))


def whole_sequences(
    layer_in,
    memory,
    out_grad,
    w_self_in,
    w_self_out,
    w_cross_in,
    w_cross_out,
    w_up,
    w_down,
    head_bias,
    up_bias,
    norm_gain,
    row_bias,
):
    place = lax.axis_index("tp")
    width = layer_in.shape[2]
    cols = w_self_in.shape[2]
    units = w_up.shape[1]
    shard = w_self_in.shape[0]
    gains = norm_gain.astype(f32)
    shifts = row_bias.astype(f32)

    def gather(*parts):
        mine = jnp.concatenate(parts, 1)
        both = lax.all_gather(mine, ("tp", "fsdp"), axis=0, tiled=True)
        return both.reshape(2, width, mine.shape[1])

    small = jnp.concatenate([head_bias.reshape(-1), up_bias])
    small = in_order(place, small[None], trade(small)[None])
    hb = small[:, : 4 * cols].reshape(2, 4, cols).astype(f32)
    ub = small[:, 4 * cols :].astype(f32)

    c3, c4 = 3 * cols, 4 * cols
    g_att, (x, mem) = gather_weights(
        jnp.concatenate(
            [
                w_self_in.reshape(shard, c3),
                w_self_out.T,
                w_cross_in.reshape(shard, c3),
                w_cross_out.T,
            ],
            1,
        ),
        (layer_in, memory),
        1,
        16,
    )
    g_att, w_up, w_down = lax.optimization_barrier((g_att, w_up, w_down))
    g_self, g_cross = g_att[:, :, :c4], g_att[:, :, c4:]
    g_ffn = gather(w_up, w_down.T)
    g_ffn, out_grad = lax.optimization_barrier((g_ffn, out_grad))
    cot = own_sequence(out_grad, place)
    xf = x.astype(f32)
    halves = (0, 1)
    zero = jnp.zeros((cols,), f32)
    scale3 = jnp.concatenate([zero + ATT_SCALE * LOG2E, zero + 1.0, zero + 1.0])
    blk = cols // 128

    sy, sa, sl = [], [], []
    for t in halves:
        bias = jnp.concatenate([hb[t, 0], zero, hb[t, 1]])
        y = ((nn(x, g_self[t, :, :c3]) + bias) * scale3).astype(bf16)
        o, lse = att_fwd(y, y, y, True, 512, 0, blk, 2 * blk, cols)
        sy.append(y)
        sa.append(o)
        sl.append(lse)
    r1 = xf + (nt(sa[0], g_self[0, :, c3:]) + nt(sa[1], g_self[1, :, c3:])) + shifts[0]
    h1, n1, i1 = norm_rows(r1, gains[0], shifts[3])
    h1b = h1.astype(bf16)

    cq, ckv, ca, cl = [], [], [], []
    for t in halves:
        kv = (nn(mem, g_cross[t, :, cols:c3]) + jnp.concatenate([zero, hb[t, 3]])).astype(bf16)
        q = ((nn(h1b, g_cross[t, :, :cols]) + hb[t, 2]) * (ATT_SCALE * LOG2E)).astype(bf16)
        o, lse = att_fwd(q, kv, kv, False, 512, 0, 0, blk, cols)
        cq.append(q)
        ckv.append(kv)
        ca.append(o)
        cl.append(lse)
    r2 = h1 + (nt(ca[0], g_cross[0, :, c3:]) + nt(ca[1], g_cross[1, :, c3:])) + shifts[1]
    h2, n2, i2 = norm_rows(r2, gains[1], shifts[4])
    h2b = h2.astype(bf16)

    act, slope = hidden_units(h2b, g_ffn, ub.reshape(1, 2 * units), 512)
    none = jnp.zeros((5, width), f32)
    mixed_rows, dr3, e3, sums3 = down_and_norms(
        act,
        g_ffn,
        h2,
        cot,
        jnp.concatenate([shifts[2:3], gains[2:3], shifts[5:6], none], 0),
        256,
    )
    gg3, gs3, gb3 = sums3[0], sums3[1], sums3[2]
    mixed = to_pieces(mixed_rows, place)

    du, gu = hidden_units_back(e3, g_ffn, slope, 1024)
    grad_ffn = weight_grads(h2b, e3, du, act, 1024)
    grad_ffn, du = lax.optimization_barrier((grad_ffn, du))
    s_ffn = lax.psum_scatter(
        grad_ffn.reshape(2 * width, 2 * units), ("tp", "fsdp"), scatter_dimension=0, tiled=True
    ).astype(f32)
    dr2, e2, sums2 = up_back_and_norm(
        du,
        g_ffn,
        dr3,
        n2,
        i2,
        jnp.concatenate([gains[1:2], none, none[:2]], 0),
        256,
    )
    gg2, gs2, gb2 = sums2[0], sums2[1], sums2[2]

    dcq, dck, dcv = [], [], []
    for t in halves:
        da = nn(e2, g_cross[t, :, c3:]).astype(bf16)
        a, b, c = att_bwd(cq[t], ckv[t], ckv[t], ca[t], da, cl[t], False, 256, 0, 0, blk)
        dcq.append(a)
        dck.append(b)
        dcv.append(c)
    low = lambda v: v.astype(bf16)
    grads = [
        tuple(low(tn(h1b, dcq[t])) for t in halves),
        tuple(low(tn(mem, dck[t])) for t in halves),
        tuple(low(tn(mem, dcv[t])) for t in halves),
        tuple(low(tn(e2, ca[t])) for t in halves),
    ]
    dmem = sum_of_products(
        dck + dcv, g_att, [(t, j) for j in (5, 6) for t in halves], None, 256
    )
    d_memory = to_pieces(dmem, place)
    dh1 = dr2 + (nt(dcq[0], g_cross[0, :, :cols]) + nt(dcq[1], g_cross[1, :, :cols]))
    dr1, gg1, gs1, gb1 = norm_rows_back(dh1, n1, i1, gains[0])
    e1 = dr1.astype(bf16)

    dsq, dsk, dsv = [], [], []
    for t in halves:
        da = nn(e1, g_self[t, :, c3:]).astype(bf16)
        y = sy[t]
        ahead = (mixed, dmem) if t == 0 else ()
        a, b, c = att_bwd(y, y, y, sa[t], da, sl[t], True, 256, 0, blk, 2 * blk, ahead)
        dsq.append(a)
        dsk.append(b)
        dsv.append(c)
    dx = sum_of_products(
        dsq + dsk + dsv, g_att, [(t, j) for j in range(3) for t in halves], dr1, 256
    )

    def col_sums(pair):
        return jnp.stack([jnp.sum(p.astype(f32), 0) for p in pair])

    gh = jnp.stack([col_sums(dsq), col_sums(dsv), col_sums(dcq), col_sums(dcv)], 1)
    flat = jnp.concatenate(
        [
            v.reshape(-1)
            for v in (gh, gu, gg1, gg2, gg3, gb1, gb2, gb3, gs1, gs2, gs3)
        ]
    )
    made = [dsq[0], dsq[1], dsk[0], dsk[1], dsv[0], dsv[1], sa[0], sa[1]]
    s_att, flat, d_layer_in = scatter_grads(
        grads, (x, e1), made, (d_memory,), dx, flat.reshape(-1, 128), 2
    )
    flat = flat.reshape(-1)
    head_sum = lax.dynamic_index_in_dim(flat[: 8 * cols].reshape(2, 4, cols), place, 0, False)
    unit_sum = lax.dynamic_index_in_dim(
        flat[8 * cols : 8 * cols + 2 * units].reshape(2, units), place, 0, False
    )
    rest = flat[8 * cols + 2 * units :].reshape(9, width)

    cross_part, self_part = s_att[:, : 4 * cols], s_att[:, 4 * cols :]
    return (
        mixed,
        d_layer_in,
        d_memory,
        self_part[:, :c3].reshape(shard, 3, cols),
        self_part[:, c3:].T,
        cross_part[:, :c3].reshape(shard, 3, cols),
        cross_part[:, c3:].T,
        s_ffn[:, :units],
        s_ffn[:, units:].T,
        head_sum,
        unit_sum,
        rest[:3],
        rest[3:],
    )


def on_device(layer_in, *rest):
    paired = lax.axis_size("tp") == 2 and layer_in.shape[0] == 2
    if paired and lax.axis_size("fsdp") == 16:
        return whole_sequences(layer_in, *rest)
    return shared_sequences(layer_in, *rest)


def solution(mesh):
    return jax.shard_map(
        on_device,
        mesh=mesh,
        in_specs=(
            P("fsdp", "tp", None),
            P("fsdp", "tp", None),
            P("fsdp", "tp", None),
            P("fsdp", None, "tp"),
            P("tp", "fsdp"),
            P("fsdp", None, "tp"),
            P("tp", "fsdp"),
            P("fsdp", "tp"),
            P("tp", "fsdp"),
            P(None, "tp"),
            P("tp"),
            P(),
            P(),
        ),
        out_specs=(
            P("fsdp", "tp", None),
            P("fsdp", "tp", None),
            P("fsdp", "tp", None),
            P("fsdp", None, "tp"),
            P("tp", "fsdp"),
            P("fsdp", None, "tp"),
            P("tp", "fsdp"),
            P("fsdp", "tp"),
            P("tp", "fsdp"),
            P(None, "tp"),
            P("tp"),
            P(),
            P(),
        ),
        check_vma=False,
    )
```

```python
import functools

import jax
import jax.numpy as jnp
from jax import lax
from jax.experimental import pallas as pl
from jax.experimental.pallas import tpu as pltpu
from jax.sharding import PartitionSpec as P

HD = 64
NORM_EPS = 1e-05
ATT_SCALE = 0.125


def times_back(left, right):
    return lax.dot_general(
        left, right, (((1,), (1,)), ((), ())), preferred_element_type=jnp.float32
    )


def over_rows(left, right):
    return lax.dot_general(
        left, right, (((0,), (0,)), ((), ())), preferred_element_type=jnp.float32
    )


def whole_rows(piece):
    return lax.all_gather(piece, "tp", axis=1, tiled=True)


def whole_grads(piece):
    return lax.all_gather(piece, "tp", axis=1, tiled=True)


def branch_sum(term):
    return lax.psum_scatter(
        term.astype(jnp.bfloat16), "tp", scatter_dimension=1, tiled=True
    ).astype(jnp.float32)


def piece_sum(term):
    return lax.psum_scatter(
        term.astype(jnp.bfloat16), "tp", scatter_dimension=1, tiled=True
    ).astype(jnp.float32)


def norm_forward(resid, gain, shift):
    center = resid - jnp.mean(resid, -1, keepdims=True)
    spread = jnp.mean(center * center, -1, keepdims=True)
    inv_std = lax.rsqrt(spread + NORM_EPS)
    normed = center * inv_std
    return (normed * gain + shift, normed, inv_std)


def norm_backward(grad_out, normed, inv_std, gain):
    grad_normed = grad_out * gain
    grad_resid = inv_std * (
        grad_normed
        - jnp.mean(grad_normed, -1, keepdims=True)
        - normed * jnp.mean(grad_normed * normed, -1, keepdims=True)
    )
    return (grad_resid, jnp.sum(grad_out * normed, (0, 1)), jnp.sum(grad_out, (0, 1)))


def gelu_exact(pre_act):
    return jax.nn.gelu(pre_act, approximate=False)


def gelu_back(pre_act, grad_act):
    unused_out, pull_back = jax.vjp(gelu_exact, pre_act)
    return pull_back(grad_act)[0]


def masked_scores(query_blk, block_start, keys_seq, causal):
    scores = jnp.einsum("qhc,khc->hqk", query_blk, keys_seq, preferred_element_type=jnp.float32)
    if causal:
        row_pos = block_start + lax.broadcasted_iota(jnp.int32, scores.shape[1:], 0)
        col_pos = lax.broadcasted_iota(jnp.int32, scores.shape[1:], 1)
        scores = jnp.where(row_pos >= col_pos, scores, -1e30)
    return scores


def attend_forward(query, keys, values, causal):
    seq_count, length, heads_dev, depth = query.shape
    block_rows = min(512, length)
    block_count = length // block_rows
    block_starts = jnp.arange(block_count, dtype=jnp.int32) * block_rows

    def one_sequence(seq_item):
        query_seq, keys_seq, values_seq = seq_item

        def one_block(blk_item):
            query_blk, block_start = blk_item
            scores = masked_scores(query_blk, block_start, keys_seq, causal)
            row_max = jnp.max(scores, -1, keepdims=True)
            log_total = row_max + jnp.log(jnp.sum(jnp.exp(scores - row_max), -1, keepdims=True))
            probs = jnp.exp(scores - log_total).astype(jnp.bfloat16)
            block_out = jnp.einsum(
                "hqk,khc->qhc", probs, values_seq, preferred_element_type=jnp.float32
            )
            return (block_out.astype(jnp.bfloat16), log_total)

        block_outs, log_totals = lax.map(
            one_block, (query_seq.reshape(block_count, block_rows, heads_dev, depth), block_starts)
        )
        return (block_outs.reshape(length, heads_dev, depth), log_totals)

    return lax.map(one_sequence, (query, keys, values))


def attend_backward(query, keys, values, log_totals, grad_out, causal):
    seq_count, length, heads_dev, depth = query.shape
    block_rows = min(512, length)
    block_count = length // block_rows
    block_starts = jnp.arange(block_count, dtype=jnp.int32) * block_rows

    def one_sequence(seq_item):
        query_seq, keys_seq, values_seq, total_seq, grad_seq = seq_item

        def one_block(carry, blk_item):
            query_blk, grad_blk, total_blk, block_start = blk_item
            probs = jnp.exp(masked_scores(query_blk, block_start, keys_seq, causal) - total_blk)
            grad_probs = jnp.einsum(
                "qhc,khc->hqk", grad_blk, values_seq, preferred_element_type=jnp.float32
            )
            row_delta = jnp.sum(probs * grad_probs, -1, keepdims=True)
            grad_scores = (probs * (grad_probs - row_delta)).astype(jnp.bfloat16)
            grad_query = jnp.einsum(
                "hqk,khc->qhc", grad_scores, keys_seq, preferred_element_type=jnp.float32
            )
            grad_keys = carry[0] + jnp.einsum(
                "hqk,qhc->khc", grad_scores, query_blk, preferred_element_type=jnp.float32
            )
            grad_values = carry[1] + jnp.einsum(
                "hqk,qhc->khc",
                probs.astype(jnp.bfloat16),
                grad_blk,
                preferred_element_type=jnp.float32,
            )
            return ((grad_keys, grad_values), grad_query)

        zero_keys = jnp.zeros(keys_seq.shape, jnp.float32)
        blk_items = (
            query_seq.reshape(block_count, block_rows, heads_dev, depth),
            grad_seq.reshape(block_count, block_rows, heads_dev, depth),
            total_seq,
            block_starts,
        )
        (grad_keys, grad_values), grad_query = lax.scan(
            one_block, (zero_keys, zero_keys), blk_items
        )
        return (grad_query.reshape(length, heads_dev, depth), grad_keys, grad_values)

    return lax.map(one_sequence, (query, keys, values, log_totals, grad_out))


def shared_sequences(
    layer_in,
    memory,
    out_grad,
    w_self_in,
    w_self_out,
    w_cross_in,
    w_cross_out,
    w_up,
    w_down,
    head_bias,
    up_bias,
    norm_gain,
    row_bias,
):
    seq_count, piece_len, model_width = layer_in.shape
    head_cols = w_self_in.shape[2]
    unit_cols = w_up.shape[1]
    heads_dev = head_cols // HD
    tp_place = lax.axis_index("tp")
    tp_count = lax.axis_size("tp")
    zero_index = jnp.zeros((), jnp.int32)
    gains = norm_gain.astype(jnp.float32)
    shifts = row_bias.astype(jnp.float32)
    col_bias = head_bias.astype(jnp.float32)
    unit_bias = up_bias.astype(jnp.float32)
    self_in, self_out, cross_in, cross_out, up_full, down_full = (
        lax.all_gather(w_self_in, "fsdp", axis=0, tiled=True),
        lax.all_gather(w_self_out, "fsdp", axis=1, tiled=True),
        lax.all_gather(w_cross_in, "fsdp", axis=0, tiled=True),
        lax.all_gather(w_cross_out, "fsdp", axis=1, tiled=True),
        lax.all_gather(w_up, "fsdp", axis=0, tiled=True),
        lax.all_gather(w_down, "fsdp", axis=1, tiled=True),
    )
    layer_whole = whole_rows(layer_in)
    length = layer_whole.shape[1]
    row_count = seq_count * length
    token_rows = layer_whole.reshape(row_count, model_width)
    self_proj = jnp.einsum("rd,dkc->rkc", token_rows, self_in, preferred_element_type=jnp.float32)
    self_query = ((self_proj[:, 0] + col_bias[0]) * ATT_SCALE).astype(jnp.bfloat16)
    self_keys = self_proj[:, 1].astype(jnp.bfloat16)
    self_values = (self_proj[:, 2] + col_bias[1]).astype(jnp.bfloat16)
    head_shape = (seq_count, length, heads_dev, HD)
    self_att, self_totals = attend_forward(
        self_query.reshape(head_shape),
        self_keys.reshape(head_shape),
        self_values.reshape(head_shape),
        True,
    )
    self_rows = self_att.reshape(row_count, head_cols)
    self_term = jnp.dot(self_rows, self_out, preferred_element_type=jnp.float32).reshape(
        seq_count, length, model_width
    )
    resid_one = layer_in.astype(jnp.float32) + branch_sum(self_term) + shifts[0]
    normed_one, unit_one, inv_one = norm_forward(resid_one, gains[0], shifts[3])
    normed_rows = whole_rows(normed_one.astype(jnp.bfloat16)).reshape(row_count, model_width)
    cross_query = (
        (jnp.dot(normed_rows, cross_in[:, 0], preferred_element_type=jnp.float32) + col_bias[2])
        * ATT_SCALE
    ).astype(jnp.bfloat16)
    memory_whole = lax.all_gather(memory, "tp", axis=1, tiled=True)
    source_len = memory_whole.shape[1]
    source_rows = memory_whole.reshape(seq_count * source_len, model_width)
    cross_proj = jnp.einsum(
        "rd,dkc->rkc", source_rows, cross_in[:, 1:], preferred_element_type=jnp.float32
    )
    cross_keys = cross_proj[:, 0].astype(jnp.bfloat16)
    cross_values = (cross_proj[:, 1] + col_bias[3]).astype(jnp.bfloat16)
    source_shape = (seq_count, source_len, heads_dev, HD)
    cross_att, cross_totals = attend_forward(
        cross_query.reshape(head_shape),
        cross_keys.reshape(source_shape),
        cross_values.reshape(source_shape),
        False,
    )
    cross_rows = cross_att.reshape(row_count, head_cols)
    cross_term = jnp.dot(cross_rows, cross_out, preferred_element_type=jnp.float32).reshape(
        seq_count, length, model_width
    )
    resid_two = normed_one + branch_sum(cross_term) + shifts[1]
    normed_two, unit_two, inv_two = norm_forward(resid_two, gains[1], shifts[4])
    normed_two_low = normed_two.astype(jnp.bfloat16)
    ffn_rows = whole_rows(normed_two_low).reshape(row_count, model_width)
    pre_act = jnp.dot(ffn_rows, up_full, preferred_element_type=jnp.float32) + unit_bias
    hidden_act = gelu_exact(pre_act).astype(jnp.bfloat16)
    ffn_term = jnp.dot(hidden_act, down_full, preferred_element_type=jnp.float32).reshape(
        seq_count, length, model_width
    )
    ffn_out = branch_sum(ffn_term)
    resid_three = normed_two + ffn_out + shifts[2]
    mixed, unit_three, inv_three = norm_forward(resid_three, gains[2], shifts[5])
    grad_three, gain_grad_three, shift_grad_three = norm_backward(
        out_grad.astype(jnp.float32), unit_three, inv_three, gains[2]
    )
    bias_grad_three = jnp.sum(grad_three, (0, 1))
    grad_three_low = grad_three.astype(jnp.bfloat16)
    grad_rows = whole_grads(grad_three_low).reshape(row_count, model_width)
    grad_act = times_back(grad_rows, down_full)
    grad_pre = gelu_back(pre_act, grad_act).astype(jnp.bfloat16)
    d_up = over_rows(ffn_rows, grad_pre)
    d_down = over_rows(hidden_act, grad_rows)
    unit_grad = jnp.sum(grad_pre, 0, dtype=jnp.float32)
    grad_two_in = piece_sum(times_back(grad_pre, up_full).reshape(seq_count, length, model_width))
    grad_normed_two = grad_three + grad_two_in
    grad_two, gain_grad_two, shift_grad_two = norm_backward(
        grad_normed_two, unit_two, inv_two, gains[1]
    )
    bias_grad_two = jnp.sum(grad_two, (0, 1))
    grad_two_rows = whole_grads(grad_two.astype(jnp.bfloat16)).reshape(row_count, model_width)
    d_cross_out = over_rows(cross_rows, grad_two_rows)
    grad_cross_att = times_back(grad_two_rows, cross_out).astype(jnp.bfloat16)
    cq_grad, ck_grad, cv_grad = attend_backward(
        cross_query.reshape(head_shape),
        cross_keys.reshape(source_shape),
        cross_values.reshape(source_shape),
        cross_totals,
        grad_cross_att.reshape(head_shape),
        False,
    )
    cq_pre = cq_grad.reshape(row_count, head_cols).astype(jnp.bfloat16) * jnp.asarray(
        ATT_SCALE, jnp.bfloat16
    )
    ckv_low = jnp.stack(
        [
            ck_grad.reshape(seq_count * source_len, head_cols),
            cv_grad.reshape(seq_count * source_len, head_cols),
        ],
        1,
    ).astype(jnp.bfloat16)
    cross_q_grad = over_rows(normed_rows, cq_pre)
    cq_bias_grad = jnp.sum(cq_pre, 0, dtype=jnp.float32)
    normed_part = times_back(cq_pre, cross_in[:, 0]).reshape(seq_count, length, model_width)
    source_part = jnp.einsum(
        "rkc,dkc->rd", ckv_low, cross_in[:, 1:], preferred_element_type=jnp.float32
    ).reshape(seq_count, source_len, model_width)
    grad_one_in, memory_grad = (
        lax.psum_scatter(
            normed_part.astype(jnp.bfloat16), "tp", scatter_dimension=1, tiled=True
        ).astype(jnp.float32),
        lax.psum_scatter(
            source_part.astype(jnp.bfloat16), "tp", scatter_dimension=1, tiled=True
        ).astype(jnp.float32),
    )
    d_memory = memory_grad.astype(jnp.bfloat16)
    cross_kv_grad = jnp.einsum(
        "rd,rkc->dkc", source_rows, ckv_low, preferred_element_type=jnp.float32
    )
    cross_grad_term = jnp.concatenate([cross_q_grad[:, None, :], cross_kv_grad], 1)
    cv_own = jnp.sum(ckv_low[:, 1], 0, dtype=jnp.float32)
    cv_wide = lax.dynamic_update_slice(
        jnp.zeros((head_cols * tp_count,), jnp.float32), cv_own, (tp_place * head_cols,)
    )
    grad_normed_one = grad_two + grad_one_in
    grad_one, gain_grad_one, shift_grad_one = norm_backward(
        grad_normed_one, unit_one, inv_one, gains[0]
    )
    bias_grad_one = jnp.sum(grad_one, (0, 1))
    grad_one_rows = whole_grads(grad_one.astype(jnp.bfloat16)).reshape(row_count, model_width)
    d_self_out = over_rows(self_rows, grad_one_rows)
    grad_self_att = times_back(grad_one_rows, self_out).astype(jnp.bfloat16)
    sq_grad, sk_grad, sv_grad = attend_backward(
        self_query.reshape(head_shape),
        self_keys.reshape(head_shape),
        self_values.reshape(head_shape),
        self_totals,
        grad_self_att.reshape(head_shape),
        True,
    )
    sq_pre = sq_grad.reshape(row_count, head_cols).astype(jnp.bfloat16) * jnp.asarray(
        ATT_SCALE, jnp.bfloat16
    )
    sqkv_low = jnp.stack(
        [
            sq_pre,
            sk_grad.reshape(row_count, head_cols).astype(jnp.bfloat16),
            sv_grad.reshape(row_count, head_cols).astype(jnp.bfloat16),
        ],
        1,
    )
    d_self_in = jnp.einsum("rd,rkc->dkc", token_rows, sqkv_low, preferred_element_type=jnp.float32)
    sq_bias_grad = jnp.sum(sq_pre, 0, dtype=jnp.float32)
    sv_bias_grad = jnp.sum(sqkv_low[:, 2], 0, dtype=jnp.float32)
    layer_part = jnp.einsum(
        "rkc,dkc->rd", sqkv_low, self_in, preferred_element_type=jnp.float32
    ).reshape(seq_count, length, model_width)
    d_layer_in = (grad_one + piece_sum(layer_part)).astype(jnp.bfloat16)
    slot_grad = jnp.stack([sq_bias_grad, sv_bias_grad, cq_bias_grad])
    slot_wide = lax.dynamic_update_slice(
        jnp.zeros((3, head_cols * tp_count), jnp.float32),
        slot_grad,
        (zero_index, tp_place * head_cols),
    )
    head_wide = jnp.concatenate([slot_wide, cv_wide[None, :]], 0)
    unit_wide_grad = lax.dynamic_update_slice(
        jnp.zeros((unit_cols * tp_count,), jnp.float32), unit_grad, (tp_place * unit_cols,)
    )
    gain_grads = jnp.stack([gain_grad_one, gain_grad_two, gain_grad_three])
    shift_grads = jnp.stack(
        [
            bias_grad_one,
            bias_grad_two,
            bias_grad_three,
            shift_grad_one,
            shift_grad_two,
            shift_grad_three,
        ]
    )
    gain_total, shift_total, head_total, unit_total = lax.psum(
        (gain_grads, shift_grads, head_wide, unit_wide_grad), ("fsdp", "tp")
    )
    d_head_bias = lax.dynamic_slice(head_total, (zero_index, tp_place * head_cols), (4, head_cols))
    d_up_bias = lax.dynamic_slice(unit_total, (tp_place * unit_cols,), (unit_cols,))
    g_self_in, g_self_out, g_cross_part, g_cross_out, g_up, g_down = (
        lax.psum_scatter(
            d_self_in.astype(jnp.bfloat16), "fsdp", scatter_dimension=0, tiled=True
        ).astype(jnp.float32),
        lax.psum_scatter(
            d_self_out.astype(jnp.bfloat16), "fsdp", scatter_dimension=1, tiled=True
        ).astype(jnp.float32),
        lax.psum_scatter(
            cross_grad_term.astype(jnp.bfloat16), "fsdp", scatter_dimension=0, tiled=True
        ).astype(jnp.float32),
        lax.psum_scatter(
            d_cross_out.astype(jnp.bfloat16), "fsdp", scatter_dimension=1, tiled=True
        ).astype(jnp.float32),
        lax.psum_scatter(d_up.astype(jnp.bfloat16), "fsdp", scatter_dimension=0, tiled=True).astype(
            jnp.float32
        ),
        lax.psum_scatter(
            d_down.astype(jnp.bfloat16), "fsdp", scatter_dimension=1, tiled=True
        ).astype(jnp.float32),
    )
    return (
        mixed.astype(jnp.bfloat16),
        d_layer_in,
        d_memory,
        g_self_in,
        g_self_out,
        g_cross_part,
        g_cross_out,
        g_up,
        g_down,
        d_head_bias,
        d_up_bias,
        gain_total,
        shift_total,
    )


NT=(((1,),(1,)),((),()))
NN=(((1,),(0,)),((),()))
f32=jnp.float32
bf16=jnp.bfloat16

LN2 = 0.6931471805599453
LOG2E = 1.4426950408889634


def att_fwd_kernel(q_ref,k_ref,v_ref,o_ref,lse_ref,*,bq,causal):
    n=q_ref.shape[0]; nk=k_ref.shape[0]
    lane=lax.broadcasted_iota(jnp.int32,(nk,128),1)
    k=k_ref[...]
    zero=jnp.zeros((),bf16)
    kh=[jnp.where(lane<HD,k,zero),jnp.where(lane>=HD,k,zero)]
    vt=v_ref[...].T
    ones=jnp.ones((8,nk),bf16)
    vh=[jnp.concatenate([vt[h*HD:(h+1)*HD],ones],0) for h in range(2)]
    for i in range(n//bq):
        q=q_ref[i*bq:(i+1)*bq,:]
        L=(i+1)*bq if causal else nk
        S=[]
        for h in range(2):
            s=lax.dot_general(kh[h][:L],q,NT,preferred_element_type=f32)
            if causal:
                keep=lax.broadcasted_iota(jnp.int32,(bq,bq),0)<=lax.broadcasted_iota(jnp.int32,(bq,bq),1)
                sd=jnp.where(keep,s[L-bq:],-1e30)
                s=jnp.concatenate([s[:L-bq],sd],0) if L>bq else sd
            S.append(s)
        M=[jnp.max(s,0,keepdims=True) for s in S]
        outs=[];lses=[]
        for h in range(2):
            p=jnp.exp2(S[h]-M[h]).astype(bf16)
            ol=lax.dot_general(vh[h][:,:L],p,NN,preferred_element_type=f32)
            l=ol[HD:HD+1]
            outs.append(ol[:HD]*(1.0/l)); lses.append(M[h]+jnp.log2(l))
        o_ref[i*bq:(i+1)*bq,:]=jnp.concatenate(outs,0).T.astype(bf16)
        lse_ref[0,:,i*bq:(i+1)*bq]=jnp.concatenate(lses,0)

def att_fwd(q,k,v,causal,bq=256,qo=0,ko=0,vo=0,width=None):
    n=q.shape[0]; nk=k.shape[0]; width=width or q.shape[1]; np_=width//128
    spec=lambda rows,off: pl.BlockSpec((rows,128),lambda p: (0,p+off))
    return pl.pallas_call(
        functools.partial(att_fwd_kernel,bq=bq,causal=causal),
        grid=(np_,),
        in_specs=[spec(n,qo),spec(nk,ko),spec(nk,vo)],
        out_specs=[spec(n,0),pl.BlockSpec((1,2,n),lambda p:(p,0,0))],
        out_shape=[jax.ShapeDtypeStruct((n,width),bf16),jax.ShapeDtypeStruct((np_,2,n),f32)],
        compiler_params=pltpu.CompilerParams(dimension_semantics=("arbitrary",),vmem_limit_bytes=56*2**20),
    )(q,k,v)

def att_bwd_kernel(q_ref,k_ref,v_ref,o_ref,do_ref,lse_ref,*refs,bq,causal):
    dq_ref,dk_ref,dv_ref,sum_q_ref,sum_v_ref,dk_acc,dv_acc=refs[-7:]
    sum_q=0.0
    n=q_ref.shape[0]; nk=k_ref.shape[0]
    lane=lax.broadcasted_iota(jnp.int32,(nk,128),1)
    lq=lax.broadcasted_iota(jnp.int32,(bq,128),1)
    k=k_ref[...]; v=v_ref[...]
    zero=jnp.zeros((),bf16)
    kh=[jnp.where(lane<HD,k,zero),jnp.where(lane>=HD,k,zero)]
    vh=[jnp.where(lane<HD,v,zero),jnp.where(lane>=HD,v,zero)]
    kt=k.T
    dk_acc[...]=jnp.zeros_like(dk_acc); dv_acc[...]=jnp.zeros_like(dv_acc)
    for i in range(n//bq):
        rows=slice(i*bq,(i+1)*bq)
        q=q_ref[rows,:]; do=do_ref[rows,:]
        L=(i+1)*bq if causal else nk
        dot_=(do.astype(f32)*o_ref[rows,:].astype(f32)).T
        qm=[jnp.where(lq<HD,q,zero),jnp.where(lq>=HD,q,zero)]
        dm=[jnp.where(lq<HD,do,zero),jnp.where(lq>=HD,do,zero)]
        dqs=[]
        for h in range(2):
            s=lax.dot_general(kh[h][:L],q,NT,preferred_element_type=f32)
            dp=lax.dot_general(vh[h][:L],do,NT,preferred_element_type=f32)
            lse=lse_ref[0,h:h+1,rows]
            delta=jnp.sum(dot_[h*HD:(h+1)*HD],0,keepdims=True)
            if causal:
                keep=lax.broadcasted_iota(jnp.int32,(bq,bq),0)<=lax.broadcasted_iota(jnp.int32,(bq,bq),1)
                sd=jnp.where(keep,s[L-bq:],-1e30)
                s=jnp.concatenate([s[:L-bq],sd],0) if L>bq else sd
            p=jnp.exp2(s-lse)
            ds=(p*(dp-delta)).astype(bf16)
            pb=p.astype(bf16)
            dv_acc[:L,:]+=lax.dot_general(pb,dm[h],NN,preferred_element_type=f32)
            dk_acc[:L,:]+=lax.dot_general(ds,qm[h],NN,preferred_element_type=f32)
            dqs.append(lax.dot_general(kt[h*HD:(h+1)*HD,:L],ds,NN,preferred_element_type=f32))
        dq=(jnp.concatenate(dqs,0)*0.125).T.astype(bf16)
        dq_ref[rows,:]=dq
        sum_q=sum_q+jnp.sum(dq.astype(f32),0,keepdims=True)
    dk_ref[...]=(dk_acc[...]*LN2).astype(bf16)
    dv=dv_acc[...].astype(bf16)
    dv_ref[...]=dv
    sum_q_ref[...]=sum_q
    sum_v_ref[...]=jnp.sum(dv.astype(f32),0,keepdims=True)

def att_bwd(q,k,v,o,do,lse,causal,bq=256,qo=0,ko=0,vo=0,ahead=()):
    n=q.shape[0]; nk=k.shape[0]; width=o.shape[1]; np_=width//128
    spec=lambda rows,off: pl.BlockSpec((rows,128),lambda p: (0,p+off))
    return pl.pallas_call(
        functools.partial(att_bwd_kernel,bq=bq,causal=causal),
        grid=(np_,),
        in_specs=[spec(n,qo),spec(nk,ko),spec(nk,vo),spec(n,0),spec(n,0),pl.BlockSpec((1,2,n),lambda p:(p,0,0))]+[pl.BlockSpec(memory_space=pl.ANY)]*len(ahead),
        out_specs=[spec(n,0),spec(nk,0),spec(nk,0),spec(1,0),spec(1,0)],
        out_shape=[jax.ShapeDtypeStruct((n,width),bf16),jax.ShapeDtypeStruct((nk,width),bf16),jax.ShapeDtypeStruct((nk,width),bf16),jax.ShapeDtypeStruct((1,width),f32),jax.ShapeDtypeStruct((1,width),f32)],
        scratch_shapes=[pltpu.VMEM((nk,128),f32)]*2,
        compiler_params=pltpu.CompilerParams(dimension_semantics=("arbitrary",),vmem_limit_bytes=56*2**20),
    )(q,k,v,o,do,lse,*ahead)


MESH = pl.DeviceIdType.MESH
LINKS = ("z1", "z2", "y", "x", "c")


def partners():
    t = lax.axis_index("tp")
    f = lax.axis_index("fsdp")
    z, y, c = f // 4, (f // 2) % 2, f % 2

    def at(z_, y_, c_, t_):
        return (z_ * 4 + y_ * 2 + c_, t_)

    ids = dict(
        z1=at(z + 1 - 2 * (z % 2), y, c, t),
        z2=at((z + 2) % 4, y, c, t),
        y=at(z, 1 - y, c, t),
        x=at(z, y, c, 1 - t),
        c=at(z, y, 1 - c, t),
    )
    return (t, z, y, c), ids


def greet(ids):
    barrier = pltpu.get_barrier_semaphore()
    for name in LINKS:
        pl.semaphore_signal(barrier, inc=1, device_id=ids[name], device_id_type=MESH)
    pl.semaphore_wait(barrier, len(LINKS))


def pipeline(chunks, stages, begin, after_step=None):
    started = {}
    for step in range(chunks + stages):
        for s in range(stages + 1):
            k = step - s
            if 0 <= k < chunks:
                if s > 0:
                    for copy in started[k, s - 1]:
                        copy.wait_recv()
                started[k, s] = begin(k, s)
        if after_step is not None:
            after_step(step)
    for copies in started.values():
        for copy in copies:
            copy.wait_send()


def start_copy(src, dst, send, recv, to):
    copy = pltpu.make_async_remote_copy(
        src_ref=src,
        dst_ref=dst,
        send_sem=send,
        recv_sem=recv,
        device_id=to,
        device_id_type=MESH,
    )
    copy.start()
    return copy


def gather_kernel(*refs, cw, chunks, swaps, shards):
    parts = []
    for ref in refs[:shards]:
        parts += [ref.at[i] for i in range(ref.shape[0])] if len(ref.shape) == 3 else [ref]
    refs = refs[shards:]
    pw = parts[0].shape[1]
    ins, outs = refs[:swaps], refs[swaps + 1 : 2 * swaps + 1]
    w_ref = refs[swaps]
    send, recv, own, swap_send, swap_recv, swap_own = refs[2 * swaps + 1 :]
    (t, z, y, c), ids = partners()
    mine = [
        pltpu.make_async_copy(part, w_ref.at[t, z, y, c, :, pl.ds(i * pw, pw)], own.at[i])
        for i, part in enumerate(parts)
    ]
    for copy in mine:
        copy.start()
    kept = [
        pltpu.make_async_copy(ins[i].at[t], outs[i].at[t], swap_own.at[i]) for i in range(swaps)
    ]
    for copy in kept:
        copy.start()
    greet(ids)
    pair = (z // 2) * 2
    traded = []

    def begin(k, s):
        cols = pl.ds(k * cw, cw)
        if s == 0:
            r, to = w_ref.at[t, z, y, c, :, cols], "z1"
            src = parts[k * cw // pw].at[:, pl.ds(k * cw % pw, cw)]
            copies = [start_copy(src, r, send.at[k, 0], recv.at[k, 0], ids[to])]
            for i in range(swaps):
                part = ins[i].shape[1] // chunks
                rows = pl.ds(k * part, part)
                traded.append(
                    start_copy(
                        ins[i].at[1 - t, rows],
                        outs[i].at[t, rows],
                        swap_send.at[i, k],
                        swap_recv.at[i, k],
                        ids["x"],
                    )
                )
            return copies
        if s == 5:
            return []
        if s == 1:
            if k == 0:
                for copy in mine:
                    copy.wait()
            r, to = w_ref.at[t, pl.ds(pair, 2), y, c, :, cols], "z2"
        elif s == 2:
            r, to = w_ref.at[t, :, y, c, :, cols], "x"
        elif s == 3:
            r, to = w_ref.at[:, :, y, c, :, cols], "y"
        else:
            r, to = w_ref.at[:, :, :, c, :, cols], "c"
        return [start_copy(r, r, send.at[k, s], recv.at[k, s], ids[to])]

    pipeline(chunks, 5, begin)
    for copy in traded:
        copy.wait()
    for copy in kept:
        copy.wait()


def gather_weights(shards, pieces, cid, chunks):
    rows, wide = shards[0].shape[-2:]
    count = sum(s.shape[0] if s.ndim == 3 else 1 for s in shards)
    cols = count * wide
    swaps = len(pieces)
    anywhere = pl.BlockSpec(memory_space=pl.ANY)
    dma = pltpu.SemaphoreType.DMA
    outs = pl.pallas_call(
        functools.partial(gather_kernel, cw=cols // chunks, chunks=chunks, swaps=swaps, shards=len(shards)),
        in_specs=[pl.BlockSpec(memory_space=pltpu.VMEM)] * len(shards) + [anywhere] * swaps,
        out_specs=[anywhere] * (1 + swaps),
        out_shape=[jax.ShapeDtypeStruct((2, 4, 2, 2, rows, cols), shards[0].dtype)]
        + [jax.ShapeDtypeStruct(p.shape, p.dtype) for p in pieces],
        scratch_shapes=[
            dma((chunks, 5)),
            dma((chunks, 5)),
            dma((count,)),
            dma((swaps, chunks)),
            dma((swaps, chunks)),
            dma((swaps,)),
        ],
        compiler_params=pltpu.CompilerParams(collective_id=cid, has_side_effects=True),
        cost_estimate=pl.CostEstimate(
            flops=0, bytes_accessed=32 * rows * cols * 20, transcendentals=0
        ),
    )(*shards, *pieces)
    whole = outs[0].reshape(2, 16 * rows, cols)
    return whole, [p.reshape(p.shape[0] * p.shape[1], p.shape[2]) for p in outs[1:]]


def scatter_kernel(*refs, given, ahead, wa):
    g_refs, refs = refs[: 2 * given], refs[2 * given :]
    made = 4
    lefts, rights, refs = refs[:2], refs[2 : 2 + 2 * made], refs[2 + 2 * made + ahead :]
    rows_ref, small_ref, out_ref, small_out, pieces_ref = refs[:5]
    own, far, turned, r1, s2, r2, s3, r3, s4, r4, s5, r5, sm, rm = refs[5:19]
    send, recv, own_sem, small_send, small_recv, swap_send, swap_recv, swap_own = refs[19:]
    chunks = given + made
    (t, z, y, c), ids = partners()
    pair = (z // 2) * 2
    away = 2 - pair
    other = 1 - z % 2
    rows, cw = r5.shape[1:]
    sides = (slice(0, wa), slice(wa, cw))

    def loc(k, half):
        return pltpu.make_async_copy(
            g_refs[2 * k + half].at[:, :, c], own.at[k, half], own_sem.at[k, half]
        )

    for k in range(given):
        loc(k, 0).start()
        loc(k, 1).start()
    kept = pltpu.make_async_copy(rows_ref.at[t], pieces_ref.at[t], swap_own)
    kept.start()
    greet(ids)
    traded = []

    def go(k, j, src, dst, to):
        return start_copy(src, dst, send.at[k, j], recv.at[k, j], ids[to])

    def small_go(j):
        to = ids[("c", "x", "y", "z2", "z1")[j]]
        return start_copy(sm.at[j], rm.at[j], small_send.at[j], small_recv.at[j], to)

    def up(v):
        return v.astype(f32)

    def after_core(k, t_, z_, y_, cols):
        return up(own[k, t_, z_, y_, :, cols]) + up(r1[k, t_, z_, y_, :, cols])

    def after_two(k, z_, y_, t_, j):
        at = 2 * z_ + y_ if j == 0 else 4 * t_ + z_
        return after_core(k, t_, z_, y_, sides[j]) + up(r2[k, at, :, sides[j]])

    def after_three(k, z_, j):
        return after_two(k, z_, y, t, j) + up(r3[k, z_, :, sides[j]])

    def begin(k, s):
        a, b = sides
        if s == 0:
            copies = []
            for half in (0, 1):
                src = g_refs[2 * k + half].at[:, :, 1 - c] if k < given else far.at[k - given, half]
                copies.append(go(k, 6 + half, src, r1.at[k, half], "c"))
            return copies
        if s == 1:
            if k < given:
                loc(k, 0).wait()
                loc(k, 1).wait()
            for z_ in range(4):
                for i in range(2):
                    s2[k, 2 * z_ + i, :, a] = after_core(k, 1 - t, z_, i, a).astype(bf16)
            da = go(k, 0, s2.at[k, :, :, pl.ds(0, wa)], r2.at[k, :, :, pl.ds(0, wa)], "x")
            for z_ in range(4):
                for i in range(2):
                    s2[k, 4 * i + z_, :, b] = after_core(k, i, z_, 1 - y, b).astype(bf16)
            side = pl.ds(wa, cw - wa)
            return [da, go(k, 1, s2.at[k, :, :, side], r2.at[k, :, :, side], "y")]
        if s == 2:
            for z_ in range(4):
                s3[k, z_, :, a] = after_two(k, z_, 1 - y, t, 0).astype(bf16)
            da = go(k, 2, s3.at[k, :, :, pl.ds(0, wa)], r3.at[k, :, :, pl.ds(0, wa)], "y")
            for z_ in range(4):
                s3[k, z_, :, b] = after_two(k, z_, y, 1 - t, 1).astype(bf16)
            side = pl.ds(wa, cw - wa)
            return [da, go(k, 3, s3.at[k, :, :, side], r3.at[k, :, :, side], "x")]
        if s == 3:
            for i in range(2):
                for j in range(2):
                    s4[k, i, :, sides[j]] = after_three(k, away + i, j).astype(bf16)
            return [go(k, 4, s4.at[k], r4.at[k], "z2")]
        for j in range(2):
            if s == 4:
                sent = after_three(k, pair + other, j) + up(r4[k, other, :, sides[j]])
                s5[k, :, sides[j]] = sent.astype(bf16)
            else:
                mine = after_three(k, z, j) + up(r4[k, z % 2, :, sides[j]])
                cols = slice(k * cw + sides[j].start, k * cw + sides[j].stop)
                out_ref[:, cols] = mine + up(r5[k, :, sides[j]])
        return [go(k, 5, s5.at[k], r5.at[k], "z1")] if s == 4 else []

    smalls = []

    def begin_with_small(k, s):
        if s == 0:
            part = rows_ref.shape[1] // chunks
            some = pl.ds(k * part, part)
            src, dst = rows_ref.at[1 - t, some], pieces_ref.at[t, some]
            traded.append(start_copy(src, dst, swap_send.at[k], swap_recv.at[k], ids["x"]))
        if k == 0:
            if s == 0:
                sm[0] = small_ref[...]
            else:
                smalls[s - 1].wait_recv()
                total = sm[s - 1] + rm[s - 1]
                if s < 5:
                    sm[s] = total
                else:
                    small_out[...] = total
            if s < 5:
                smalls.append(small_go(s))
        return begin(k, s)

    def make(step):
        if step == 1:
            turned[...] = lefts[0][...].T
        elif step == made + 2:
            turned[...] = lefts[1][...].T
        ready = {2: [(0, 0)], 3: [(0, 1)]}
        for i in range(1, made):
            ready[3 + i] = [(i, 0), (i, 1)]
        for i, half in ready.get(step, []):
            d = rights[2 * i + half][...]
            g = lax.dot_general(turned[...], d, NN, preferred_element_type=f32)
            g = g.astype(bf16).reshape(4, 2, 2, rows, cw)
            own[given + i, half] = jnp.where(c == 0, g[:, :, 0], g[:, :, 1])
            far[i, half] = jnp.where(c == 0, g[:, :, 1], g[:, :, 0])

    pipeline(chunks, 5, begin_with_small, make)
    for copy in smalls:
        copy.wait_send()
    for copy in traded:
        copy.wait()
    kept.wait()


def scatter_grads(pairs, lefts, rights, ahead, seq_rows, small, cid):
    given = len(pairs)
    chunks = given + 4
    tokens, width = lefts[0].shape
    cw = pairs[0][0].shape[1]
    rows, cols = width // 16, cw * chunks
    V = pltpu.VMEM
    dma = pltpu.SemaphoreType.DMA
    flat = [g.reshape(4, 2, 2, rows, cw) for pair in pairs for g in pair]
    seq_rows = seq_rows.reshape(2, seq_rows.shape[0] // 2, seq_rows.shape[1])
    whole = pl.BlockSpec(memory_space=pltpu.VMEM)
    anywhere = pl.BlockSpec(memory_space=pl.ANY)
    return pl.pallas_call(
        functools.partial(scatter_kernel, given=given, ahead=len(ahead), wa=cw // 4),
        in_specs=[anywhere] * len(flat)
        + [whole] * (2 + len(rights))
        + [anywhere] * (len(ahead) + 1)
        + [whole],
        out_specs=[whole, whole, anywhere],
        out_shape=[
            jax.ShapeDtypeStruct((rows, cols), f32),
            jax.ShapeDtypeStruct(small.shape, f32),
            jax.ShapeDtypeStruct(seq_rows.shape, seq_rows.dtype),
        ],
        scratch_shapes=[
            V((chunks, 2, 4, 2, rows, cw), bf16),
            V((4, 2, 4, 2, rows, cw), bf16),
            V((width, tokens), bf16),
            V((chunks, 2, 4, 2, rows, cw), bf16),
            V((chunks, 8, rows, cw), bf16),
            V((chunks, 8, rows, cw), bf16),
            V((chunks, 4, rows, cw), bf16),
            V((chunks, 4, rows, cw), bf16),
            V((chunks, 2, rows, cw), bf16),
            V((chunks, 2, rows, cw), bf16),
            V((chunks, rows, cw), bf16),
            V((chunks, rows, cw), bf16),
            V((5,) + small.shape, f32),
            V((5,) + small.shape, f32),
            dma((chunks, 8)),
            dma((chunks, 8)),
            dma((given, 2)),
            dma((5,)),
            dma((5,)),
            dma((chunks,)),
            dma((chunks,)),
            dma,
        ],
        compiler_params=pltpu.CompilerParams(
            collective_id=cid, has_side_effects=True, vmem_limit_bytes=62 * 2**20
        ),
        cost_estimate=pl.CostEstimate(
            flops=0, bytes_accessed=32 * rows * cols * 20, transcendentals=0
        ),
    )(*flat, *lefts, *rights, *ahead, seq_rows, small)


ERFC_SLOPE = 0.44
ERFC_COEFS = (
    0.12411048270139104,
    0.12443557227306976,
    0.1086564621750582,
    0.10790840846971936,
    -0.01009671066483208,
    0.1483525285505606,
    -0.13897999621011298,
    0.03561334337852199,
)


def gelu_and_slope(u):
    a = jnp.abs(u) * 0.7071067811865476
    t = 1.0 / (1.0 + ERFC_SLOPE * a)
    q = jnp.full_like(t, ERFC_COEFS[-1])
    for c in ERFC_COEFS[-2::-1]:
        q = q * t + c
    e = jnp.exp(-(a * a))
    tail = e * (t * q)
    phi = jnp.where(u < 0, tail, 1.0 - tail)
    return u * phi, phi + u * (e * 0.3989422804014327)


def up_kernel(x_ref, w_ref, b_ref, act_ref, slope_ref):
    for i in range(8):
        rows = slice(128 * i, 128 * (i + 1))
        u = lax.dot_general(x_ref[rows, :], w_ref[0], NN, preferred_element_type=f32) + b_ref[...]
        g, d = gelu_and_slope(u)
        act_ref[rows, :] = g.astype(bf16)
        slope_ref[rows, :] = d.astype(bf16)


def hidden_units(x, w, bias, tile):
    rows, width = x.shape
    units = w.shape[2] // 2
    per = units // tile
    col = pl.BlockSpec((rows, tile), lambda j: (0, j))
    return pl.pallas_call(
        up_kernel,
        grid=(2 * per,),
        in_specs=[
            pl.BlockSpec((rows, width), lambda j: (0, 0)),
            pl.BlockSpec((1, width, tile), lambda j: (j // per, 0, j % per)),
            pl.BlockSpec((1, tile), lambda j: (0, j)),
        ],
        out_specs=[col, col],
        out_shape=[jax.ShapeDtypeStruct((rows, 2 * units), bf16)] * 2,
        compiler_params=pltpu.CompilerParams(vmem_limit_bytes=56 * 2**20),
    )(x, w, bias)


def units_back_kernel(e_ref, w_ref, slope_ref, du_ref, sum_ref):
    total = 0.0
    for i in range(4):
        rows = slice(256 * i, 256 * (i + 1))
        d = lax.dot_general(e_ref[rows, :], w_ref[0], NN, preferred_element_type=f32)
        du = (d * slope_ref[rows, :].astype(f32)).astype(bf16)
        du_ref[rows, :] = du
        total = total + jnp.sum(du.astype(f32), 0, keepdims=True)
    sum_ref[...] = total


def hidden_units_back(e, w, slope, tile):
    rows, width = e.shape
    units = w.shape[2] // 2
    per = units // tile
    col = pl.BlockSpec((rows, tile), lambda j: (0, j))
    return pl.pallas_call(
        units_back_kernel,
        grid=(2 * per,),
        in_specs=[
            pl.BlockSpec((rows, width), lambda j: (0, 0)),
            pl.BlockSpec((1, width, tile), lambda j: (j // per, 0, per + j % per)),
            col,
        ],
        out_specs=[col, pl.BlockSpec((1, tile), lambda j: (0, j))],
        out_shape=[
            jax.ShapeDtypeStruct((rows, 2 * units), bf16),
            jax.ShapeDtypeStruct((1, 2 * units), f32),
        ],
        compiler_params=pltpu.CompilerParams(vmem_limit_bytes=56 * 2**20),
    )(e, w, slope)


def down_kernel(act_ref, w_ref, h_ref, cot_ref, vec_ref, mixed_ref, dr_ref, e_ref, sum_ref):
    units = w_ref.shape[2]
    r = h_ref[...] + vec_ref[0:1]
    for t in range(2):
        part = act_ref[:, t * units : (t + 1) * units]
        r = r + lax.dot_general(part, w_ref[t], NT, preferred_element_type=f32)
    gain = vec_ref[1:2]
    h, n, inv = norm_rows(r, gain, vec_ref[2:3])
    mixed_ref[...] = h.astype(bf16)
    rows_back(cot_ref[...].astype(f32), n, inv, gain, dr_ref, e_ref, sum_ref)


def rows_back(e, n, inv, gain, dr_ref, e_ref, sum_ref):
    dr, gg, gs, gb = norm_rows_back(e, n, inv, gain)
    dr_ref[...] = dr
    e_ref[...] = dr.astype(bf16)

    @pl.when(pl.program_id(0) == 0)
    def _():
        sum_ref[...] = jnp.zeros_like(sum_ref)

    sum_ref[0:3] += jnp.concatenate([gg[None], gs[None], gb[None]], 0)


def down_and_norms(act, w, h, cot, vecs, block):
    rows, width = h.shape
    units = w.shape[2] // 2
    row = pl.BlockSpec((block, width), lambda i: (i, 0))
    top = pl.BlockSpec((8, width), lambda i: (0, 0))
    return pl.pallas_call(
        down_kernel,
        grid=(rows // block,),
        in_specs=[
            pl.BlockSpec((block, 2 * units), lambda i: (i, 0)),
            pl.BlockSpec((2, width, units), lambda i: (0, 0, 1), pipeline_mode=pl.Buffered(1)),
            row,
            row,
            top,
        ],
        out_specs=[row, row, row, top],
        out_shape=[
            jax.ShapeDtypeStruct((rows, width), bf16),
            jax.ShapeDtypeStruct((rows, width), f32),
            jax.ShapeDtypeStruct((rows, width), bf16),
            jax.ShapeDtypeStruct((8, width), f32),
        ],
        compiler_params=pltpu.CompilerParams(vmem_limit_bytes=56 * 2**20),
    )(act, w, h, cot, vecs)


def up_back_kernel(du_ref, w_ref, dr3_ref, n_ref, inv_ref, vec_ref, dr_ref, e_ref, sum_ref):
    units = w_ref.shape[2]
    e = dr3_ref[...]
    for t in range(2):
        part = du_ref[:, t * units : (t + 1) * units]
        e = e + lax.dot_general(part, w_ref[t], NT, preferred_element_type=f32)
    rows_back(e, n_ref[...], inv_ref[...], vec_ref[0:1], dr_ref, e_ref, sum_ref)


def up_back_and_norm(du, w, dr3, n, inv, vecs, block):
    rows, width = dr3.shape
    units = w.shape[2] // 2
    row = pl.BlockSpec((block, width), lambda i: (i, 0))
    top = pl.BlockSpec((8, width), lambda i: (0, 0))
    return pl.pallas_call(
        up_back_kernel,
        grid=(rows // block,),
        in_specs=[
            pl.BlockSpec((block, 2 * units), lambda i: (i, 0)),
            pl.BlockSpec((2, width, units), lambda i: (0, 0, 0), pipeline_mode=pl.Buffered(1)),
            row,
            row,
            pl.BlockSpec((block, 1), lambda i: (i, 0)),
            top,
        ],
        out_specs=[row, row, top],
        out_shape=[
            jax.ShapeDtypeStruct((rows, width), f32),
            jax.ShapeDtypeStruct((rows, width), bf16),
            jax.ShapeDtypeStruct((8, width), f32),
        ],
        compiler_params=pltpu.CompilerParams(vmem_limit_bytes=56 * 2**20),
    )(du, w, dr3, n, inv, vecs)


def products_kernel(*refs, count, based):
    total = refs[2 * count][...] if based else 0.0
    for i in range(count):
        total = total + lax.dot_general(
            refs[i][...], refs[count + i][0], NT, preferred_element_type=f32
        )
    refs[-1][...] = total.astype(refs[-1].dtype)


def sum_of_products(lefts, w, places, base, block):
    rows, cols = lefts[0].shape
    width = w.shape[1]
    row = pl.BlockSpec((block, width), lambda i: (i, 0))
    left = pl.BlockSpec((block, cols), lambda i: (i, 0))

    def weight(t, j):
        return pl.BlockSpec((1, width, cols), lambda i: (t, 0, j), pipeline_mode=pl.Buffered(1))

    based = [] if base is None else [base]
    return pl.pallas_call(
        functools.partial(products_kernel, count=len(lefts), based=len(based)),
        grid=(rows // block,),
        in_specs=[left] * len(lefts) + [weight(t, j) for t, j in places] + [row] * len(based),
        out_specs=row,
        out_shape=jax.ShapeDtypeStruct((rows, width), bf16),
        compiler_params=pltpu.CompilerParams(vmem_limit_bytes=40 * 2**20),
    )(*lefts, *([w] * len(lefts)), *based)


def unpack_kernel(att_ref, ffn_ref, flat_ref, *outs):
    self_in, self_out, cross_in, cross_out, up, down, head, unit, gain, row = outs
    cols, units = head.shape[1], up.shape[1]
    place = lax.axis_index("tp")
    for j in range(3):
        cross_in[j] = att_ref[:, j * cols : (j + 1) * cols]
        self_in[j] = att_ref[:, (4 + j) * cols : (5 + j) * cols]
    cross_out[...] = att_ref[:, 3 * cols : 4 * cols]
    self_out[...] = att_ref[:, 7 * cols : 8 * cols]
    up[...] = ffn_ref[:, :units].astype(f32)
    down[...] = ffn_ref[:, units:].astype(f32)
    lines = cols // 128
    for i in range(4):
        for j in range(lines):
            head[i : i + 1, 128 * j : 128 * (j + 1)] = flat_ref[
                pl.ds((place * 4 + i) * lines + j, 1), :
            ]
    first, lines = 8 * lines, units // 128
    for j in range(lines):
        unit[:, 128 * j : 128 * (j + 1)] = flat_ref[pl.ds(first + place * lines + j, 1), :]
    first, lines = first + 2 * lines, gain.shape[1] // 128
    for ref in (gain, row):
        for i in range(ref.shape[0]):
            for j in range(lines):
                ref[i : i + 1, 128 * j : 128 * (j + 1)] = flat_ref[first + j : first + j + 1, :]
            first += lines


def unpack(att, ffn, flat, cols, units):
    rows, width = att.shape[0], 16 * att.shape[0]
    shapes = [
        (3, rows, cols),
        (rows, cols),
        (3, rows, cols),
        (rows, cols),
        (rows, units),
        (rows, units),
        (4, cols),
        (1, units),
        (3, width),
        (6, width),
    ]
    whole = pl.BlockSpec(memory_space=pltpu.VMEM)
    outs = pl.pallas_call(
        unpack_kernel,
        in_specs=[whole] * 3,
        out_specs=[whole] * len(shapes),
        out_shape=[jax.ShapeDtypeStruct(s, f32) for s in shapes],
    )(att, ffn, flat)
    self_in, self_out, cross_in, cross_out, up, down = outs[:6]
    self_in, cross_in = self_in.transpose(1, 0, 2), cross_in.transpose(1, 0, 2)
    return self_in, self_out.T, cross_in, cross_out.T, up, down.T, outs[6:]


def weight_grads_kernel(a_ref,b_ref,da_ref,db_ref,out_ref,at,bt,*,tiles):
    j=pl.program_id(0)
    @pl.when(j==0)
    def _():
        at[...]=a_ref[...].T
        bt[...]=b_ref[...].T
    kind=(j//tiles)%2
    @pl.when(kind==0)
    def _():
        out_ref[0]=lax.dot_general(at[...],da_ref[...],NN,preferred_element_type=f32).astype(bf16)
    @pl.when(kind==1)
    def _():
        out_ref[0]=lax.dot_general(bt[...],db_ref[...],NN,preferred_element_type=f32).astype(bf16)

def weight_grads(a,b,da,db,tile=512):
    rows,width=a.shape; half=da.shape[1]//2; tiles=half//tile
    whole=pl.BlockSpec((rows,width),lambda j:(0,0))
    t=lambda j: j//(2*tiles)
    kind=lambda j:(j//tiles)%2
    i=lambda j: j%tiles
    return pl.pallas_call(
        functools.partial(weight_grads_kernel,tiles=tiles),
        grid=(4*tiles,),
        in_specs=[whole,whole,
          pl.BlockSpec((rows,tile),lambda j:(0,t(j)*tiles+jnp.where(kind(j)==0,i(j),tiles-1))),
          pl.BlockSpec((rows,tile),lambda j:(0,t(j)*tiles+jnp.where(kind(j)==1,i(j),0)))],
        out_specs=pl.BlockSpec((1,width,tile),lambda j:(t(j),0,kind(j)*tiles+i(j))),
        out_shape=jax.ShapeDtypeStruct((2,width,2*half),bf16),
        scratch_shapes=[pltpu.VMEM((width,rows),bf16)]*2,
        compiler_params=pltpu.CompilerParams(vmem_limit_bytes=56*2**20),
    )(a,b,da,db)


def nn(a, b):
    return lax.dot_general(a, b, NN, preferred_element_type=f32)


def nt(a, b):
    return lax.dot_general(a, b, NT, preferred_element_type=f32)


def tn(a, b):
    return lax.dot_general(a, b, (((0,), (0,)), ((), ())), preferred_element_type=f32)


def norm_rows(r, gain, shift):
    center = r - jnp.mean(r, -1, keepdims=True)
    inv = lax.rsqrt(jnp.mean(center * center, -1, keepdims=True) + NORM_EPS)
    n = center * inv
    return n * gain + shift, n, inv


def norm_rows_back(e, n, inv, gain):
    eg = e * gain
    grad = inv * (eg - jnp.mean(eg, -1, keepdims=True) - n * jnp.mean(eg * n, -1, keepdims=True))
    return grad, jnp.sum(e * n, 0), jnp.sum(e, 0), jnp.sum(grad, 0)


def trade(x):
    return lax.ppermute(x, "tp", [(0, 1), (1, 0)])


def in_order(place, own, other, axis=0):
    return jnp.where(
        place == 0,
        jnp.concatenate([own, other], axis),
        jnp.concatenate([other, own], axis),
    )


def own_sequence(piece, place):
    own = lax.dynamic_index_in_dim(piece, place, 0, keepdims=False)
    away = lax.dynamic_index_in_dim(piece, 1 - place, 0, keepdims=False)
    return in_order(place, own, trade(away))


def to_pieces(rows, place):
    half = rows.shape[0] // 2
    halves = rows.reshape(2, half, rows.shape[1])
    own = lax.dynamic_index_in_dim(halves, place, 0, keepdims=True)
    away = lax.dynamic_index_in_dim(halves, 1 - place, 0, keepdims=True)
    return in_order(place, own, trade(away))


def whole_sequences(
    layer_in,
    memory,
    out_grad,
    w_self_in,
    w_self_out,
    w_cross_in,
    w_cross_out,
    w_up,
    w_down,
    head_bias,
    up_bias,
    norm_gain,
    row_bias,
):
    place = lax.axis_index("tp")
    width = layer_in.shape[2]
    cols = w_self_in.shape[2]
    units = w_up.shape[1]
    shard = w_self_in.shape[0]
    gains = norm_gain.astype(f32)
    shifts = row_bias.astype(f32)

    def gather(*parts):
        mine = jnp.concatenate(parts, 1)
        both = lax.all_gather(mine, ("tp", "fsdp"), axis=0, tiled=True)
        return both.reshape(2, width, mine.shape[1])

    small = jnp.concatenate([head_bias.reshape(-1), up_bias])
    small = in_order(place, small[None], trade(small)[None])
    hb = small[:, : 4 * cols].reshape(2, 4, cols).astype(f32)
    ub = small[:, 4 * cols :].astype(f32)

    c3, c4 = 3 * cols, 4 * cols
    g_att, (x, mem) = gather_weights(
        (w_self_in.transpose(1, 0, 2), w_self_out.T, w_cross_in.transpose(1, 0, 2), w_cross_out.T),
        (layer_in, memory),
        1,
        16,
    )
    g_att, w_up, w_down = lax.optimization_barrier((g_att, w_up, w_down))
    g_self, g_cross = g_att[:, :, :c4], g_att[:, :, c4:]
    g_ffn = gather(w_up, w_down.T)
    g_ffn, out_grad = lax.optimization_barrier((g_ffn, out_grad))
    cot = own_sequence(out_grad, place)
    xf = x.astype(f32)
    halves = (0, 1)
    zero = jnp.zeros((cols,), f32)
    scale3 = jnp.concatenate([zero + ATT_SCALE * LOG2E, zero + 1.0, zero + 1.0])
    blk = cols // 128

    sy, sa, sl = [], [], []
    for t in halves:
        bias = jnp.concatenate([hb[t, 0], zero, hb[t, 1]])
        y = ((nn(x, g_self[t, :, :c3]) + bias) * scale3).astype(bf16)
        o, lse = att_fwd(y, y, y, True, 512, 0, blk, 2 * blk, cols)
        sy.append(y)
        sa.append(o)
        sl.append(lse)
    r1 = xf + (nt(sa[0], g_self[0, :, c3:]) + nt(sa[1], g_self[1, :, c3:])) + shifts[0]
    h1, n1, i1 = norm_rows(r1, gains[0], shifts[3])
    h1b = h1.astype(bf16)

    cq, ckv, ca, cl = [], [], [], []
    for t in halves:
        kv = (nn(mem, g_cross[t, :, cols:c3]) + jnp.concatenate([zero, hb[t, 3]])).astype(bf16)
        q = ((nn(h1b, g_cross[t, :, :cols]) + hb[t, 2]) * (ATT_SCALE * LOG2E)).astype(bf16)
        o, lse = att_fwd(q, kv, kv, False, 512, 0, 0, blk, cols)
        cq.append(q)
        ckv.append(kv)
        ca.append(o)
        cl.append(lse)
    r2 = h1 + (nt(ca[0], g_cross[0, :, c3:]) + nt(ca[1], g_cross[1, :, c3:])) + shifts[1]
    h2, n2, i2 = norm_rows(r2, gains[1], shifts[4])
    h2b = h2.astype(bf16)

    act, slope = hidden_units(h2b, g_ffn, ub.reshape(1, 2 * units), 512)
    none = jnp.zeros((5, width), f32)
    mixed_rows, dr3, e3, sums3 = down_and_norms(
        act,
        g_ffn,
        h2,
        cot,
        jnp.concatenate([shifts[2:3], gains[2:3], shifts[5:6], none], 0),
        256,
    )
    gg3, gs3, gb3 = sums3[0], sums3[1], sums3[2]
    mixed = to_pieces(mixed_rows, place)

    du, gu = hidden_units_back(e3, g_ffn, slope, 1024)
    grad_ffn = weight_grads(h2b, e3, du, act, 1024)
    grad_ffn, du = lax.optimization_barrier((grad_ffn, du))
    s_ffn = lax.psum_scatter(
        grad_ffn.reshape(2 * width, 2 * units), ("tp", "fsdp"), scatter_dimension=0, tiled=True
    )
    dr2, e2, sums2 = up_back_and_norm(
        du,
        g_ffn,
        dr3,
        n2,
        i2,
        jnp.concatenate([gains[1:2], none, none[:2]], 0),
        256,
    )
    gg2, gs2, gb2 = sums2[0], sums2[1], sums2[2]

    dcq, dck, dcv, bcq, bcv = [], [], [], [], []
    for t in halves:
        da = nn(e2, g_cross[t, :, c3:]).astype(bf16)
        a, b, c, sq, sv = att_bwd(cq[t], ckv[t], ckv[t], ca[t], da, cl[t], False, 256, 0, 0, blk)
        dcq.append(a)
        dck.append(b)
        dcv.append(c)
        bcq.append(sq[0])
        bcv.append(sv[0])
    low = lambda v: v.astype(bf16)
    grads = [
        tuple(low(tn(h1b, dcq[t])) for t in halves),
        tuple(low(tn(mem, dck[t])) for t in halves),
        tuple(low(tn(mem, dcv[t])) for t in halves),
        tuple(low(tn(e2, ca[t])) for t in halves),
    ]
    dmem = sum_of_products(
        dck + dcv, g_att, [(t, j) for j in (5, 6) for t in halves], None, 256
    )
    d_memory = to_pieces(dmem, place)
    dh1 = dr2 + (nt(dcq[0], g_cross[0, :, :cols]) + nt(dcq[1], g_cross[1, :, :cols]))
    dr1, gg1, gs1, gb1 = norm_rows_back(dh1, n1, i1, gains[0])
    e1 = dr1.astype(bf16)

    dsq, dsk, dsv, bsq, bsv = [], [], [], [], []
    for t in halves:
        da = nn(e1, g_self[t, :, c3:]).astype(bf16)
        y = sy[t]
        ahead = (mixed, dmem) if t == 0 else ()
        a, b, c, sq, sv = att_bwd(y, y, y, sa[t], da, sl[t], True, 256, 0, blk, 2 * blk, ahead)
        dsq.append(a)
        dsk.append(b)
        dsv.append(c)
        bsq.append(sq[0])
        bsv.append(sv[0])
    dx = sum_of_products(
        dsq + dsk + dsv, g_att, [(t, j) for j in range(3) for t in halves], dr1, 256
    )

    gh = jnp.stack([jnp.stack([bsq[t], bsv[t], bcq[t], bcv[t]]) for t in halves])
    flat = jnp.concatenate(
        [
            v.reshape(-1)
            for v in (gh, gu, gg1, gg2, gg3, gb1, gb2, gb3, gs1, gs2, gs3)
        ]
    )
    made = [dsq[0], dsq[1], dsk[0], dsk[1], dsv[0], dsv[1], sa[0], sa[1]]
    s_att, flat, d_layer_in = scatter_grads(
        grads, (x, e1), made, (d_memory,), dx, flat.reshape(-1, 128), 2
    )
    d_self_in, d_self_out, d_cross_in, d_cross_out, d_up, d_down, small = unpack(
        s_att, s_ffn, flat, cols, units
    )
    d_head_bias, d_up_bias, d_norm_gain, d_row_bias = small
    return (
        mixed,
        d_layer_in.reshape(layer_in.shape),
        d_memory,
        d_self_in,
        d_self_out,
        d_cross_in,
        d_cross_out,
        d_up,
        d_down,
        d_head_bias,
        d_up_bias.reshape(units),
        d_norm_gain,
        d_row_bias,
    )


def on_device(layer_in, *rest):
    paired = lax.axis_size("tp") == 2 and layer_in.shape[0] == 2
    if paired and lax.axis_size("fsdp") == 16:
        return whole_sequences(layer_in, *rest)
    return shared_sequences(layer_in, *rest)


def solution(mesh):
    return jax.shard_map(
        on_device,
        mesh=mesh,
        in_specs=(
            P("fsdp", "tp", None),
            P("fsdp", "tp", None),
            P("fsdp", "tp", None),
            P("fsdp", None, "tp"),
            P("tp", "fsdp"),
            P("fsdp", None, "tp"),
            P("tp", "fsdp"),
            P("fsdp", "tp"),
            P("tp", "fsdp"),
            P(None, "tp"),
            P("tp"),
            P(),
            P(),
        ),
        out_specs=(
            P("fsdp", "tp", None),
            P("fsdp", "tp", None),
            P("fsdp", "tp", None),
            P("fsdp", None, "tp"),
            P("tp", "fsdp"),
            P("fsdp", None, "tp"),
            P("tp", "fsdp"),
            P("fsdp", "tp"),
            P("tp", "fsdp"),
            P(None, "tp"),
            P("tp"),
            P(),
            P(),
        ),
        check_vma=False,
    )
```
